32 devices in a mesh: group: 2 (over y), seq: 4 (over z), doc: 4 (over x, core).
Axes of the slice: x: 2, y: 2, z: 4, core: 2. Of those that a mesh axis runs over, the one named last changes fastest.
Arguments:
- query_vectors: bfloat16 [8, 512, 1024], P(('group', 'doc'), 'seq'), parts along dimension 0, may hold values from -6 to 6
- key_vectors: bfloat16 [8, 512, 1024], P(('group', 'doc'), 'seq'), parts along dimension 0, may hold values from -6 to 6
- value_vectors: bfloat16 [8, 512, 1024], P(('group', 'doc'), 'seq'), parts along dimension 0, may hold values from -6 to 6
- out_grad: bfloat16 [8, 512, 1024], P(('group', 'doc'), 'seq'), parts along dimension 0, may hold values from -6 to 6
- pad_length: int32 [8], P(('group', 'doc')), parts along dimension 0, may hold values from 1 to 256
Outputs:
- attended: bfloat16 [8, 512, 1024], P(('group', 'doc'), 'seq'), parts along dimension 0
- query_grad: bfloat16 [8, 512, 1024], P(('group', 'doc'), 'seq'), parts along dimension 0
- key_grad: bfloat16 [8, 512, 1024], P(('group', 'doc'), 'seq'), parts along dimension 0
- value_grad: bfloat16 [8, 512, 1024], P(('group', 'doc'), 'seq'), parts along dimension 0
The draws below stay inside these ranges and needn't reach their ends.
There are 2 independent parts, one for each index of `group`. The reference program is written for one: setup_inputs(seed, part) draws one part's arguments, and reference() takes and returns one part's arrays. A program takes and returns all parts, laid end to end along the dimension named above; each array names one. Nothing has to cross between parts.
All inputs are finite; a program needn't handle non-finite values.
Results may differ from the reference program's by a relative error of at most 0.015.
Values may be sent and summed in bfloat16 or wider, within the bound.
A program may use at most 64 MiB of HBM per device.

```python
import math
import jax
import jax.numpy as jnp
from jax import lax

D = 1024
H = 16
W = 128
G = 64
TOK_DEV = 128
DOCS = 4
LENGTH = 512


def draw_query_vectors(key, part):
    result = jnp.clip(jax.random.normal(jax.random.fold_in(key, 1), (DOCS, LENGTH, D), jnp.float32), -6.0, 6.0)
    return result.astype(jnp.bfloat16)


def draw_key_vectors(key, part):
    result = jnp.clip(jax.random.normal(jax.random.fold_in(key, 3), (DOCS, LENGTH, D), jnp.float32), -6.0, 6.0)
    return result.astype(jnp.bfloat16)


def touch_ends(entries, key, low, top_value):
    dims = entries.shape
    index_at = [jax.random.randint(jax.random.fold_in(key, axis), (), 0, dims[axis]) for axis in range(len(dims))]
    entries = entries.at[tuple(index_at)].set(low)
    longest = dims.index(max(dims))
    index_at[longest] = (index_at[longest] + 1) % dims[longest]
    return entries.at[tuple(index_at)].set(top_value)


def steps_of(stream_key, shape, split, least, high):
    level = 1.0
    for position, shards_of in split:
        heights = jax.random.uniform(jax.random.fold_in(jax.random.fold_in(stream_key, 6), position), (shards_of,), jnp.float32, least / len(split), high / len(split))
        level = level * jnp.repeat(jnp.exp(heights), shape[position] // shards_of).reshape((-1,) + (1,) * (len(shape) - 1 - position))
    return level


def scatter_about(own_key, extent, scale, most, shards=(), kind=jnp.bfloat16):
    loudness = steps_of(own_key, extent, shards, -0.22, 0.18) if shards else 1.0
    drawn = jax.random.normal(own_key, extent, jnp.float32) * scale * loudness
    return jnp.minimum(jnp.maximum(drawn, -most), most).astype(kind)


def setup_inputs(seed: int = 0, part: int = 0) -> dict:
    arg_keys = jax.random.split(jax.random.key(seed), 6)
    part_splits = jax.random.split(jax.random.fold_in(arg_keys[5], part), 6)
    query_vectors = draw_query_vectors(jax.random.fold_in(jax.random.fold_in(arg_keys[5], part), 71), part)
    key_vectors = draw_key_vectors(jax.random.fold_in(jax.random.fold_in(arg_keys[5], part), 71), part)
    value_vectors = scatter_about(part_splits[2], (DOCS, LENGTH, D), 1.0, 6.0, ((0, 4), (1, 4)))
    out_grad = scatter_about(part_splits[3], (DOCS, LENGTH, D), 1.0, 6.0, ((0, 4), (1, 4)))
    pad_length = touch_ends(jax.random.randint(part_splits[4], (DOCS,), 1, 2 * TOK_DEV + 1), jax.random.fold_in(part_splits[4], 1), 1, 2 * TOK_DEV).astype(jnp.int32)
    return {"query_vectors": query_vectors, "key_vectors": key_vectors, "value_vectors": value_vectors, "out_grad": out_grad, "pad_length": pad_length}


very_negative = -1e+30

def split_heads(block_rows):
    return block_rows.reshape(block_rows.shape[0], H, D // H)

def join_heads(block_rows):
    return block_rows.reshape(block_rows.shape[0], D)

def product(form, left_side, right_side):
    return jnp.einsum(form, left_side.astype(jnp.float32), right_side.astype(jnp.float32), precision=lax.Precision.HIGHEST)

def band_terms(query_rows, grad_rows, key_all, value_all, allowed, row_live):
    score_scale = 1.0 / math.sqrt(D // H)
    query_heads = split_heads(query_rows)
    grad_heads = split_heads(grad_rows)
    key_heads = split_heads(key_all)
    value_heads = split_heads(value_all)
    scores = product('qhd,khd->hqk', query_heads, key_heads) * score_scale
    scores = jnp.where(allowed[None], scores, very_negative)
    largest = lax.optimization_barrier(jnp.max(scores, axis=2, keepdims=True))
    expo = jnp.where(allowed[None], jnp.exp(scores - largest), 0.0)
    totals = lax.optimization_barrier(jnp.sum(expo, axis=2, keepdims=True))
    probs = expo / totals
    probs_low = probs.astype(jnp.bfloat16)
    attn = product('hqk,khd->qhd', probs_low, value_heads)
    delta = lax.optimization_barrier(jnp.sum(grad_heads.astype(jnp.float32) * attn, axis=2)).T
    dprob = product('qhd,khd->hqk', grad_heads, value_heads)
    keep_rows = row_live[None, :, None]
    dscore = jnp.where(keep_rows, probs * (dprob - delta[:, :, None]), 0.0).astype(jnp.bfloat16)
    kept_low = jnp.where(keep_rows, probs_low, jnp.zeros_like(probs_low))
    query_grad = product('hqk,khd->qhd', dscore, key_heads) * score_scale
    key_grad = product('hqk,qhd->khd', dscore, query_heads) * score_scale
    value_grad = product('hqk,qhd->khd', kept_low, grad_heads)
    return (join_heads(attn), join_heads(query_grad), join_heads(key_grad), join_heads(value_grad))

def one_doc(doc_inputs):
    query_doc, key_doc, value_doc, grad_doc, pad_count = doc_inputs
    doc_length = query_doc.shape[0]
    block_rows = TOK_DEV
    block_count = doc_length // block_rows
    score_scale = 1.0 / math.sqrt(D // H)
    suffix_start = doc_length - G
    valid_end = suffix_start - pad_count
    query_glob = query_doc[suffix_start:]
    key_glob = key_doc[suffix_start:]
    value_glob = value_doc[suffix_start:]
    grad_glob = grad_doc[suffix_start:]
    key_padded = jnp.pad(key_doc, ((W, W), (0, 0)))
    value_padded = jnp.pad(value_doc, ((W, W), (0, 0)))

    def one_block(block_index):
        first_row = block_index * block_rows
        query_pos = first_row + jnp.arange(block_rows, dtype=jnp.int32)
        window_pos = first_row - W + jnp.arange(block_rows + 2 * W, dtype=jnp.int32)
        query_rows = lax.dynamic_slice_in_dim(query_doc, first_row, block_rows, 0)
        grad_rows = lax.dynamic_slice_in_dim(grad_doc, first_row, block_rows, 0)
        key_window = lax.dynamic_slice_in_dim(key_padded, first_row, block_rows + 2 * W, 0)
        value_window = lax.dynamic_slice_in_dim(value_padded, first_row, block_rows + 2 * W, 0)
        within = (jnp.abs(query_pos[:, None] - window_pos[None, :]) <= W) & (window_pos >= 0)[None, :] & (window_pos < valid_end)[None, :]
        allowed = jnp.concatenate([within, jnp.ones((block_rows, G), dtype=bool)], axis=1)
        key_all = jnp.concatenate([key_window, key_glob], axis=0)
        value_all = jnp.concatenate([value_window, value_glob], axis=0)
        return band_terms(query_rows, grad_rows, key_all, value_all, allowed, query_pos < suffix_start)
    attn_all, qgrad_all, kgrad_all, vgrad_all = lax.map(one_block, jnp.arange(block_count, dtype=jnp.int32))
    attn_band = attn_all.reshape(doc_length, D)
    query_band = qgrad_all.reshape(doc_length, D)

    def gather_band(grad_all):
        middle = grad_all[:, W:W + block_rows]
        middle = middle.at[:-1, block_rows - W:].add(grad_all[1:, :W])
        middle = middle.at[1:, :W].add(grad_all[:-1, W + block_rows:2 * W + block_rows])
        return (middle.reshape(doc_length, D), lax.optimization_barrier(jnp.sum(grad_all[:, 2 * W + block_rows:], axis=0)))
    key_band, key_suffix = gather_band(kgrad_all)
    value_band, value_suffix = gather_band(vgrad_all)
    positions = jnp.arange(doc_length, dtype=jnp.int32)
    local_live = (positions < valid_end) | (positions >= suffix_start)
    query_gh = split_heads(query_glob)
    grad_gh = split_heads(grad_glob)
    key_heads = split_heads(key_doc)
    value_heads = split_heads(value_doc)
    gscores = product('ghd,khd->hgk', query_gh, key_heads) * score_scale
    gscores = jnp.where(local_live[None, None, :], gscores, very_negative)
    largest = lax.optimization_barrier(jnp.max(gscores, axis=2, keepdims=True))
    expo = jnp.where(local_live[None, None, :], jnp.exp(gscores - largest), 0.0)
    gprobs = expo / lax.optimization_barrier(jnp.sum(expo, axis=2, keepdims=True))
    gprobs_low = gprobs.astype(jnp.bfloat16)
    attn_glob = product('hgk,khd->ghd', gprobs_low, value_heads)
    delta_glob = lax.optimization_barrier(jnp.sum(grad_gh.astype(jnp.float32) * attn_glob, axis=2)).T
    gdprob = product('ghd,khd->hgk', grad_gh, value_heads)
    gdscore = (gprobs * (gdprob - delta_glob[:, :, None])).astype(jnp.bfloat16)
    query_suffix = join_heads(product('hgk,khd->ghd', gdscore, key_heads)) * score_scale
    key_add = join_heads(product('hgk,ghd->khd', gdscore, query_gh)) * score_scale
    value_add = join_heads(product('hgk,ghd->khd', gprobs_low, grad_gh))
    attended = attn_band.at[suffix_start:].set(join_heads(attn_glob))
    query_grad = query_band.at[suffix_start:].add(query_suffix)
    key_grad = (key_band + key_add).at[suffix_start:].add(key_suffix)
    value_grad = (value_band + value_add).at[suffix_start:].add(value_suffix)
    return (attended.astype(jnp.bfloat16), query_grad.astype(jnp.bfloat16), key_grad.astype(jnp.bfloat16), value_grad.astype(jnp.bfloat16))

def reference(query_vectors, key_vectors, value_vectors, out_grad, pad_length):
    attended, query_grad, key_grad, value_grad = lax.map(one_doc, (query_vectors, key_vectors, value_vectors, out_grad, pad_length))
    return (attended, query_grad, key_grad, value_grad)
```

```python
import functools
import math

import jax
import jax.numpy as jnp
from jax import lax
from jax.experimental import pallas as pl
from jax.experimental.pallas import tpu as pltpu
from jax.sharding import PartitionSpec as P

D = 1024
H = 16
W = 128
G = 64
HEAD = D // H
PAIR = 2 * HEAD
AHEAD = 2
UP_LAG = 1

MESH = pl.DeviceIdType.MESH
very_negative = -1e30
scale = 1.0 / math.sqrt(HEAD)
f32 = jnp.float32
bf16 = jnp.bfloat16


def dot_nt(a, b):
    return lax.dot_general(a, b, (((1,), (1,)), ((), ())), preferred_element_type=f32)


def dot_nn(a, b):
    return lax.dot_general(a, b, (((1,), (0,)), ((), ())), preferred_element_type=f32)


def dot_tn(a, b):
    return lax.dot_general(a, b, (((0,), (0,)), ((), ())), preferred_element_type=f32)


def iota(shape, dim):
    return lax.broadcasted_iota(jnp.int32, shape, dim)


def pair_mask(value):
    lane = iota((1, PAIR), 1)
    first = jnp.where(lane < HEAD, value, 0.0).astype(bf16)
    second = jnp.where(lane < HEAD, 0.0, value).astype(bf16)
    return first, second


def two_heads(rows, value):
    first, second = pair_mask(value)
    return jnp.concatenate([rows * first, rows * second], axis=0)


def one_pair(stacked):
    half = stacked.shape[0] // 2
    lane = iota((half, PAIR), 1)
    return jnp.where(lane < HEAD, stacked[:half], stacked[half:])


def merge(one, two):
    top = jnp.maximum(one[0], two[0])
    share_one = jnp.exp(one[0] - top)
    share_two = jnp.exp(two[0] - top)
    total = share_one + share_two
    mean = (share_one * one[1] + share_two * two[1]) / total
    return top + jnp.log(total), mean


def kernel(
    n, rows, chunks,
    pad_ref, q_ref, k_ref, v_ref, g_ref,
    att_ref, qgrad_ref, kgrad_ref, vgrad_ref,
    pad, kv, qg, own_qg, stats, bias, key_bias, expo_s, dprob_s,
    band_grad, fin_grad, suf_grad, down_out, down_in, up_out, up_in,
    chain_out, chain_in, add_out, add_in, from_above, to_below, from_below, to_above,
    up_ok, pad_sem, load_sem,
    qg_send, qg_recv, suf_send, suf_recv, low_send, low_recv, high_send, high_recv,
    down_send, down_recv, up_send, up_recv, chain_send, chain_recv, add_send, add_recv,
    fall_send, fall_recv, rise_send, rise_recv,
):
    me = lax.axis_index("seq")
    last = n - 1
    below = lax.rem(me + n - 1, n)
    above = lax.rem(me + 1, n)
    has_below = me > 0
    has_above = me < last
    is_last = me == last
    middle = has_below & has_above
    all_keys = rows + 2 * W + G
    own = slice(W, W + rows)
    low = slice(0, W)
    high = slice(W + rows, 2 * W + rows)
    suf = slice(2 * W + rows, all_keys)
    tail = slice(rows - G, rows)
    near = min(W, rows - G)

    def columns_of(c):
        if isinstance(c, int):
            return pl.ds(c * PAIR, PAIR)
        return pl.ds(pl.multiple_of(c * PAIR, PAIR), PAIR)

    def remote(src, dst, send, recv, target):
        return pltpu.make_async_remote_copy(
            src_ref=src, dst_ref=dst, send_sem=send, recv_sem=recv,
            device_id={"seq": target}, device_id_type=MESH,
        )

    def start_pair(sources, source_rows, target_of, send, recv, target, c):
        for k, source in enumerate(sources):
            remote(
                source.at[0, source_rows, columns_of(c)], target_of(k), send, recv, target
            ).start()

    def send_qg(c):
        return remote(qg.at[c], qg.at[c], qg_send.at[c], qg_recv.at[c], below)

    def send_suf(c):
        return remote(kv.at[c, :, suf], kv.at[c, :, suf], suf_send.at[c], suf_recv.at[c], below)

    def send_low(c):
        return remote(kv.at[c, :, own], kv.at[c, :, high], low_send.at[c], low_recv.at[c], below)

    def send_low_last(c):
        return remote(
            kv.at[c, :, W : W + near],
            kv.at[c, :, W + rows : W + rows + near],
            low_send.at[c], low_recv.at[c], below,
        )

    def send_high(c):
        return remote(kv.at[c, :, own], kv.at[c, :, low], high_send.at[c], high_recv.at[c], above)

    def start_qg_last(c):
        start_pair(
            (q_ref, g_ref), tail, lambda k: qg.at[c, k], qg_send.at[c], qg_recv.at[c], below, c
        )

    def start_suf_last(c):
        start_pair(
            (k_ref, v_ref), tail, lambda k: kv.at[c, k, suf],
            suf_send.at[c], suf_recv.at[c], below, c,
        )

    def start_low(c):
        start_pair(
            (k_ref, v_ref), slice(0, rows), lambda k: kv.at[c, k, high],
            low_send.at[c], low_recv.at[c], below, c,
        )

    def start_low_last(c):
        start_pair(
            (k_ref, v_ref), slice(0, near), lambda k: kv.at[c, k, W + rows : W + rows + near],
            low_send.at[c], low_recv.at[c], below, c,
        )

    def start_high(c):
        start_pair(
            (k_ref, v_ref), slice(0, rows), lambda k: kv.at[c, k, low],
            high_send.at[c], high_recv.at[c], above, c,
        )

    def send_down(c):
        return remote(down_out.at[c], down_in.at[c], down_send.at[c], down_recv.at[c], below)

    def send_up(c):
        return remote(up_out.at[c], up_in.at[c], up_send.at[c], up_recv.at[c], above)

    def send_up_last(c):
        return remote(
            up_out.at[c, :, :near], up_in.at[c, :, :near], up_send.at[c], up_recv.at[c], above
        )

    def send_chain(c):
        return remote(chain_out.at[c], chain_in.at[c], chain_send.at[c], chain_recv.at[c], above)

    def send_add(c):
        return remote(add_out.at[c], add_in.at[c], add_send.at[c], add_recv.at[c], above)

    def send_fall(c):
        return remote(to_below.at[c], from_above.at[c], fall_send.at[c], fall_recv.at[c], below)

    def send_rise(c):
        return remote(to_above.at[c], from_below.at[c], rise_send.at[c], rise_recv.at[c], above)

    barrier = pltpu.get_barrier_semaphore()

    @pl.when(has_above)
    def _():
        pl.semaphore_signal(barrier, inc=1, device_id={"seq": above}, device_id_type=MESH)

    pad_copy = pltpu.make_async_copy(pad_ref, pad, pad_sem)
    pad_copy.start()

    @pl.when(has_below)
    def _():
        pl.semaphore_wait(barrier, 1)
        pl.semaphore_signal(up_ok, inc=1, device_id={"seq": below}, device_id_type=MESH)

    @pl.when(is_last)
    def _():
        for c in range(AHEAD):
            start_qg_last(c)
            start_suf_last(c)

    @pl.when(middle)
    def _():
        for c in range(AHEAD):
            start_low(c)

    loads = []
    for c in range(chunks):
        pieces = (
            (k_ref, kv.at[c, 0, own]),
            (v_ref, kv.at[c, 1, own]),
            (q_ref, own_qg.at[c, 0]),
            (g_ref, own_qg.at[c, 1]),
        )
        for k, (source, target) in enumerate(pieces):
            copy = pltpu.make_async_copy(source.at[0, :, columns_of(c)], target, load_sem.at[c, k])
            copy.start()
            loads.append(copy)

    @pl.when(has_above)
    def _():
        pl.semaphore_wait(up_ok, 1)
        for c in range(chunks):
            start_high(c)

    @pl.when(is_last)
    def _():
        for c in range(chunks):
            kv[c, :, high] = jnp.zeros((2, W, PAIR), bf16)

    @pl.when(me == last - 1)
    def _():
        for c in range(chunks):
            kv[c, :, W + rows + near : 2 * W + rows] = jnp.zeros((2, W - near, PAIR), bf16)

    @pl.when(me == 0)
    def _():
        for c in range(chunks):
            kv[c, :, low] = jnp.zeros((2, W, PAIR), bf16)

    pad_copy.wait()
    suffix_start = rows * n - G
    valid_end = suffix_start - pad[0]
    first_row = me * rows
    j = iota((all_keys, 2 * rows), 0)
    i = iota((all_keys, 2 * rows), 1)
    i = jnp.where(i >= rows, i - rows, i)
    key_pos = first_row - W + j
    apart = i - (j - W)
    within = (apart <= W) & (apart >= -W) & (key_pos >= 0) & (key_pos < valid_end)
    bias[...] = jnp.where(within | (j >= 2 * W + rows), 0.0, very_negative)
    near_pos = first_row - W + iota((W + rows, 2 * G), 0)
    key_bias[...] = jnp.where(
        (near_pos < valid_end) | (near_pos >= suffix_start), 0.0, very_negative
    )
    query_lane = iota((1, 2 * rows), 1)
    query_pos = first_row + jnp.where(query_lane >= rows, query_lane - rows, query_lane)
    row_live = jnp.where(query_pos < suffix_start, 1.0, 0.0)

    for copy in loads:
        copy.wait()

    @pl.when(is_last)
    def _():
        for c in range(chunks):
            qg[c] = own_qg[c, :, tail]
            kv[c, :, suf] = kv[c, :, W + rows - G : W + rows]

    def suffix_stats(c, keys):
        query_two = two_heads(qg[c, 0], scale)
        grad_two = two_heads(qg[c, 1], 1.0)
        scores = dot_nt(kv[c, 0, keys], query_two) + key_bias[keys]
        largest = jnp.max(scores, axis=0, keepdims=True)
        expo = jnp.exp(scores - largest)
        dprob = dot_nt(kv[c, 1, keys], grad_two)
        total = jnp.sum(expo, axis=0, keepdims=True)
        weighted = jnp.sum(expo * dprob, axis=0, keepdims=True)
        expo_s[c, keys] = expo
        dprob_s[c, keys] = dprob
        stats[c, 0:1] = largest
        stats[c, 1:2] = largest + jnp.log(total)
        stats[c, 2:3] = weighted / total

    def pair_of(ref, c, at):
        return ref[c, at : at + 1], ref[c, at + 1 : at + 2]

    def put(ref, c, values):
        ref[c, 0:1] = values[0]
        ref[c, 1:2] = values[1]

    def suffix_parts(c, keys, whole):
        top, delta = whole
        probs = expo_s[c, keys] * jnp.exp(stats[c, 0:1] - top)
        probs_low = probs.astype(bf16)
        dscore = (probs * (dprob_s[c, keys] - delta)).astype(bf16)
        query_two = two_heads(qg[c, 0], scale)
        grad_two = two_heads(qg[c, 1], 1.0)
        att_part = one_pair(dot_tn(probs_low, kv[c, 1, keys]))
        query_part = one_pair(dot_tn(dscore, kv[c, 0, keys])) * scale
        fin_grad[c, 0, keys] = dot_nn(dscore, query_two)
        fin_grad[c, 1, keys] = dot_nn(probs_low, grad_two)
        return att_part, query_part

    both = slice(0, W + rows)

    def suffix_pass(c, carry):
        @pl.when(middle)
        def _():
            send_qg(c).wait_recv()

            @pl.when(me > 1)
            def _():
                send_qg(c).start()

            send_suf(c).wait_recv()
            send_suf(c).start()

        @pl.when(is_last & (c + AHEAD < chunks))
        def _():
            start_qg_last(c + AHEAD)
            start_suf_last(c + AHEAD)

        @pl.when((me == 1) & (c + AHEAD < chunks))
        def _():
            start_low(c + AHEAD)

        @pl.when(me > 1)
        def _():
            suffix_stats(c, own)

            @pl.when(has_above)
            def _():
                send_fall(c).wait_recv()
                put(to_below, c, merge(pair_of(stats, c, 1), pair_of(from_above, c, 0)))

            @pl.when(is_last)
            def _():
                put(to_below, c, pair_of(stats, c, 1))

            send_fall(c).start()

        @pl.when(me == 1)
        def _():
            send_high(c).wait_recv()
            suffix_stats(c, both)
            put(to_above, c, pair_of(stats, c, 1))
            send_rise(c).start()
            send_fall(c).wait_recv()
            whole = merge(pair_of(stats, c, 1), pair_of(from_above, c, 0))
            att_part, query_part = suffix_parts(c, both, whole)
            chain_out[c, 0] = att_part.astype(bf16)
            chain_out[c, 1] = query_part.astype(bf16)
            send_chain(c).start()

        return carry

    @pl.when(has_below)
    def _():
        lax.fori_loop(0, chunks, suffix_pass, 0)

    @pl.when(is_last)
    def _():
        for c in range(chunks):
            start_low_last(c)

    @pl.when(middle & (me > 1))
    def _():
        for c in range(AHEAD, chunks):
            start_low(c)

    def finish(c):
        columns = columns_of(c)
        send_rise(c).wait_recv()
        to_here = merge(pair_of(stats, c, 1), pair_of(from_below, c, 0))

        def parts(whole):
            att_part, query_part = suffix_parts(c, own, whole)
            send_chain(c).wait_recv()
            att_sum = att_part + chain_in[c, 0].astype(f32)
            query_sum = query_part + chain_in[c, 1].astype(f32)
            return att_sum.astype(bf16), query_sum.astype(bf16)

        @pl.when(has_above)
        def _():
            put(to_above, c, to_here)
            send_rise(c).start()
            att_sum, query_sum = parts(merge(to_here, pair_of(from_above, c, 0)))
            chain_out[c, 0] = att_sum
            chain_out[c, 1] = query_sum
            send_chain(c).start()

        @pl.when(is_last)
        def _():
            att_sum, query_sum = parts(to_here)
            att_ref[tail, columns] = att_sum
            qgrad_ref[tail, columns] = query_sum

    def band(c):
        @pl.when(me > 1)
        def _():
            send_high(c).wait_recv()

        @pl.when(me == 0)
        def _():
            send_suf(c).wait_recv()

        @pl.when(me < last - 1)
        def _():
            send_low(c).wait_recv()

        @pl.when(me == last - 1)
        def _():
            send_low_last(c).wait_recv()

        columns = columns_of(c)
        query_two = two_heads(own_qg[c, 0], scale)
        grad_two = two_heads(own_qg[c, 1], 1.0)
        keys = kv[c, 0]
        values = kv[c, 1]
        scores = dot_nt(keys, query_two) + bias[...]
        largest = jnp.max(scores, axis=0, keepdims=True)
        expo = jnp.exp(scores - largest)
        total = jnp.sum(expo, axis=0, keepdims=True)
        dprob = dot_nt(values, grad_two)
        inverse = 1.0 / total
        delta = jnp.sum(expo * dprob, axis=0, keepdims=True) * inverse
        probs = expo * (inverse * row_live)
        probs_low = probs.astype(bf16)
        dscore = (probs * (dprob - delta)).astype(bf16)
        att_ref[:, columns] = one_pair(dot_tn(probs_low, values)).astype(bf16)
        qgrad_ref[:, columns] = (one_pair(dot_tn(dscore, keys)) * scale).astype(bf16)
        key_all = dot_nn(dscore, query_two)
        value_all = dot_nn(probs_low, grad_two)

        @pl.when(me == 1)
        def _():
            down_out[c, 0] = (key_all[low] + fin_grad[c, 0, low]).astype(bf16)
            down_out[c, 1] = (value_all[low] + fin_grad[c, 1, low]).astype(bf16)

        @pl.when(me != 1)
        def _():
            down_out[c, 0] = key_all[low].astype(bf16)
            down_out[c, 1] = value_all[low].astype(bf16)

        @pl.when(me == 0)
        def _():
            add_out[c, 0] = key_all[suf].astype(bf16)
            add_out[c, 1] = value_all[suf].astype(bf16)
            send_add(c).start()

        up_out[c, 0] = key_all[high].astype(bf16)
        up_out[c, 1] = value_all[high].astype(bf16)
        band_grad[c, 0] = key_all[own]
        band_grad[c, 1] = value_all[own]
        suf_grad[c, 0] = key_all[suf]
        suf_grad[c, 1] = value_all[suf]

        @pl.when(has_below)
        def _():
            send_down(c).start()

    def combine(c):
        columns = columns_of(c)

        @pl.when(has_below)
        def _():
            band_grad[c] = band_grad[c] + fin_grad[c, :, own]

            @pl.when(me < last)
            def _():
                send_up(c).wait_recv()
                band_grad[c, :, 0:W] = band_grad[c, :, 0:W] + up_in[c].astype(f32)

            @pl.when(is_last)
            def _():
                send_up_last(c).wait_recv()
                band_grad[c, :, 0:near] = band_grad[c, :, 0:near] + up_in[c, :, 0:near].astype(f32)
                send_add(c).wait_recv()
                band_grad[c, :, tail] = (
                    band_grad[c, :, tail] + suf_grad[c] + add_in[c].astype(f32)
                )

        @pl.when(has_above)
        def _():
            send_down(c).wait_recv()
            band_grad[c, :, rows - W : rows] = band_grad[c, :, rows - W : rows] + down_in[
                c
            ].astype(f32)

        kgrad_ref[:, columns] = band_grad[c, 0].astype(bf16)
        vgrad_ref[:, columns] = band_grad[c, 1].astype(bf16)

    def within_chunks(t):
        return (t >= 0) & (t < chunks)

    def step(t, carry):
        f = jnp.where(is_last, t - chunks, t)

        @pl.when(within_chunks(f) & (me > 1))
        def _():
            finish(f)

        @pl.when(t < chunks)
        def _():
            band(t)

        b = jnp.where(me == 1, t - 1, t - chunks)

        @pl.when(within_chunks(b) & middle)
        def _():
            send_add(b).wait_recv()
            add_out[b] = (suf_grad[b] + add_in[b].astype(f32)).astype(bf16)
            send_add(b).start()

        u = t - UP_LAG

        @pl.when(within_chunks(u))
        def _():
            @pl.when(me < last - 1)
            def _():
                send_up(u).start()

            @pl.when(me == last - 1)
            def _():
                send_up_last(u).start()

        k = jnp.where(me < 2, t - chunks - 1, jnp.where(is_last, t - 2 * chunks, t - chunks - 2))

        @pl.when(within_chunks(k))
        def _():
            combine(k)

        return carry

    lax.fori_loop(0, 3 * chunks, step, 0)

    def drain(c, carry):
        @pl.when(has_below)
        def _():
            send_suf(c).wait_send()
            send_down(c).wait_send()

            @pl.when(has_above)
            def _():
                send_low(c).wait_send()

            @pl.when(is_last)
            def _():
                send_low_last(c).wait_send()

            @pl.when(me > 1)
            def _():
                send_qg(c).wait_send()
                send_fall(c).wait_send()

            @pl.when(has_above)
            def _():
                send_rise(c).wait_send()
                send_chain(c).wait_send()

        @pl.when(has_above)
        def _():
            send_high(c).wait_send()
            send_add(c).wait_send()

        @pl.when(me < last - 1)
        def _():
            send_up(c).wait_send()

        @pl.when(me == last - 1)
        def _():
            send_up_last(c).wait_send()

        return carry

    lax.fori_loop(0, chunks, drain, 0)


def spill(*refs):
    sems = refs[8]
    copies = [
        pltpu.make_async_copy(refs[k], refs[4 + k].at[0], sems.at[k]) for k in range(4)
    ]
    for copy in copies:
        copy.start()
    for copy in copies:
        copy.wait()


def per_device(n, query_vectors, key_vectors, value_vectors, out_grad, pad_length):
    rows, features = query_vectors.shape[1:]
    chunks = features // PAIR
    all_keys = rows + 2 * W + G
    vmem = pl.BlockSpec(memory_space=pltpu.VMEM)
    out = jax.ShapeDtypeStruct((rows, features), bf16)
    dma = pltpu.SemaphoreType.DMA
    hbm = pl.BlockSpec(memory_space=pltpu.HBM)
    outs = pl.pallas_call(
        functools.partial(kernel, n, rows, chunks),
        out_shape=(out,) * 4,
        in_specs=[hbm] * 5,
        out_specs=(vmem,) * 4,
        scratch_shapes=[
            pltpu.SMEM((1,), jnp.int32),
            pltpu.VMEM((chunks, 2, all_keys, PAIR), bf16),
            pltpu.VMEM((chunks, 2, G, PAIR), bf16),
            pltpu.VMEM((chunks, 2, rows, PAIR), bf16),
            pltpu.VMEM((chunks, 8, 2 * G), f32),
            pltpu.VMEM((all_keys, 2 * rows), f32),
            pltpu.VMEM((W + rows, 2 * G), f32),
            pltpu.VMEM((chunks, W + rows, 2 * G), f32),
            pltpu.VMEM((chunks, W + rows, 2 * G), f32),
            pltpu.VMEM((chunks, 2, rows, PAIR), f32),
            pltpu.VMEM((chunks, 2, W + rows, PAIR), f32),
            pltpu.VMEM((chunks, 2, G, PAIR), f32),
        ]
        + [pltpu.VMEM((chunks, 2, W, PAIR), bf16)] * 4
        + [pltpu.VMEM((chunks, 2, G, PAIR), bf16)] * 4
        + [pltpu.VMEM((chunks, 8, 2 * G), f32)] * 4
        + [pltpu.SemaphoreType.REGULAR, dma, dma((chunks, 4))]
        + [dma((chunks,))] * 20,
        compiler_params=pltpu.CompilerParams(
            collective_id=0, has_side_effects=True, vmem_limit_bytes=63 << 20
        ),
    )(pad_length, query_vectors, key_vectors, value_vectors, out_grad)
    anywhere = pl.BlockSpec(memory_space=pl.ANY)
    return pl.pallas_call(
        spill,
        out_shape=(jax.ShapeDtypeStruct((1, rows, features), bf16),) * 4,
        in_specs=[vmem] * 4,
        out_specs=(anywhere,) * 4,
        scratch_shapes=[dma((4,))],
    )(*outs)


def solution(mesh):
    rows = P(("group", "doc"), "seq", None)
    return jax.shard_map(
        functools.partial(per_device, mesh.shape["seq"]),
        mesh=mesh,
        in_specs=(rows, rows, rows, rows, P(("group", "doc"))),
        out_specs=(rows,) * 4,
        check_vma=False,
    )
```

```python
import functools
import math

import jax
import jax.numpy as jnp
from jax import lax
from jax.experimental import pallas as pl
from jax.experimental.pallas import tpu as pltpu
from jax.sharding import PartitionSpec as P

D = 1024
H = 16
W = 128
G = 64
HEAD = D // H
PAIR = 2 * HEAD
AHEAD = 2
HOP_AHEAD = 3
FAR_AHEAD = 5
EARLY = 3
UP_HOLD = 2

MESH = pl.DeviceIdType.MESH
very_negative = -1e30
scale = 1.0 / math.sqrt(HEAD)
f32 = jnp.float32
bf16 = jnp.bfloat16


def dot_nt(a, b):
    return lax.dot_general(a, b, (((1,), (1,)), ((), ())), preferred_element_type=f32)


def dot_nn(a, b):
    return lax.dot_general(a, b, (((1,), (0,)), ((), ())), preferred_element_type=f32)


def dot_tn(a, b):
    return lax.dot_general(a, b, (((0,), (0,)), ((), ())), preferred_element_type=f32)


def iota(shape, dim):
    return lax.broadcasted_iota(jnp.int32, shape, dim)


def pair_mask(value):
    lane = iota((1, PAIR), 1)
    first = jnp.where(lane < HEAD, value, 0.0).astype(bf16)
    second = jnp.where(lane < HEAD, 0.0, value).astype(bf16)
    return first, second


def two_heads(rows, value):
    first, second = pair_mask(value)
    return jnp.concatenate([rows * first, rows * second], axis=0)


def one_pair(stacked):
    half = stacked.shape[0] // 2
    lane = iota((half, PAIR), 1)
    return jnp.where(lane < HEAD, stacked[:half], stacked[half:])


def merge(one, two):
    top = jnp.maximum(one[0], two[0])
    share_one = jnp.exp(one[0] - top)
    share_two = jnp.exp(two[0] - top)
    total = share_one + share_two
    mean = (share_one * one[1] + share_two * two[1]) / total
    return top + jnp.log(total), mean


def kernel(
    n, rows, chunks,
    pad_ref, q_ref, k_ref, v_ref, g_ref,
    att_ref, qgrad_ref, kgrad_ref, vgrad_ref,
    att, qgrad, kgrad, vgrad, pad, kv, qg, own_qg, stats, bias, key_bias, expo_s, dprob_s,
    band_grad, fin_grad, suf_grad, down_out, down_in, up_out, up_in,
    chain_out, chain_in, add_out, add_in, from_above, to_below, from_below, to_above,
    up_ok, pad_sem, load_sem, out_sem,
    qg_send, suf_send, low_send, high_send, down_send, up_send, chain_send, add_send,
    fall_send, rise_send,
    qg_recv, suf_recv, low_recv, high_recv, down_recv, up_recv, chain_recv, add_recv,
    fall_recv, rise_recv,
):
    me = lax.axis_index("seq")
    last = n - 1
    below = lax.rem(me + n - 1, n)
    above = lax.rem(me + 1, n)
    has_below = me > 0
    has_above = me < last
    is_last = me == last
    middle = has_below & has_above
    all_keys = rows + 2 * W + G
    own = slice(W, W + rows)
    low = slice(0, W)
    high = slice(W + rows, 2 * W + rows)
    suf = slice(2 * W + rows, all_keys)
    tail = slice(rows - G, rows)
    near = min(W, rows - G)

    def columns_of(c):
        if isinstance(c, int):
            return pl.ds(c * PAIR, PAIR)
        return pl.ds(pl.multiple_of(c * PAIR, PAIR), PAIR)

    def remote(src, dst, send, recv, target):
        return pltpu.make_async_remote_copy(
            src_ref=src, dst_ref=dst, send_sem=send, recv_sem=recv,
            device_id={"seq": target}, device_id_type=MESH,
        )

    def start_pair(sources, source_rows, target_of, send, recv, target, c):
        for k, source in enumerate(sources):
            remote(
                source.at[0, source_rows, columns_of(c)], target_of(k), send, recv, target
            ).start()

    def send_qg(c):
        return remote(qg.at[c], qg.at[c], qg_send, qg_recv.at[c], below)

    def send_suf(c):
        return remote(kv.at[c, :, suf], kv.at[c, :, suf], suf_send, suf_recv.at[c], below)

    def send_low(c):
        return remote(kv.at[c, :, own], kv.at[c, :, high], low_send, low_recv.at[c], below)

    def send_low_last(c):
        return remote(
            kv.at[c, :, W : W + near],
            kv.at[c, :, W + rows : W + rows + near],
            low_send, low_recv.at[c], below,
        )

    def send_high(c):
        return remote(kv.at[c, :, own], kv.at[c, :, low], high_send, high_recv.at[c], above)

    def start_qg_last(c):
        start_pair(
            (q_ref, g_ref), tail, lambda k: qg.at[c, k], qg_send, qg_recv.at[c], below, c
        )

    def start_suf_last(c):
        start_pair(
            (k_ref, v_ref), tail, lambda k: kv.at[c, k, suf],
            suf_send, suf_recv.at[c], below, c,
        )

    def start_low(c):
        start_pair(
            (k_ref, v_ref), slice(0, rows), lambda k: kv.at[c, k, high],
            low_send, low_recv.at[c], below, c,
        )

    def start_low_last(c):
        start_pair(
            (k_ref, v_ref), slice(0, near), lambda k: kv.at[c, k, W + rows : W + rows + near],
            low_send, low_recv.at[c], below, c,
        )

    def start_high(c):
        start_pair(
            (k_ref, v_ref), slice(0, rows), lambda k: kv.at[c, k, low],
            high_send, high_recv.at[c], above, c,
        )

    def send_down(c):
        return remote(down_out.at[c], down_in.at[c], down_send, down_recv.at[c], below)

    def send_up(c):
        return remote(up_out.at[c], up_in.at[c], up_send, up_recv.at[c], above)

    def send_up_last(c):
        return remote(
            up_out.at[c, :, :near], up_in.at[c, :, :near], up_send, up_recv.at[c], above
        )

    def send_chain(c):
        return remote(chain_out.at[c], chain_in.at[c], chain_send, chain_recv.at[c], above)

    def send_add(c):
        return remote(add_out.at[c], add_in.at[c], add_send, add_recv.at[c], above)

    def send_fall(c):
        return remote(to_below.at[c], from_above.at[c], fall_send, fall_recv.at[c], below)

    def send_rise(c):
        return remote(to_above.at[c], from_below.at[c], rise_send, rise_recv.at[c], above)

    def store(c, k):
        source = (att, qgrad, kgrad, vgrad)[k]
        target = (att_ref, qgrad_ref, kgrad_ref, vgrad_ref)[k]
        return pltpu.make_async_copy(
            source.at[c], target.at[:, columns_of(c)], out_sem.at[k]
        )

    early = min(EARLY, chunks)
    lead = HOP_AHEAD + FAR_AHEAD * (last - 1 - me)
    barrier = pltpu.get_barrier_semaphore()

    @pl.when(has_above)
    def _():
        pl.semaphore_signal(barrier, inc=1, device_id={"seq": above}, device_id_type=MESH)

    pad_copy = pltpu.make_async_copy(pad_ref, pad, pad_sem)
    pad_copy.start()

    @pl.when(has_below)
    def _():
        pl.semaphore_wait(barrier, 1)
        pl.semaphore_signal(up_ok, inc=1, device_id={"seq": below}, device_id_type=MESH)

    @pl.when(is_last)
    def _():
        for c in range(AHEAD):
            start_qg_last(c)
            start_suf_last(c)

    for c in range(chunks):
        @pl.when(middle & (c < lead))
        def _():
            start_low(c)

    for c in range(chunks):
        pieces = (
            (k_ref, kv.at[c, 0, own]),
            (v_ref, kv.at[c, 1, own]),
            (q_ref, own_qg.at[c, 0]),
            (g_ref, own_qg.at[c, 1]),
        )
        for k, (source, target) in enumerate(pieces):
            copy = pltpu.make_async_copy(source.at[0, :, columns_of(c)], target, load_sem.at[k])
            copy.start()

    @pl.when(has_above)
    def _():
        pl.semaphore_wait(up_ok, 1)
        for c in range(chunks):
            start_high(c)

    @pl.when(is_last)
    def _():
        for c in range(chunks):
            kv[c, :, high] = jnp.zeros((2, W, PAIR), bf16)

    @pl.when(me == last - 1)
    def _():
        for c in range(chunks):
            kv[c, :, W + rows + near : 2 * W + rows] = jnp.zeros((2, W - near, PAIR), bf16)

    @pl.when(me == 0)
    def _():
        for c in range(chunks):
            kv[c, :, low] = jnp.zeros((2, W, PAIR), bf16)

    pad_copy.wait()
    suffix_start = rows * n - G
    valid_end = suffix_start - pad[0]
    first_row = me * rows
    j = iota((all_keys, 2 * rows), 0)
    i = iota((all_keys, 2 * rows), 1)
    i = jnp.where(i >= rows, i - rows, i)
    key_pos = first_row - W + j
    apart = i - (j - W)
    within = (apart <= W) & (apart >= -W) & (key_pos >= 0) & (key_pos < valid_end)
    bias[...] = jnp.where(within | (j >= 2 * W + rows), 0.0, very_negative)
    near_pos = first_row - W + iota((W + rows, 2 * G), 0)
    key_bias[...] = jnp.where(
        (near_pos < valid_end) | (near_pos >= suffix_start), 0.0, very_negative
    )
    query_lane = iota((1, 2 * rows), 1)
    query_pos = first_row + jnp.where(query_lane >= rows, query_lane - rows, query_lane)
    row_live = jnp.where(query_pos < suffix_start, 1.0, 0.0)

    loaded = (kv.at[:, 0, own], kv.at[:, 1, own], own_qg.at[:, 0], own_qg.at[:, 1])
    for k, target in enumerate(loaded):
        pltpu.make_async_copy(target, target, load_sem.at[k]).wait()

    @pl.when(is_last)
    def _():
        for c in range(chunks):
            qg[c] = own_qg[c, :, tail]
            kv[c, :, suf] = kv[c, :, W + rows - G : W + rows]

    def suffix_stats(c, keys):
        query_two = two_heads(qg[c, 0], scale)
        grad_two = two_heads(qg[c, 1], 1.0)
        scores = dot_nt(kv[c, 0, keys], query_two) + key_bias[keys]
        largest = jnp.max(scores, axis=0, keepdims=True)
        expo = jnp.exp(scores - largest)
        dprob = dot_nt(kv[c, 1, keys], grad_two)
        total = jnp.sum(expo, axis=0, keepdims=True)
        weighted = jnp.sum(expo * dprob, axis=0, keepdims=True)
        expo_s[c, keys] = expo
        dprob_s[c, keys] = dprob
        stats[c, 0:1] = largest
        stats[c, 1:2] = largest + jnp.log(total)
        stats[c, 2:3] = weighted / total

    def pair_of(ref, c, at):
        return ref[c, at : at + 1], ref[c, at + 1 : at + 2]

    def put(ref, c, values):
        ref[c, 0:1] = values[0]
        ref[c, 1:2] = values[1]

    def suffix_parts(c, keys, whole):
        top, delta = whole
        probs = expo_s[c, keys] * jnp.exp(stats[c, 0:1] - top)
        probs_low = probs.astype(bf16)
        dscore = (probs * (dprob_s[c, keys] - delta)).astype(bf16)
        query_two = two_heads(qg[c, 0], scale)
        grad_two = two_heads(qg[c, 1], 1.0)
        att_part = one_pair(dot_tn(probs_low, kv[c, 1, keys]))
        query_part = one_pair(dot_tn(dscore, kv[c, 0, keys])) * scale
        fin_grad[c, 0, keys] = dot_nn(dscore, query_two)
        fin_grad[c, 1, keys] = dot_nn(probs_low, grad_two)
        return att_part, query_part

    both = slice(0, W + rows)

    def suffix_pass(c):
        @pl.when(middle)
        def _():
            send_qg(c).wait_recv()

            @pl.when(me > 1)
            def _():
                send_qg(c).start()

            send_suf(c).wait_recv()
            send_suf(c).start()

        @pl.when((me == 1) & (c + lead < chunks))
        def _():
            start_low(c + lead)

        @pl.when(me > 1)
        def _():
            suffix_stats(c, own)

        @pl.when(me == 1)
        def _():
            send_high(c).wait_recv()
            suffix_stats(c, both)
            put(to_above, c, pair_of(stats, c, 1))
            send_rise(c).start()

        @pl.when(is_last)
        def _():
            put(to_below, c, pair_of(stats, c, 1))
            send_fall(c).start()

            @pl.when(c + AHEAD < chunks)
            def _():
                start_qg_last(c + AHEAD)
                start_suf_last(c + AHEAD)

        @pl.when((c == chunks - 1) & is_last)
        def _():
            for k in range(chunks):
                start_low_last(k)

    def pass_down(c):
        send_fall(c).wait_recv()
        put(to_below, c, merge(pair_of(stats, c, 1), pair_of(from_above, c, 0)))
        send_fall(c).start()

        @pl.when(c == chunks - 1)
        def _():
            for k in range(chunks):
                @pl.when(k >= lead)
                def _():
                    start_low(k)

    def finish_first(c):
        send_fall(c).wait_recv()
        whole = merge(pair_of(stats, c, 1), pair_of(from_above, c, 0))
        att_part, query_part = suffix_parts(c, both, whole)
        chain_out[c, 0] = att_part.astype(bf16)
        chain_out[c, 1] = query_part.astype(bf16)
        send_chain(c).start()

        @pl.when(c == chunks - 1)
        def _():
            for k in range(early):
                send_down(k).start()

    def finish(c):
        send_rise(c).wait_recv()
        to_here = merge(pair_of(stats, c, 1), pair_of(from_below, c, 0))

        def parts(whole):
            att_part, query_part = suffix_parts(c, own, whole)
            send_chain(c).wait_recv()
            att_sum = att_part + chain_in[c, 0].astype(f32)
            query_sum = query_part + chain_in[c, 1].astype(f32)
            return att_sum.astype(bf16), query_sum.astype(bf16)

        @pl.when(has_above)
        def _():
            put(to_above, c, to_here)
            send_rise(c).start()
            att_sum, query_sum = parts(merge(to_here, pair_of(from_above, c, 0)))
            chain_out[c, 0] = att_sum
            chain_out[c, 1] = query_sum
            send_chain(c).start()

        @pl.when(is_last)
        def _():
            att_sum, query_sum = parts(to_here)
            att[c, tail] = att_sum
            qgrad[c, tail] = query_sum
            store(c, 0).start()
            store(c, 1).start()

    def band(c):
        @pl.when(me > 1)
        def _():
            send_high(c).wait_recv()

        @pl.when(me == 0)
        def _():
            send_suf(c).wait_recv()

        @pl.when(me < last - 1)
        def _():
            send_low(c).wait_recv()

        @pl.when(me == last - 1)
        def _():
            send_low_last(c).wait_recv()

        query_two = two_heads(own_qg[c, 0], scale)
        grad_two = two_heads(own_qg[c, 1], 1.0)
        keys = kv[c, 0]
        values = kv[c, 1]
        scores = dot_nt(keys, query_two) + bias[...]
        largest = jnp.max(scores, axis=0, keepdims=True)
        expo = jnp.exp(scores - largest)
        total = jnp.sum(expo, axis=0, keepdims=True)
        dprob = dot_nt(values, grad_two)
        inverse = 1.0 / total
        delta = jnp.sum(expo * dprob, axis=0, keepdims=True) * inverse
        probs = expo * (inverse * row_live)
        probs_low = probs.astype(bf16)
        dscore = (probs * (dprob - delta)).astype(bf16)
        att[c] = one_pair(dot_tn(probs_low, values)).astype(bf16)
        qgrad[c] = (one_pair(dot_tn(dscore, keys)) * scale).astype(bf16)
        key_all = dot_nn(dscore, query_two)
        value_all = dot_nn(probs_low, grad_two)

        @pl.when(me == 1)
        def _():
            down_out[c, 0] = (key_all[low] + fin_grad[c, 0, low]).astype(bf16)
            down_out[c, 1] = (value_all[low] + fin_grad[c, 1, low]).astype(bf16)

        @pl.when(me != 1)
        def _():
            down_out[c, 0] = key_all[low].astype(bf16)
            down_out[c, 1] = value_all[low].astype(bf16)

        @pl.when(me == 0)
        def _():
            add_out[c, 0] = key_all[suf].astype(bf16)
            add_out[c, 1] = value_all[suf].astype(bf16)
            send_add(c).start()

        up_out[c, 0] = key_all[high].astype(bf16)
        up_out[c, 1] = value_all[high].astype(bf16)
        band_grad[c, 0] = key_all[own]
        band_grad[c, 1] = value_all[own]
        suf_grad[c, 0] = key_all[suf]
        suf_grad[c, 1] = value_all[suf]

        @pl.when(has_below & ((me > 1) | (c >= early)))
        def _():
            send_down(c).start()

        @pl.when(has_above)
        def _():
            store(c, 0).start()
            store(c, 1).start()

    def combine(c):
        @pl.when(has_below)
        def _():
            band_grad[c] = band_grad[c] + fin_grad[c, :, own]

            @pl.when(me < last)
            def _():
                send_up(c).wait_recv()
                band_grad[c, :, 0:W] = band_grad[c, :, 0:W] + up_in[c].astype(f32)

            @pl.when(is_last)
            def _():
                send_up_last(c).wait_recv()
                band_grad[c, :, 0:near] = band_grad[c, :, 0:near] + up_in[c, :, 0:near].astype(f32)
                send_add(c).wait_recv()
                band_grad[c, :, tail] = (
                    band_grad[c, :, tail] + suf_grad[c] + add_in[c].astype(f32)
                )

        @pl.when(has_above)
        def _():
            send_down(c).wait_recv()
            band_grad[c, :, rows - W : rows] = band_grad[c, :, rows - W : rows] + down_in[
                c
            ].astype(f32)

        kgrad[c] = band_grad[c, 0].astype(bf16)
        vgrad[c] = band_grad[c, 1].astype(bf16)
        store(c, 2).start()
        store(c, 3).start()

    def within_chunks(t):
        return (t >= 0) & (t < chunks)

    def by_role(bottom, first, between, top):
        return jnp.where(
            me == 0, bottom, jnp.where(me == 1, first, jnp.where(is_last, top, between))
        )

    never = 0 * me - 1

    def step(t, carry):
        @pl.when((t < chunks) & has_below)
        def _():
            suffix_pass(t)

        @pl.when(within_chunks(t - 1) & (me > 1) & has_above)
        def _():
            pass_down(t - 1)

        @pl.when(within_chunks(t - 1) & (me == 1))
        def _():
            finish_first(t - 1)

        f = jnp.where(is_last, t - 2 * chunks, t - chunks + 1)

        @pl.when(within_chunks(f) & (me > 1))
        def _():
            finish(f)

        first_band = jnp.where(
            t <= early, t - 1, jnp.where(t <= chunks, never, t - chunks - 1 + early)
        )
        b = by_role(t, first_band, t - chunks, t - chunks)

        @pl.when(within_chunks(b))
        def _():
            band(b)

        a = by_role(never, t - chunks - 1, t - 2 * chunks, never)

        @pl.when(within_chunks(a))
        def _():
            send_add(a).wait_recv()
            add_out[a] = (suf_grad[a] + add_in[a].astype(f32)).astype(bf16)
            send_add(a).start()

        held = t - chunks - 1 - UP_HOLD
        first_up = jnp.where(t <= early, t - 1, jnp.where(held < early, never, held))
        u = by_role(t - 1, first_up, t - chunks - 1, never)

        @pl.when(within_chunks(u))
        def _():
            @pl.when(me < last - 1)
            def _():
                send_up(u).start()

            @pl.when(me == last - 1)
            def _():
                send_up_last(u).start()

        k = by_role(
            t - chunks - 1, t - 2 * chunks - 1 - UP_HOLD, t - 2 * chunks - 2, t - 3 * chunks
        )

        @pl.when(within_chunks(k))
        def _():
            combine(k)

        return carry

    steps = by_role(
        2 * chunks + 1, 3 * chunks + 1 + UP_HOLD, 3 * chunks + 2, 4 * chunks
    )
    lax.fori_loop(0, steps, step, 0)

    def sent(source, sem):
        remote(source, source, sem, qg_recv.at[0], below).wait_send()

    @pl.when(has_below)
    def _():
        sent(kv.at[:, :, suf], suf_send)
        sent(down_out, down_send)

        @pl.when(has_above)
        def _():
            sent(kv.at[:, :, own], low_send)
            sent(to_above, rise_send)
            sent(chain_out, chain_send)

        @pl.when(is_last)
        def _():
            sent(kv.at[:, :, W : W + near], low_send)

        @pl.when(me > 1)
        def _():
            sent(qg, qg_send)
            sent(to_below, fall_send)

    @pl.when(has_above)
    def _():
        sent(kv.at[:, :, own], high_send)
        sent(add_out, add_send)

    @pl.when(me < last - 1)
    def _():
        sent(up_out, up_send)

    @pl.when(me == last - 1)
    def _():
        sent(up_out.at[:, :, :near], up_send)

    for k, source in enumerate((att, qgrad, kgrad, vgrad)):
        pltpu.make_async_copy(source, source, out_sem.at[k]).wait()


def spill(*refs):
    sems = refs[8]
    copies = [
        pltpu.make_async_copy(refs[k], refs[4 + k].at[0], sems.at[k]) for k in range(4)
    ]
    for copy in copies:
        copy.start()
    for copy in copies:
        copy.wait()


def per_device(n, query_vectors, key_vectors, value_vectors, out_grad, pad_length):
    rows, features = query_vectors.shape[1:]
    chunks = features // PAIR
    all_keys = rows + 2 * W + G
    vmem = pl.BlockSpec(memory_space=pltpu.VMEM)
    dma = pltpu.SemaphoreType.DMA
    hbm = pl.BlockSpec(memory_space=pltpu.HBM)
    outs = pl.pallas_call(
        functools.partial(kernel, n, rows, chunks),
        out_shape=(pltpu.VMEM((rows, features), bf16),) * 4,
        in_specs=[hbm] * 5,
        out_specs=(pl.BlockSpec(memory_space=pl.ANY),) * 4,
        scratch_shapes=[pltpu.VMEM((chunks, rows, PAIR), bf16)] * 4
        + [
            pltpu.SMEM((1,), jnp.int32),
            pltpu.VMEM((chunks, 2, all_keys, PAIR), bf16),
            pltpu.VMEM((chunks, 2, G, PAIR), bf16),
            pltpu.VMEM((chunks, 2, rows, PAIR), bf16),
            pltpu.VMEM((chunks, 8, 2 * G), f32),
            pltpu.VMEM((all_keys, 2 * rows), f32),
            pltpu.VMEM((W + rows, 2 * G), f32),
            pltpu.VMEM((chunks, W + rows, 2 * G), f32),
            pltpu.VMEM((chunks, W + rows, 2 * G), f32),
            pltpu.VMEM((chunks, 2, rows, PAIR), f32),
            pltpu.VMEM((chunks, 2, W + rows, PAIR), f32),
            pltpu.VMEM((chunks, 2, G, PAIR), f32),
        ]
        + [pltpu.VMEM((chunks, 2, W, PAIR), bf16)] * 4
        + [pltpu.VMEM((chunks, 2, G, PAIR), bf16)] * 4
        + [pltpu.VMEM((chunks, 2, 2 * G), f32)] * 4
        + [pltpu.SemaphoreType.REGULAR, dma] + [dma((4,))] * 2
            + [dma] * 10
        + [dma((chunks,))] * 10,
        compiler_params=pltpu.CompilerParams(
            collective_id=0, has_side_effects=True, vmem_limit_bytes=48 << 20
        ),
    )(pad_length, *(pltpu.with_memory_space_constraint(x, pltpu.HBM) for x in (query_vectors, key_vectors, value_vectors, out_grad)))
    anywhere = pl.BlockSpec(memory_space=pl.ANY)
    return pl.pallas_call(
        spill,
        out_shape=(jax.ShapeDtypeStruct((1, rows, features), bf16),) * 4,
        in_specs=[vmem] * 4,
        out_specs=(anywhere,) * 4,
        scratch_shapes=[dma((4,))],
    )(*(pltpu.with_memory_space_constraint(x, pltpu.VMEM) for x in outs))


def solution(mesh):
    rows = P(("group", "doc"), "seq", None)
    return jax.shard_map(
        functools.partial(per_device, mesh.shape["seq"]),
        mesh=mesh,
        in_specs=(rows, rows, rows, rows, P(("group", "doc"))),
        out_specs=(rows,) * 4,
        check_vma=False,
    )
```

```python
import functools
import math

import jax
import jax.numpy as jnp
from jax import lax
from jax.experimental import pallas as pl
from jax.experimental.pallas import tpu as pltpu
from jax.sharding import PartitionSpec as P

D = 1024
H = 16
W = 128
G = 64
HEAD = D // H
PAIR = 2 * HEAD
AHEAD = 2
HOP_AHEAD = 3
FAR_AHEAD = 2
BOTTOM_HOLD = 4
BETWEEN_HOLD = 8
EARLY = 3
UP_HOLD = 4

MESH = pl.DeviceIdType.MESH
very_negative = -1e30
scale = 1.0 / math.sqrt(HEAD)
f32 = jnp.float32
bf16 = jnp.bfloat16


def dot_nt(a, b):
    return lax.dot_general(a, b, (((1,), (1,)), ((), ())), preferred_element_type=f32)


def dot_nn(a, b):
    return lax.dot_general(a, b, (((1,), (0,)), ((), ())), preferred_element_type=f32)


def dot_tn(a, b):
    return lax.dot_general(a, b, (((0,), (0,)), ((), ())), preferred_element_type=f32)


def iota(shape, dim):
    return lax.broadcasted_iota(jnp.int32, shape, dim)


def pair_mask(value):
    lane = iota((1, PAIR), 1)
    first = jnp.where(lane < HEAD, value, 0.0).astype(bf16)
    second = jnp.where(lane < HEAD, 0.0, value).astype(bf16)
    return first, second


def two_heads(rows, value):
    first, second = pair_mask(value)
    return jnp.concatenate([rows * first, rows * second], axis=0)


def one_pair(stacked):
    half = stacked.shape[0] // 2
    lane = iota((half, PAIR), 1)
    return jnp.where(lane < HEAD, stacked[:half], stacked[half:])


def merge(one, two):
    top = jnp.maximum(one[0], two[0])
    share_one = jnp.exp(one[0] - top)
    share_two = jnp.exp(two[0] - top)
    total = share_one + share_two
    mean = (share_one * one[1] + share_two * two[1]) / total
    return top + jnp.log(total), mean


def kernel(
    n, rows, chunks,
    pad_ref, q_ref, k_ref, v_ref, g_ref,
    att_ref, qgrad_ref, kgrad_ref, vgrad_ref,
    pad, kv, qg, own_qg, stats, bias, key_bias, expo_s, dprob_s,
    band_grad, fin_grad, suf_grad, down_out, down_in, up_out, up_in,
    chain_out, chain_in, add_out, add_in, from_above, to_below, from_below, to_above,
    reply, pad_sem, load_sem,
    qg_send, suf_send, low_send, high_send, down_send, up_send, chain_send, add_send,
    fall_send, rise_send,
    qg_recv, suf_recv, fall_recv, low_recv, chain_recv, add_recv, rise_recv,
    high_recv, down_recv, up_recv,
):
    me = lax.axis_index("seq")
    last = n - 1
    below = lax.rem(me + n - 1, n)
    above = lax.rem(me + 1, n)
    has_below = me > 0
    has_above = me < last
    is_last = me == last
    middle = has_below & has_above
    all_keys = rows + 2 * W + G
    own = slice(W, W + rows)
    low = slice(0, W)
    high = slice(W + rows, 2 * W + rows)
    suf = slice(2 * W + rows, all_keys)
    tail = slice(rows - G, rows)
    near = min(W, rows - G)

    def columns_of(c):
        if isinstance(c, int):
            return pl.ds(c * PAIR, PAIR)
        return pl.ds(pl.multiple_of(c * PAIR, PAIR), PAIR)

    def remote(src, dst, send, recv, target):
        return pltpu.make_async_remote_copy(
            src_ref=src, dst_ref=dst, send_sem=send, recv_sem=recv,
            device_id={"seq": target}, device_id_type=MESH,
        )

    def start_pair(sources, source_rows, target_of, send, recv, target, c):
        for k, source in enumerate(sources):
            remote(
                source.at[0, source_rows, columns_of(c)], target_of(k), send, recv, target
            ).start()

    def send_qg(c):
        return remote(qg.at[c], qg.at[c], qg_send, qg_recv.at[c], below)

    def send_suf(c):
        return remote(kv.at[c, :, suf], kv.at[c, :, suf], suf_send, suf_recv.at[c], below)

    def send_low(c):
        return remote(kv.at[c, :, own], kv.at[c, :, high], low_send, low_recv.at[c], below)

    def send_low_last(c):
        return remote(
            kv.at[c, :, W : W + near],
            kv.at[c, :, W + rows : W + rows + near],
            low_send, low_recv.at[c], below,
        )

    def send_high(c):
        return remote(kv.at[c, :, own], kv.at[c, :, low], high_send, high_recv.at[c // 4], above)

    def start_qg_last(c):
        start_pair(
            (q_ref, g_ref), tail, lambda k: qg.at[c, k], qg_send, qg_recv.at[c], below, c
        )

    def start_suf_last(c):
        start_pair(
            (k_ref, v_ref), tail, lambda k: kv.at[c, k, suf],
            suf_send, suf_recv.at[c], below, c,
        )

    def start_low(c):
        start_pair(
            (k_ref, v_ref), slice(0, rows), lambda k: kv.at[c, k, high],
            low_send, low_recv.at[c], below, c,
        )

    def start_low_last(c):
        start_pair(
            (k_ref, v_ref), slice(0, near), lambda k: kv.at[c, k, W + rows : W + rows + near],
            low_send, low_recv.at[c], below, c,
        )

    def start_high(c):
        start_pair(
            (k_ref, v_ref), slice(0, rows), lambda k: kv.at[c, k, low],
            high_send, high_recv.at[c // 4], above, c,
        )

    def send_down(c):
        return remote(down_out.at[c], down_in.at[c], down_send, down_recv.at[(c + 1) // 2], below)

    def send_up(c):
        return remote(up_out.at[c], up_in.at[c], up_send, up_recv.at[(c + 1) // 2], above)

    def send_up_last(c):
        return remote(
            up_out.at[c, :, :near], up_in.at[c, :, :near], up_send, up_recv.at[(c + 1) // 2], above
        )

    def send_chain(c):
        return remote(chain_out.at[c], chain_in.at[c], chain_send, chain_recv.at[c], above)

    def send_add(c):
        return remote(add_out.at[c], add_in.at[c], add_send, add_recv.at[c], above)

    def send_fall(c):
        return remote(to_below.at[c], from_above.at[c], fall_send, fall_recv.at[c], below)

    def send_rise(c):
        return remote(to_above.at[c], from_below.at[c], rise_send, rise_recv.at[c], above)

    def pairs_from(c, ref, part, sem):
        single = (c == 0) | ((c == chunks - 1) & (c % 2 == 1))

        @pl.when(single)
        def _():
            part_ref = ref.at[pl.ds(c, 1)] if part is None else ref.at[pl.ds(c, 1), :, part]
            pltpu.make_async_copy(part_ref, part_ref, sem.at[(c + 1) // 2]).wait()

        @pl.when((c % 2 == 1) & (c < chunks - 1))
        def _():
            part_ref = ref.at[pl.ds(c, 2)] if part is None else ref.at[pl.ds(c, 2), :, part]
            pltpu.make_async_copy(part_ref, part_ref, sem.at[(c + 1) // 2]).wait()

    def wait_high(c):
        @pl.when(c % 4 == 0)
        def _():
            four = kv.at[pl.ds(c, 4), :, low]
            pltpu.make_async_copy(four, four, high_recv.at[c // 4]).wait()

    early = min(EARLY, chunks)
    lead = HOP_AHEAD + FAR_AHEAD * (last - 1 - me)
    barrier = pltpu.get_barrier_semaphore()

    def tell(sem, target):
        pl.semaphore_signal(sem, inc=1, device_id={"seq": target}, device_id_type=MESH)

    pad_copy = pltpu.make_async_copy(pad_ref, pad, pad_sem)
    if n == 4:
        @pl.when(middle)
        def _():
            tell(barrier, below)
            tell(barrier, above)

        pad_copy.start()
        pl.semaphore_wait(barrier, 1)

        @pl.when(me == 0)
        def _():
            tell(reply, above)

        @pl.when(is_last)
        def _():
            tell(reply, below)
    else:
        @pl.when(has_above)
        def _():
            tell(barrier, above)

        pad_copy.start()

        @pl.when(has_below)
        def _():
            pl.semaphore_wait(barrier, 1)
            tell(reply, below)

    @pl.when(is_last)
    def _():
        for c in range(AHEAD):
            start_qg_last(c)
            start_suf_last(c)

    if n == 4:
        @pl.when(me == 1)
        def _():
            for c in range(chunks):
                start_high(c)
            pl.semaphore_wait(reply, 1)

    for c in range(chunks):
        @pl.when(middle & (c < lead))
        def _():
            start_low(c)

    for c in range(chunks):
        pieces = (
            (k_ref, kv.at[c, 0, own]),
            (v_ref, kv.at[c, 1, own]),
            (q_ref, own_qg.at[c, 0]),
            (g_ref, own_qg.at[c, 1]),
        )
        for k, (source, target) in enumerate(pieces):
            copy = pltpu.make_async_copy(source.at[0, :, columns_of(c)], target, load_sem.at[k // 2])
            copy.start()

    if n == 4:
        @pl.when(me == 2)
        def _():
            pl.semaphore_wait(reply, 1)

        @pl.when((me == 0) | (me == 2))
        def _():
            for c in range(chunks):
                start_high(c)
    else:
        @pl.when(has_above)
        def _():
            pl.semaphore_wait(reply, 1)
            for c in range(chunks):
                start_high(c)

    @pl.when(is_last)
    def _():
        for c in range(chunks):
            kv[c, :, high] = jnp.zeros((2, W, PAIR), bf16)

    @pl.when(me == last - 1)
    def _():
        for c in range(chunks):
            kv[c, :, W + rows + near : 2 * W + rows] = jnp.zeros((2, W - near, PAIR), bf16)

    @pl.when(me == 0)
    def _():
        for c in range(chunks):
            kv[c, :, low] = jnp.zeros((2, W, PAIR), bf16)

    pad_copy.wait()
    suffix_start = rows * n - G
    valid_end = suffix_start - pad[0]
    first_row = me * rows
    j = iota((all_keys, 2 * rows), 0)
    i = iota((all_keys, 2 * rows), 1)
    i = jnp.where(i >= rows, i - rows, i)
    key_pos = first_row - W + j
    apart = i - (j - W)
    within = (apart <= W) & (apart >= -W) & (key_pos >= 0) & (key_pos < valid_end)
    bias[...] = jnp.where(within | (j >= 2 * W + rows), 0.0, very_negative)
    near_pos = first_row - W + iota((W + rows, 2 * G), 0)
    key_bias[...] = jnp.where(
        (near_pos < valid_end) | (near_pos >= suffix_start), 0.0, very_negative
    )
    query_lane = iota((1, 2 * rows), 1)
    query_pos = first_row + jnp.where(query_lane >= rows, query_lane - rows, query_lane)
    row_live = jnp.where(query_pos < suffix_start, 1.0, 0.0)

    loaded = (kv.at[:, :, own], own_qg)
    for k, target in enumerate(loaded):
        pltpu.make_async_copy(target, target, load_sem.at[k]).wait()

    @pl.when(is_last)
    def _():
        for c in range(chunks):
            qg[c] = own_qg[c, :, tail]
            kv[c, :, suf] = kv[c, :, W + rows - G : W + rows]

    def suffix_stats(c, keys):
        query_two = two_heads(qg[c, 0], scale)
        grad_two = two_heads(qg[c, 1], 1.0)
        scores = dot_nt(kv[c, 0, keys], query_two) + key_bias[keys]
        largest = jnp.max(scores, axis=0, keepdims=True)
        expo = jnp.exp(scores - largest)
        dprob = dot_nt(kv[c, 1, keys], grad_two)
        total = jnp.sum(expo, axis=0, keepdims=True)
        weighted = jnp.sum(expo * dprob, axis=0, keepdims=True)
        expo_s[c, keys] = expo
        dprob_s[c, keys] = dprob
        stats[c, 0:1] = largest
        stats[c, 1:2] = largest + jnp.log(total)
        stats[c, 2:3] = weighted / total

    def pair_of(ref, c, at):
        return ref[c, at : at + 1], ref[c, at + 1 : at + 2]

    def put(ref, c, values):
        ref[c, 0:1] = values[0]
        ref[c, 1:2] = values[1]

    def suffix_parts(c, keys, whole):
        top, delta = whole
        probs = expo_s[c, keys] * jnp.exp(stats[c, 0:1] - top)
        probs_low = probs.astype(bf16)
        dscore = (probs * (dprob_s[c, keys] - delta)).astype(bf16)
        query_two = two_heads(qg[c, 0], scale)
        grad_two = two_heads(qg[c, 1], 1.0)
        att_part = one_pair(dot_tn(probs_low, kv[c, 1, keys]))
        query_part = one_pair(dot_tn(dscore, kv[c, 0, keys])) * scale
        fin_grad[c, 0, keys] = dot_nn(dscore, query_two)
        fin_grad[c, 1, keys] = dot_nn(probs_low, grad_two)
        return att_part, query_part

    both = slice(0, W + rows)

    def suffix_pass(c):
        @pl.when(middle)
        def _():
            send_qg(c).wait_recv()

            @pl.when(me > 1)
            def _():
                send_qg(c).start()

            send_suf(c).wait_recv()
            send_suf(c).start()

        @pl.when((me == 1) & (c % 2 == 1) & (lead + c // 2 < chunks))
        def _():
            start_low(lead + c // 2)

        @pl.when(me > 1)
        def _():
            suffix_stats(c, own)

        @pl.when(me == 1)
        def _():
            wait_high(c)
            suffix_stats(c, both)
            put(to_above, c, pair_of(stats, c, 1))
            send_rise(c).start()

        @pl.when(is_last)
        def _():
            put(to_below, c, pair_of(stats, c, 1))
            send_fall(c).start()

            @pl.when(c + AHEAD < chunks)
            def _():
                start_qg_last(c + AHEAD)
                start_suf_last(c + AHEAD)

        @pl.when((c == chunks - 1) & is_last)
        def _():
            for k in range(chunks):
                start_low_last(k)

    def pass_down(c):
        send_fall(c).wait_recv()
        put(to_below, c, merge(pair_of(stats, c, 1), pair_of(from_above, c, 0)))
        send_fall(c).start()

        @pl.when(c == chunks - 1)
        def _():
            for k in range(chunks):
                @pl.when(k >= lead)
                def _():
                    start_low(k)

    def finish_first(c):
        send_fall(c).wait_recv()
        whole = merge(pair_of(stats, c, 1), pair_of(from_above, c, 0))
        att_part, query_part = suffix_parts(c, both, whole)
        chain_out[c, 0] = att_part.astype(bf16)
        chain_out[c, 1] = query_part.astype(bf16)
        send_chain(c).start()

        @pl.when(c == chunks - 1)
        def _():
            for k in range(early):
                send_down(k).start()

    def finish(c):
        send_rise(c).wait_recv()
        to_here = merge(pair_of(stats, c, 1), pair_of(from_below, c, 0))

        def parts(whole):
            att_part, query_part = suffix_parts(c, own, whole)
            send_chain(c).wait_recv()
            att_sum = att_part + chain_in[c, 0].astype(f32)
            query_sum = query_part + chain_in[c, 1].astype(f32)
            return att_sum.astype(bf16), query_sum.astype(bf16)

        @pl.when(has_above)
        def _():
            put(to_above, c, to_here)
            send_rise(c).start()
            att_sum, query_sum = parts(merge(to_here, pair_of(from_above, c, 0)))
            chain_out[c, 0] = att_sum
            chain_out[c, 1] = query_sum
            send_chain(c).start()

        @pl.when(is_last)
        def _():
            att_sum, query_sum = parts(to_here)
            att_ref[tail, columns_of(c)] = att_sum
            qgrad_ref[tail, columns_of(c)] = query_sum

    def band(c):
        @pl.when(me > 1)
        def _():
            wait_high(c)

        @pl.when(me == 0)
        def _():
            send_suf(c).wait_recv()

        @pl.when(me < last - 1)
        def _():
            send_low(c).wait_recv()

        @pl.when(me == last - 1)
        def _():
            send_low_last(c).wait_recv()

        query_two = two_heads(own_qg[c, 0], scale)
        grad_two = two_heads(own_qg[c, 1], 1.0)
        keys = kv[c, 0]
        values = kv[c, 1]
        scores = dot_nt(keys, query_two) + bias[...]
        largest = jnp.max(scores, axis=0, keepdims=True)
        expo = jnp.exp(scores - largest)
        total = jnp.sum(expo, axis=0, keepdims=True)
        dprob = dot_nt(values, grad_two)
        inverse = 1.0 / total
        delta = jnp.sum(expo * dprob, axis=0, keepdims=True) * inverse
        probs = expo * (inverse * row_live)
        probs_low = probs.astype(bf16)
        dscore = (probs * (dprob - delta)).astype(bf16)
        att_ref[:, columns_of(c)] = one_pair(dot_tn(probs_low, values)).astype(bf16)
        qgrad_ref[:, columns_of(c)] = (one_pair(dot_tn(dscore, keys)) * scale).astype(bf16)
        key_all = dot_nn(dscore, query_two)
        value_all = dot_nn(probs_low, grad_two)

        @pl.when(me == 1)
        def _():
            down_out[c, 0] = (key_all[low] + fin_grad[c, 0, low]).astype(bf16)
            down_out[c, 1] = (value_all[low] + fin_grad[c, 1, low]).astype(bf16)

        @pl.when(me != 1)
        def _():
            down_out[c, 0] = key_all[low].astype(bf16)
            down_out[c, 1] = value_all[low].astype(bf16)

        @pl.when(me == 0)
        def _():
            add_out[c, 0] = key_all[suf].astype(bf16)
            add_out[c, 1] = value_all[suf].astype(bf16)
            send_add(c).start()

        up_out[c, 0] = key_all[high].astype(bf16)
        up_out[c, 1] = value_all[high].astype(bf16)
        band_grad[c, 0] = key_all[own]
        band_grad[c, 1] = value_all[own]
        suf_grad[c, 0] = key_all[suf]
        suf_grad[c, 1] = value_all[suf]

        @pl.when(has_below & ((me > 1) | (c >= early)))
        def _():
            send_down(c).start()

    def combine(c):
        @pl.when(has_below)
        def _():
            band_grad[c] = band_grad[c] + fin_grad[c, :, own]

            @pl.when(me < last)
            def _():
                pairs_from(c, up_in, None, up_recv)
                band_grad[c, :, 0:W] = band_grad[c, :, 0:W] + up_in[c].astype(f32)

            @pl.when(is_last)
            def _():
                pairs_from(c, up_in, slice(0, near), up_recv)
                band_grad[c, :, 0:near] = band_grad[c, :, 0:near] + up_in[c, :, 0:near].astype(f32)
                send_add(c).wait_recv()
                band_grad[c, :, tail] = (
                    band_grad[c, :, tail] + suf_grad[c] + add_in[c].astype(f32)
                )

        @pl.when(has_above)
        def _():
            pairs_from(c, down_in, None, down_recv)
            band_grad[c, :, rows - W : rows] = band_grad[c, :, rows - W : rows] + down_in[
                c
            ].astype(f32)

        kgrad_ref[:, columns_of(c)] = band_grad[c, 0].astype(bf16)
        vgrad_ref[:, columns_of(c)] = band_grad[c, 1].astype(bf16)

    def within_chunks(t):
        return (t >= 0) & (t < chunks)

    def by_role(bottom, first, between, top):
        return jnp.where(
            me == 0, bottom, jnp.where(me == 1, first, jnp.where(is_last, top, between))
        )

    never = 0 * me - 1

    def step(t, carry):
        @pl.when((t < chunks) & has_below)
        def _():
            suffix_pass(t)

        @pl.when(within_chunks(t - 1) & (me > 1) & has_above)
        def _():
            pass_down(t - 1)

        @pl.when(within_chunks(t - 1) & (me == 1))
        def _():
            finish_first(t - 1)

        first_band = jnp.where(
            t <= early, t - 1, jnp.where(t <= chunks, never, t - chunks - 1 + early)
        )
        b = by_role(t, first_band, t - chunks, t - chunks)

        @pl.when(within_chunks(b))
        def _():
            band(b)

        f = jnp.where(is_last, t - 2 * chunks, t - chunks + 1)

        @pl.when(within_chunks(f) & (me > 1))
        def _():
            finish(f)

        a = by_role(never, t - chunks - 1, t - 2 * chunks, never)

        @pl.when(within_chunks(a))
        def _():
            send_add(a).wait_recv()
            add_out[a] = (suf_grad[a] + add_in[a].astype(f32)).astype(bf16)
            send_add(a).start()

        held = t - chunks - 1 - UP_HOLD
        first_up = jnp.where(t <= early, t - 1, jnp.where(held < early, never, held))
        u = by_role(t - 1 - BOTTOM_HOLD, first_up, t - chunks - 1, never)

        @pl.when(within_chunks(u))
        def _():
            @pl.when(me < last - 1)
            def _():
                send_up(u).start()

            @pl.when(me == last - 1)
            def _():
                send_up_last(u).start()

        k = by_role(
            t - chunks - 1, t - 2 * chunks - 1 - UP_HOLD, t - 2 * chunks - BETWEEN_HOLD, t - 3 * chunks
        )

        @pl.when(within_chunks(k))
        def _():
            combine(k)

        return carry

    steps = by_role(
        2 * chunks + 1 + BOTTOM_HOLD, 3 * chunks + 1 + UP_HOLD, 3 * chunks + BETWEEN_HOLD, 4 * chunks
    )
    lax.fori_loop(0, steps, step, 0)

    def sent(source, sem):
        remote(source, source, sem, qg_recv.at[0], below).wait_send()

    @pl.when(has_below)
    def _():
        sent(kv.at[:, :, suf], suf_send)
        sent(down_out, down_send)

        @pl.when(has_above)
        def _():
            sent(kv.at[:, :, own], low_send)
            sent(to_above, rise_send)
            sent(chain_out, chain_send)

        @pl.when(is_last)
        def _():
            sent(kv.at[:, :, W : W + near], low_send)

        @pl.when(me > 1)
        def _():
            sent(qg, qg_send)
            sent(to_below, fall_send)

    @pl.when(has_above)
    def _():
        sent(kv.at[:, :, own], high_send)
        sent(add_out, add_send)

    @pl.when(me < last - 1)
    def _():
        sent(up_out, up_send)

    @pl.when(me == last - 1)
    def _():
        sent(up_out.at[:, :, :near], up_send)


def spill(*refs):
    sems = refs[8]
    copies = [
        pltpu.make_async_copy(refs[k], refs[4 + k].at[0], sems.at[k]) for k in range(4)
    ]
    for copy in copies:
        copy.start()
    for copy in copies:
        copy.wait()


def per_device(n, query_vectors, key_vectors, value_vectors, out_grad, pad_length):
    rows, features = query_vectors.shape[1:]
    chunks = features // PAIR
    all_keys = rows + 2 * W + G
    vmem = pl.BlockSpec(memory_space=pltpu.VMEM)
    dma = pltpu.SemaphoreType.DMA
    hbm = pl.BlockSpec(memory_space=pltpu.HBM)
    outs = pl.pallas_call(
        functools.partial(kernel, n, rows, chunks),
        out_shape=(pltpu.VMEM((rows, features), bf16),) * 4,
        in_specs=[hbm] * 5,
        out_specs=(vmem,) * 4,
        scratch_shapes=[
            pltpu.SMEM((1,), jnp.int32),
            pltpu.VMEM((chunks, 2, all_keys, PAIR), bf16),
            pltpu.VMEM((chunks, 2, G, PAIR), bf16),
            pltpu.VMEM((chunks, 2, rows, PAIR), bf16),
            pltpu.VMEM((chunks, 8, 2 * G), f32),
            pltpu.VMEM((all_keys, 2 * rows), f32),
            pltpu.VMEM((W + rows, 2 * G), f32),
            pltpu.VMEM((chunks, W + rows, 2 * G), f32),
            pltpu.VMEM((chunks, W + rows, 2 * G), f32),
            pltpu.VMEM((chunks, 2, rows, PAIR), f32),
            pltpu.VMEM((chunks, 2, W + rows, PAIR), f32),
            pltpu.VMEM((chunks, 2, G, PAIR), f32),
        ]
        + [pltpu.VMEM((chunks, 2, W, PAIR), bf16)] * 4
        + [pltpu.VMEM((chunks, 2, G, PAIR), bf16)] * 4
        + [pltpu.VMEM((chunks, 2, 2 * G), f32)] * 4
        + [pltpu.SemaphoreType.REGULAR, dma, dma((2,))]
            + [dma] * 10
        + [dma((chunks,))] * 7
        + [dma((chunks // 4,))]
        + [dma((chunks // 2 + 1,))] * 2,
        compiler_params=pltpu.CompilerParams(
            collective_id=0, has_side_effects=True, vmem_limit_bytes=48 << 20
        ),
    )(pad_length, *(pltpu.with_memory_space_constraint(x, pltpu.HBM) for x in (query_vectors, key_vectors, value_vectors, out_grad)))
    anywhere = pl.BlockSpec(memory_space=pl.ANY)
    return pl.pallas_call(
        spill,
        out_shape=(jax.ShapeDtypeStruct((1, rows, features), bf16),) * 4,
        in_specs=[vmem] * 4,
        out_specs=(anywhere,) * 4,
        scratch_shapes=[dma((4,))],
    )(*(pltpu.with_memory_space_constraint(x, pltpu.VMEM) for x in outs))


def solution(mesh):
    rows = P(("group", "doc"), "seq", None)
    return jax.shard_map(
        functools.partial(per_device, mesh.shape["seq"]),
        mesh=mesh,
        in_specs=(rows, rows, rows, rows, P(("group", "doc"))),
        out_specs=(rows,) * 4,
        check_vma=False,
    )
```

```python
import functools
import math

import jax
import jax.numpy as jnp
from jax import lax
from jax.experimental import pallas as pl
from jax.experimental.pallas import tpu as pltpu
from jax.sharding import PartitionSpec as P

D = 1024
H = 16
W = 128
G = 64
HEAD = D // H
PAIR = 2 * HEAD
AHEAD = 2
HOP_AHEAD = 3
FAR_AHEAD = 2
BOTTOM_HOLD = 6
BETWEEN_HOLD = 8
EARLY = 3
UP_HOLD = 1
UP_TURN = 2
UP_FREE = 2
FIRST_ADD = 0
BETWEEN_ADD = 6
FIRST_LAST = 3

MESH = pl.DeviceIdType.MESH
very_negative = -1e30
scale = 1.0 / math.sqrt(HEAD)
f32 = jnp.float32
bf16 = jnp.bfloat16


def dot_nt(a, b):
    return lax.dot_general(a, b, (((1,), (1,)), ((), ())), preferred_element_type=f32)


def dot_nn(a, b):
    return lax.dot_general(a, b, (((1,), (0,)), ((), ())), preferred_element_type=f32)


def dot_tn(a, b):
    return lax.dot_general(a, b, (((0,), (0,)), ((), ())), preferred_element_type=f32)


def iota(shape, dim):
    return lax.broadcasted_iota(jnp.int32, shape, dim)


def pair_mask(value):
    lane = iota((1, PAIR), 1)
    first = jnp.where(lane < HEAD, value, 0.0).astype(bf16)
    second = jnp.where(lane < HEAD, 0.0, value).astype(bf16)
    return first, second


def two_heads(rows, value):
    first, second = pair_mask(value)
    return jnp.concatenate([rows * first, rows * second], axis=0)


def one_pair(stacked):
    half = stacked.shape[0] // 2
    lane = iota((half, PAIR), 1)
    return jnp.where(lane < HEAD, stacked[:half], stacked[half:])


def merge(one, two):
    top = jnp.maximum(one[0], two[0])
    share_one = jnp.exp(one[0] - top)
    share_two = jnp.exp(two[0] - top)
    total = share_one + share_two
    mean = (share_one * one[1] + share_two * two[1]) / total
    return top + jnp.log(total), mean


def kernel(
    n, rows, chunks,
    pad_ref, q_ref, k_ref, v_ref, g_ref,
    att_ref, qgrad_ref, kgrad_ref, vgrad_ref,
    pad, kv, qg, own_qg, stats, bias, key_bias, expo_s, dprob_s,
    band_grad, fin_grad, suf_grad, down_out, down_in, up_out, up_in,
    chain_out, chain_in, add_out, add_in, from_above, to_below, from_below, to_above,
    reply, pad_sem, load_sem,
    qg_send, suf_send, low_send, high_send, down_send, up_send, chain_send, add_send,
    fall_send, rise_send,
    qg_recv, suf_recv, fall_recv, low_recv, chain_recv, add_recv, rise_recv,
    high_recv, down_recv, up_recv,
):
    me = lax.axis_index("seq")
    last = n - 1
    below = lax.rem(me + n - 1, n)
    above = lax.rem(me + 1, n)
    has_below = me > 0
    has_above = me < last
    is_last = me == last
    middle = has_below & has_above
    all_keys = rows + 2 * W + G
    own = slice(W, W + rows)
    low = slice(0, W)
    high = slice(W + rows, 2 * W + rows)
    suf = slice(2 * W + rows, all_keys)
    tail = slice(rows - G, rows)
    near = min(W, rows - G)

    def columns_of(c):
        if isinstance(c, int):
            return pl.ds(c * PAIR, PAIR)
        return pl.ds(pl.multiple_of(c * PAIR, PAIR), PAIR)

    def remote(src, dst, send, recv, target):
        return pltpu.make_async_remote_copy(
            src_ref=src, dst_ref=dst, send_sem=send, recv_sem=recv,
            device_id={"seq": target}, device_id_type=MESH,
        )

    def start_pair(sources, source_rows, target_of, send, recv, target, c):
        for k, source in enumerate(sources):
            remote(
                source.at[0, source_rows, columns_of(c)], target_of(k), send, recv, target
            ).start()

    def send_qg(c):
        return remote(qg.at[c], qg.at[c], qg_send, qg_recv.at[c], below)

    def send_suf(c):
        return remote(kv.at[c, :, suf], kv.at[c, :, suf], suf_send, suf_recv.at[c], below)

    def send_low(c):
        return remote(kv.at[c, :, own], kv.at[c, :, high], low_send, low_recv.at[c], below)

    def send_low_last(c):
        return remote(
            kv.at[c, :, W : W + near],
            kv.at[c, :, W + rows : W + rows + near],
            low_send, low_recv.at[c], below,
        )

    def send_high(c):
        return remote(kv.at[c, :, own], kv.at[c, :, low], high_send, high_recv.at[c // 4], above)

    def start_qg_last(c):
        start_pair(
            (q_ref, g_ref), tail, lambda k: qg.at[c, k], qg_send, qg_recv.at[c], below, c
        )

    def start_suf_last(c):
        start_pair(
            (k_ref, v_ref), tail, lambda k: kv.at[c, k, suf],
            suf_send, suf_recv.at[c], below, c,
        )

    def start_low(c):
        start_pair(
            (k_ref, v_ref), slice(0, rows), lambda k: kv.at[c, k, high],
            low_send, low_recv.at[c], below, c,
        )

    def start_low_last(c):
        start_pair(
            (k_ref, v_ref), slice(0, near), lambda k: kv.at[c, k, W + rows : W + rows + near],
            low_send, low_recv.at[c], below, c,
        )

    def start_high(c):
        start_pair(
            (k_ref, v_ref), slice(0, rows), lambda k: kv.at[c, k, low],
            high_send, high_recv.at[c // 4], above, c,
        )

    def send_down(c):
        return remote(down_out.at[c], down_in.at[c], down_send, down_recv.at[(c + 1) // 2], below)

    def send_up(c):
        return remote(up_out.at[c], up_in.at[c], up_send, up_recv.at[(c + 1) // 2], above)

    def send_up_last(c):
        return remote(
            up_out.at[c, :, :near], up_in.at[c, :, :near], up_send, up_recv.at[(c + 1) // 2], above
        )

    def send_chain(c):
        return remote(chain_out.at[c], chain_in.at[c], chain_send, chain_recv.at[c], above)

    def send_add(c):
        return remote(add_out.at[c], add_in.at[c], add_send, add_recv.at[c], above)

    def send_fall(c):
        return remote(to_below.at[c], from_above.at[c], fall_send, fall_recv.at[c], below)

    def send_rise(c):
        return remote(to_above.at[c], from_below.at[c], rise_send, rise_recv.at[c], above)

    def pairs_from(c, ref, part, sem):
        single = (c == 0) | ((c == chunks - 1) & (c % 2 == 1))

        @pl.when(single)
        def _():
            part_ref = ref.at[pl.ds(c, 1)] if part is None else ref.at[pl.ds(c, 1), :, part]
            pltpu.make_async_copy(part_ref, part_ref, sem.at[(c + 1) // 2]).wait()

        @pl.when((c % 2 == 1) & (c < chunks - 1))
        def _():
            part_ref = ref.at[pl.ds(c, 2)] if part is None else ref.at[pl.ds(c, 2), :, part]
            pltpu.make_async_copy(part_ref, part_ref, sem.at[(c + 1) // 2]).wait()

    def wait_high(c):
        @pl.when(c % 4 == 0)
        def _():
            four = kv.at[pl.ds(c, 4), :, low]
            pltpu.make_async_copy(four, four, high_recv.at[c // 4]).wait()

    early = min(EARLY, chunks)
    lead = HOP_AHEAD + FAR_AHEAD * (last - 1 - me)
    barrier = pltpu.get_barrier_semaphore()

    def tell(sem, target):
        pl.semaphore_signal(sem, inc=1, device_id={"seq": target}, device_id_type=MESH)

    pad_copy = pltpu.make_async_copy(pad_ref, pad, pad_sem)
    if n == 4:
        @pl.when(middle)
        def _():
            tell(barrier, below)
            tell(barrier, above)

        pad_copy.start()
        pl.semaphore_wait(barrier, 1)

        @pl.when(me == 0)
        def _():
            tell(reply, above)

        @pl.when(is_last)
        def _():
            tell(reply, below)
    else:
        @pl.when(has_above)
        def _():
            tell(barrier, above)

        pad_copy.start()

        @pl.when(has_below)
        def _():
            pl.semaphore_wait(barrier, 1)
            tell(reply, below)

    @pl.when(is_last)
    def _():
        for c in range(AHEAD):
            start_qg_last(c)
            start_suf_last(c)

    if n == 4:
        @pl.when(me == 1)
        def _():
            for c in range(chunks):
                start_high(c)
            pl.semaphore_wait(reply, 1)

    for c in range(chunks):
        @pl.when(middle & (c < lead))
        def _():
            start_low(c)

    for c in range(chunks):
        pieces = (
            (k_ref, kv.at[c, 0, own]),
            (v_ref, kv.at[c, 1, own]),
            (q_ref, own_qg.at[c, 0]),
            (g_ref, own_qg.at[c, 1]),
        )
        for k, (source, target) in enumerate(pieces):
            copy = pltpu.make_async_copy(source.at[0, :, columns_of(c)], target, load_sem.at[k // 2])
            copy.start()

    if n == 4:
        @pl.when(me == 2)
        def _():
            pl.semaphore_wait(reply, 1)

        @pl.when((me == 0) | (me == 2))
        def _():
            for c in range(chunks):
                start_high(c)
    else:
        @pl.when(has_above)
        def _():
            pl.semaphore_wait(reply, 1)
            for c in range(chunks):
                start_high(c)

    @pl.when(is_last)
    def _():
        for c in range(chunks):
            kv[c, :, high] = jnp.zeros((2, W, PAIR), bf16)

    @pl.when(me == last - 1)
    def _():
        for c in range(chunks):
            kv[c, :, W + rows + near : 2 * W + rows] = jnp.zeros((2, W - near, PAIR), bf16)

    @pl.when(me == 0)
    def _():
        for c in range(chunks):
            kv[c, :, low] = jnp.zeros((2, W, PAIR), bf16)

    pad_copy.wait()
    suffix_start = rows * n - G
    valid_end = suffix_start - pad[0]
    first_row = me * rows
    j = iota((all_keys, 2 * rows), 0)
    i = iota((all_keys, 2 * rows), 1)
    i = jnp.where(i >= rows, i - rows, i)
    key_pos = first_row - W + j
    apart = i - (j - W)
    within = (apart <= W) & (apart >= -W) & (key_pos >= 0) & (key_pos < valid_end)
    bias[...] = jnp.where(within | (j >= 2 * W + rows), 0.0, very_negative)
    near_pos = first_row - W + iota((W + rows, 2 * G), 0)
    key_bias[...] = jnp.where(
        (near_pos < valid_end) | (near_pos >= suffix_start), 0.0, very_negative
    )
    query_lane = iota((1, 2 * rows), 1)
    query_pos = first_row + jnp.where(query_lane >= rows, query_lane - rows, query_lane)
    row_live = jnp.where(query_pos < suffix_start, 1.0, 0.0)

    loaded = (kv.at[:, :, own], own_qg)
    for k, target in enumerate(loaded):
        pltpu.make_async_copy(target, target, load_sem.at[k]).wait()

    @pl.when(is_last)
    def _():
        for c in range(chunks):
            qg[c] = own_qg[c, :, tail]
            kv[c, :, suf] = kv[c, :, W + rows - G : W + rows]

    def suffix_stats(c, keys):
        query_two = two_heads(qg[c, 0], scale)
        grad_two = two_heads(qg[c, 1], 1.0)
        scores = dot_nt(kv[c, 0, keys], query_two) + key_bias[keys]
        largest = jnp.max(scores, axis=0, keepdims=True)
        expo = jnp.exp(scores - largest)
        dprob = dot_nt(kv[c, 1, keys], grad_two)
        total = jnp.sum(expo, axis=0, keepdims=True)
        weighted = jnp.sum(expo * dprob, axis=0, keepdims=True)
        expo_s[c, keys] = expo
        dprob_s[c, keys] = dprob
        stats[c, 0:1] = largest
        stats[c, 1:2] = largest + jnp.log(total)
        stats[c, 2:3] = weighted / total

    def pair_of(ref, c, at):
        return ref[c, at : at + 1], ref[c, at + 1 : at + 2]

    def put(ref, c, values):
        ref[c, 0:1] = values[0]
        ref[c, 1:2] = values[1]

    def suffix_parts(c, keys, whole):
        top, delta = whole
        probs = expo_s[c, keys] * jnp.exp(stats[c, 0:1] - top)
        probs_low = probs.astype(bf16)
        dscore = (probs * (dprob_s[c, keys] - delta)).astype(bf16)
        query_two = two_heads(qg[c, 0], scale)
        grad_two = two_heads(qg[c, 1], 1.0)
        att_part = one_pair(dot_tn(probs_low, kv[c, 1, keys]))
        query_part = one_pair(dot_tn(dscore, kv[c, 0, keys])) * scale
        fin_grad[c, 0, keys] = dot_nn(dscore, query_two)
        fin_grad[c, 1, keys] = dot_nn(probs_low, grad_two)
        return att_part, query_part

    both = slice(0, W + rows)

    def suffix_pass(c):
        @pl.when(middle)
        def _():
            send_qg(c).wait_recv()

            @pl.when(me > 1)
            def _():
                send_qg(c).start()

            send_suf(c).wait_recv()
            send_suf(c).start()

        @pl.when((me == 1) & (c % 2 == 1) & (lead + c // 2 < chunks))
        def _():
            start_low(lead + c // 2)

        @pl.when(me > 1)
        def _():
            suffix_stats(c, own)

        @pl.when(me == 1)
        def _():
            wait_high(c)
            suffix_stats(c, both)
            put(to_above, c, pair_of(stats, c, 1))
            send_rise(c).start()

        @pl.when(is_last)
        def _():
            put(to_below, c, pair_of(stats, c, 1))
            send_fall(c).start()

            @pl.when(c + AHEAD < chunks)
            def _():
                start_qg_last(c + AHEAD)
                start_suf_last(c + AHEAD)

        @pl.when((c == chunks - 1) & is_last)
        def _():
            for k in range(chunks):
                start_low_last(k)

    def pass_down(c):
        send_fall(c).wait_recv()
        put(to_below, c, merge(pair_of(stats, c, 1), pair_of(from_above, c, 0)))
        send_fall(c).start()

        @pl.when(c == chunks - 1)
        def _():
            for k in range(chunks):
                @pl.when(k >= lead)
                def _():
                    start_low(k)

    def finish_first(c):
        send_fall(c).wait_recv()
        whole = merge(pair_of(stats, c, 1), pair_of(from_above, c, 0))
        att_part, query_part = suffix_parts(c, both, whole)
        chain_out[c, 0] = att_part.astype(bf16)
        chain_out[c, 1] = query_part.astype(bf16)
        send_chain(c).start()

        @pl.when(c == chunks - 1)
        def _():
            for k in range(early):
                send_down(k).start()

    def finish(c):
        send_rise(c).wait_recv()
        to_here = merge(pair_of(stats, c, 1), pair_of(from_below, c, 0))

        def parts(whole):
            att_part, query_part = suffix_parts(c, own, whole)
            send_chain(c).wait_recv()
            att_sum = att_part + chain_in[c, 0].astype(f32)
            query_sum = query_part + chain_in[c, 1].astype(f32)
            return att_sum.astype(bf16), query_sum.astype(bf16)

        @pl.when(has_above)
        def _():
            put(to_above, c, to_here)
            send_rise(c).start()
            att_sum, query_sum = parts(merge(to_here, pair_of(from_above, c, 0)))
            chain_out[c, 0] = att_sum
            chain_out[c, 1] = query_sum
            send_chain(c).start()

        @pl.when(is_last)
        def _():
            att_sum, query_sum = parts(to_here)
            att_ref[tail, columns_of(c)] = att_sum
            qgrad_ref[tail, columns_of(c)] = query_sum

    def band(c):
        @pl.when(me > 1)
        def _():
            wait_high(c)

        @pl.when(me == 0)
        def _():
            send_suf(c).wait_recv()

        @pl.when(me < last - 1)
        def _():
            send_low(c).wait_recv()

        @pl.when(me == last - 1)
        def _():
            send_low_last(c).wait_recv()

        query_two = two_heads(own_qg[c, 0], scale)
        grad_two = two_heads(own_qg[c, 1], 1.0)
        keys = kv[c, 0]
        values = kv[c, 1]
        scores = dot_nt(keys, query_two) + bias[...]
        largest = jnp.max(scores, axis=0, keepdims=True)
        expo = jnp.exp(scores - largest)
        total = jnp.sum(expo, axis=0, keepdims=True)
        dprob = dot_nt(values, grad_two)
        inverse = 1.0 / total
        delta = jnp.sum(expo * dprob, axis=0, keepdims=True) * inverse
        probs = expo * (inverse * row_live)
        probs_low = probs.astype(bf16)
        dscore = (probs * (dprob - delta)).astype(bf16)
        att_ref[:, columns_of(c)] = one_pair(dot_tn(probs_low, values)).astype(bf16)
        qgrad_ref[:, columns_of(c)] = (one_pair(dot_tn(dscore, keys)) * scale).astype(bf16)
        key_all = dot_nn(dscore, query_two)
        value_all = dot_nn(probs_low, grad_two)

        @pl.when(me == 1)
        def _():
            down_out[c, 0] = (key_all[low] + fin_grad[c, 0, low]).astype(bf16)
            down_out[c, 1] = (value_all[low] + fin_grad[c, 1, low]).astype(bf16)

        @pl.when(me != 1)
        def _():
            down_out[c, 0] = key_all[low].astype(bf16)
            down_out[c, 1] = value_all[low].astype(bf16)

        @pl.when(me == 0)
        def _():
            add_out[c, 0] = key_all[suf].astype(bf16)
            add_out[c, 1] = value_all[suf].astype(bf16)
            send_add(c).start()

        up_out[c, 0] = key_all[high].astype(bf16)
        up_out[c, 1] = value_all[high].astype(bf16)
        band_grad[c, 0] = key_all[own]
        band_grad[c, 1] = value_all[own]
        suf_grad[c, 0] = key_all[suf]
        suf_grad[c, 1] = value_all[suf]

        @pl.when(has_below & ((me > 1) | (c >= early)))
        def _():
            send_down(c).start()

    def combine(c):
        @pl.when(has_below)
        def _():
            band_grad[c] = band_grad[c] + fin_grad[c, :, own]

            @pl.when(me < last)
            def _():
                pairs_from(c, up_in, None, up_recv)
                band_grad[c, :, 0:W] = band_grad[c, :, 0:W] + up_in[c].astype(f32)

            @pl.when(is_last)
            def _():
                pairs_from(c, up_in, slice(0, near), up_recv)
                band_grad[c, :, 0:near] = band_grad[c, :, 0:near] + up_in[c, :, 0:near].astype(f32)
                send_add(c).wait_recv()
                band_grad[c, :, tail] = (
                    band_grad[c, :, tail] + suf_grad[c] + add_in[c].astype(f32)
                )

        @pl.when(has_above)
        def _():
            pairs_from(c, down_in, None, down_recv)
            band_grad[c, :, rows - W : rows] = band_grad[c, :, rows - W : rows] + down_in[
                c
            ].astype(f32)

        kgrad_ref[:, columns_of(c)] = band_grad[c, 0].astype(bf16)
        vgrad_ref[:, columns_of(c)] = band_grad[c, 1].astype(bf16)

    def within_chunks(t):
        return (t >= 0) & (t < chunks)

    def by_role(bottom, first, between, top):
        return jnp.where(
            me == 0, bottom, jnp.where(me == 1, first, jnp.where(is_last, top, between))
        )

    never = 0 * me - 1

    def step(t, carry):
        @pl.when((t < chunks) & has_below)
        def _():
            suffix_pass(t)

        @pl.when(within_chunks(t - 1) & (me > 1) & has_above)
        def _():
            pass_down(t - 1)

        @pl.when(within_chunks(t - 1) & (me == 1))
        def _():
            finish_first(t - 1)

        a = by_role(never, t - chunks - FIRST_ADD, t - chunks - BETWEEN_ADD, never)

        @pl.when(within_chunks(a))
        def _():
            send_add(a).wait_recv()
            add_out[a] = (suf_grad[a] + add_in[a].astype(f32)).astype(bf16)
            send_add(a).start()

        first_band = jnp.where(
            t <= early, t - 1, jnp.where(t <= chunks, never, t - chunks - 1 + early)
        )
        b = by_role(t, first_band, t - chunks, t - chunks)

        @pl.when(within_chunks(b))
        def _():
            band(b)

        f = jnp.where(is_last, t - 2 * chunks, t - chunks + 1)

        @pl.when(within_chunks(f) & (me > 1))
        def _():
            finish(f)

        first_up = jnp.where(t <= early, t - 1, never)
        for c in range(early, chunks):
            turn = chunks + UP_TURN + c + (UP_HOLD if c >= early + UP_FREE else 0)
            first_up = jnp.where(t == turn, c, first_up)
        u = by_role(t - 1 - BOTTOM_HOLD, first_up, t - chunks - 1, never)

        @pl.when(within_chunks(u))
        def _():
            @pl.when(me < last - 1)
            def _():
                send_up(u).start()

            @pl.when(me == last - 1)
            def _():
                send_up_last(u).start()

        k = by_role(
            t - chunks - 1, t - 2 * chunks - FIRST_LAST, t - 2 * chunks - BETWEEN_HOLD, t - 3 * chunks
        )

        @pl.when(within_chunks(k))
        def _():
            combine(k)

        return carry

    steps = by_role(
        2 * chunks + 1 + BOTTOM_HOLD, 3 * chunks + FIRST_LAST, 3 * chunks + BETWEEN_HOLD, 4 * chunks
    )
    lax.fori_loop(0, steps, step, 0)

    def sent(source, sem):
        remote(source, source, sem, qg_recv.at[0], below).wait_send()

    @pl.when(has_below)
    def _():
        sent(kv.at[:, :, suf], suf_send)
        sent(down_out, down_send)

        @pl.when(has_above)
        def _():
            sent(kv.at[:, :, own], low_send)
            sent(to_above, rise_send)
            sent(chain_out, chain_send)

        @pl.when(is_last)
        def _():
            sent(kv.at[:, :, W : W + near], low_send)

        @pl.when(me > 1)
        def _():
            sent(qg, qg_send)
            sent(to_below, fall_send)

    @pl.when(has_above)
    def _():
        sent(kv.at[:, :, own], high_send)
        sent(add_out, add_send)

    @pl.when(me < last - 1)
    def _():
        sent(up_out, up_send)

    @pl.when(me == last - 1)
    def _():
        sent(up_out.at[:, :, :near], up_send)


def spill(*refs):
    sems = refs[8]
    copies = [
        pltpu.make_async_copy(refs[k], refs[4 + k].at[0], sems.at[k]) for k in range(4)
    ]
    for copy in copies:
        copy.start()
    for copy in copies:
        copy.wait()


def per_device(n, query_vectors, key_vectors, value_vectors, out_grad, pad_length):
    rows, features = query_vectors.shape[1:]
    chunks = features // PAIR
    all_keys = rows + 2 * W + G
    vmem = pl.BlockSpec(memory_space=pltpu.VMEM)
    dma = pltpu.SemaphoreType.DMA
    hbm = pl.BlockSpec(memory_space=pltpu.HBM)
    outs = pl.pallas_call(
        functools.partial(kernel, n, rows, chunks),
        out_shape=(pltpu.VMEM((rows, features), bf16),) * 4,
        in_specs=[hbm] * 5,
        out_specs=(vmem,) * 4,
        scratch_shapes=[
            pltpu.SMEM((1,), jnp.int32),
            pltpu.VMEM((chunks, 2, all_keys, PAIR), bf16),
            pltpu.VMEM((chunks, 2, G, PAIR), bf16),
            pltpu.VMEM((chunks, 2, rows, PAIR), bf16),
            pltpu.VMEM((chunks, 8, 2 * G), f32),
            pltpu.VMEM((all_keys, 2 * rows), f32),
            pltpu.VMEM((W + rows, 2 * G), f32),
            pltpu.VMEM((chunks, W + rows, 2 * G), f32),
            pltpu.VMEM((chunks, W + rows, 2 * G), f32),
            pltpu.VMEM((chunks, 2, rows, PAIR), f32),
            pltpu.VMEM((chunks, 2, W + rows, PAIR), f32),
            pltpu.VMEM((chunks, 2, G, PAIR), f32),
        ]
        + [pltpu.VMEM((chunks, 2, W, PAIR), bf16)] * 4
        + [pltpu.VMEM((chunks, 2, G, PAIR), bf16)] * 4
        + [pltpu.VMEM((chunks, 2, 2 * G), f32)] * 4
        + [pltpu.SemaphoreType.REGULAR, dma, dma((2,))]
            + [dma] * 10
        + [dma((chunks,))] * 7
        + [dma((chunks // 4,))]
        + [dma((chunks // 2 + 1,))] * 2,
        compiler_params=pltpu.CompilerParams(
            collective_id=0, has_side_effects=True, vmem_limit_bytes=48 << 20
        ),
    )(pad_length, *(pltpu.with_memory_space_constraint(x, pltpu.HBM) for x in (query_vectors, key_vectors, value_vectors, out_grad)))
    anywhere = pl.BlockSpec(memory_space=pl.ANY)
    return pl.pallas_call(
        spill,
        out_shape=(jax.ShapeDtypeStruct((1, rows, features), bf16),) * 4,
        in_specs=[vmem] * 4,
        out_specs=(anywhere,) * 4,
        scratch_shapes=[dma((4,))],
    )(*(pltpu.with_memory_space_constraint(x, pltpu.VMEM) for x in outs))


def solution(mesh):
    rows = P(("group", "doc"), "seq", None)
    return jax.shard_map(
        functools.partial(per_device, mesh.shape["seq"]),
        mesh=mesh,
        in_specs=(rows, rows, rows, rows, P(("group", "doc"))),
        out_specs=(rows,) * 4,
        check_vma=False,
    )
```

```python
import functools
import math

import jax
import jax.numpy as jnp
from jax import lax
from jax.experimental import pallas as pl
from jax.experimental.pallas import tpu as pltpu
from jax.sharding import PartitionSpec as P

D = 1024
H = 16
W = 128
G = 64
HEAD = D // H
PAIR = 2 * HEAD
AHEAD = 2
HOP_AHEAD = 3
FAR_AHEAD = 2
BOTTOM_HOLD = 6
BETWEEN_HOLD = 8
EARLY = 3
HIGH_GROUP = 4
UP_HOLD = 1
UP_TURN = 2
UP_FREE = 2
FIRST_ADD = 0
BETWEEN_ADD = 6
FIRST_LAST = 3

MESH = pl.DeviceIdType.MESH
very_negative = -1e30
scale = 1.0 / math.sqrt(HEAD)
f32 = jnp.float32
bf16 = jnp.bfloat16


def dot_nt(a, b):
    return lax.dot_general(a, b, (((1,), (1,)), ((), ())), preferred_element_type=f32)


def dot_nn(a, b):
    return lax.dot_general(a, b, (((1,), (0,)), ((), ())), preferred_element_type=f32)


def dot_tn(a, b):
    return lax.dot_general(a, b, (((0,), (0,)), ((), ())), preferred_element_type=f32)


def iota(shape, dim):
    return lax.broadcasted_iota(jnp.int32, shape, dim)


def pair_mask(value):
    lane = iota((1, PAIR), 1)
    first = jnp.where(lane < HEAD, value, 0.0).astype(bf16)
    second = jnp.where(lane < HEAD, 0.0, value).astype(bf16)
    return first, second


def two_heads(rows, value):
    first, second = pair_mask(value)
    return jnp.concatenate([rows * first, rows * second], axis=0)


def one_pair(stacked):
    half = stacked.shape[0] // 2
    lane = iota((half, PAIR), 1)
    return jnp.where(lane < HEAD, stacked[:half], stacked[half:])


def merge(one, two):
    top = jnp.maximum(one[0], two[0])
    share_one = jnp.exp(one[0] - top)
    share_two = jnp.exp(two[0] - top)
    total = share_one + share_two
    mean = (share_one * one[1] + share_two * two[1]) / total
    return top + jnp.log(total), mean


def kernel(
    n, rows, chunks,
    pad_ref, q_ref, k_ref, v_ref, g_ref,
    att_ref, qgrad_ref, kgrad_ref, vgrad_ref,
    pad, kv, sfx, own_qg, stats, bias, key_bias, expo_s, dprob_s,
    band_grad, fin_grad, suf_grad, down_out, down_in, up_out, up_in,
    chain_out, chain_in, add_out, add_in, from_above, to_below, from_below, to_above,
    reply, pad_sem, load_sem,
    suf_send, low_send, high_send, down_send, up_send, chain_send, add_send,
    fall_send, rise_send,
    suf_recv, fall_recv, low_recv, chain_recv, add_recv, rise_recv,
    high_recv, down_recv, up_recv,
):
    me = lax.axis_index("seq")
    last = n - 1
    below = lax.rem(me + n - 1, n)
    above = lax.rem(me + 1, n)
    has_below = me > 0
    has_above = me < last
    is_last = me == last
    middle = has_below & has_above
    all_keys = rows + 2 * W + G
    own = slice(W, W + rows)
    low = slice(0, W)
    high = slice(W + rows, 2 * W + rows)
    suf = slice(2 * W + rows, all_keys)
    tail = slice(rows - G, rows)
    near = min(W, rows - G)

    def columns_of(c):
        if isinstance(c, int):
            return pl.ds(c * PAIR, PAIR)
        return pl.ds(pl.multiple_of(c * PAIR, PAIR), PAIR)

    def remote(src, dst, send, recv, target):
        return pltpu.make_async_remote_copy(
            src_ref=src, dst_ref=dst, send_sem=send, recv_sem=recv,
            device_id={"seq": target}, device_id_type=MESH,
        )

    def start_pair(sources, source_rows, target_of, send, recv, target, c):
        for k, source in enumerate(sources):
            remote(
                source.at[0, source_rows, columns_of(c)], target_of(k), send, recv, target
            ).start()

    def send_suf(c):
        return remote(sfx.at[c], sfx.at[c], suf_send, suf_recv.at[c], below)

    def send_suf_bottom(c):
        keys = sfx.at[c, 2:4]
        return remote(keys, keys, suf_send, suf_recv.at[c], below)

    def send_low(c):
        return remote(kv.at[c, :, own], kv.at[c, :, high], low_send, low_recv.at[c], below)

    def send_low_last(c):
        return remote(
            kv.at[c, :, W : W + near],
            kv.at[c, :, W + rows : W + rows + near],
            low_send, low_recv.at[c], below,
        )

    def send_high(c):
        some = pl.ds(c, HIGH_GROUP)
        return remote(
            kv.at[some, :, own], kv.at[some, :, low],
            high_send, high_recv.at[c // HIGH_GROUP], above,
        )

    def early_suf_last(c):
        start_pair(
            (q_ref, g_ref, k_ref, v_ref), tail, lambda k: sfx.at[c, k],
            suf_send, suf_recv.at[c], below, c,
        )

    def early_low(c):
        start_pair(
            (k_ref, v_ref), slice(0, rows), lambda k: kv.at[c, k, high],
            low_send, low_recv.at[c], below, c,
        )

    def send_down(c):
        return remote(down_out.at[c], down_in.at[c], down_send, down_recv.at[(c + 1) // 2], below)

    def send_up(c):
        return remote(up_out.at[c], up_in.at[c], up_send, up_recv.at[(c + 1) // 2], above)

    def send_up_last(c):
        return remote(
            up_out.at[c, :, :near], up_in.at[c, :, :near], up_send, up_recv.at[(c + 1) // 2], above
        )

    def send_chain(c):
        return remote(chain_out.at[c], chain_in.at[c], chain_send, chain_recv.at[c], above)

    def send_add(c):
        return remote(add_out.at[c], add_in.at[c], add_send, add_recv.at[c], above)

    def send_fall(c):
        return remote(to_below.at[c], from_above.at[c], fall_send, fall_recv.at[c], below)

    def send_rise(c):
        return remote(to_above.at[c], from_below.at[c], rise_send, rise_recv.at[c], above)

    def pairs_from(c, ref, part, sem):
        single = (c == 0) | ((c == chunks - 1) & (c % 2 == 1))

        @pl.when(single)
        def _():
            part_ref = ref.at[pl.ds(c, 1)] if part is None else ref.at[pl.ds(c, 1), :, part]
            pltpu.make_async_copy(part_ref, part_ref, sem.at[(c + 1) // 2]).wait()

        @pl.when((c % 2 == 1) & (c < chunks - 1))
        def _():
            part_ref = ref.at[pl.ds(c, 2)] if part is None else ref.at[pl.ds(c, 2), :, part]
            pltpu.make_async_copy(part_ref, part_ref, sem.at[(c + 1) // 2]).wait()

    def wait_high(c):
        @pl.when(c % HIGH_GROUP == 0)
        def _():
            send_high(c).wait_recv()

    early = min(EARLY, chunks)
    lead = HOP_AHEAD + FAR_AHEAD * (last - 1 - me)
    barrier = pltpu.get_barrier_semaphore()

    def tell(sem, target):
        pl.semaphore_signal(sem, inc=1, device_id={"seq": target}, device_id_type=MESH)

    pad_copy = pltpu.make_async_copy(pad_ref, pad, pad_sem)
    if n == 4:
        @pl.when(middle)
        def _():
            tell(barrier, below)
            tell(barrier, above)
    else:
        @pl.when(has_above)
        def _():
            tell(barrier, above)

    pad_copy.start()
    for c in range(chunks):
        pieces = (
            (k_ref, kv.at[c, 0, own]),
            (v_ref, kv.at[c, 1, own]),
            (q_ref, own_qg.at[c, 0]),
            (g_ref, own_qg.at[c, 1]),
        )
        for k, (source, target) in enumerate(pieces):
            pltpu.make_async_copy(
                source.at[0, :, columns_of(c)], target, load_sem.at[k // 2]
            ).start()

    if n == 4:
        pl.semaphore_wait(barrier, 1)

        @pl.when(me == 0)
        def _():
            tell(reply, above)

        @pl.when(is_last)
        def _():
            tell(reply, below)
    else:
        @pl.when(has_below)
        def _():
            pl.semaphore_wait(barrier, 1)
            tell(reply, below)

    @pl.when(is_last)
    def _():
        for c in range(AHEAD):
            early_suf_last(c)

    for c in range(chunks):
        @pl.when(middle & (me > 1) & (c < lead))
        def _():
            early_low(c)

    loaded = (kv.at[:, :, own], own_qg)
    for k, target in enumerate(loaded):
        pltpu.make_async_copy(target, target, load_sem.at[k]).wait()

    def start_high():
        for c in range(0, chunks, HIGH_GROUP):
            send_high(c).start()

    def start_low_first():
        for c in range(chunks):
            @pl.when(c < lead)
            def _():
                send_low(c).start()

    if n == 4:
        @pl.when(me == 0)
        def _():
            start_high()

        @pl.when(me == 1)
        def _():
            start_high()
            pl.semaphore_wait(reply, 1)
            start_low_first()

        @pl.when(me == 2)
        def _():
            pl.semaphore_wait(reply, 1)
            start_high()
    else:
        @pl.when(me == 1)
        def _():
            start_low_first()

        @pl.when(has_above)
        def _():
            pl.semaphore_wait(reply, 1)
            start_high()

    @pl.when(is_last)
    def _():
        for c in range(chunks):
            kv[c, :, high] = jnp.zeros((2, W, PAIR), bf16)

    @pl.when(me == last - 1)
    def _():
        for c in range(chunks):
            kv[c, :, W + rows + near : 2 * W + rows] = jnp.zeros((2, W - near, PAIR), bf16)

    @pl.when(me == 0)
    def _():
        for c in range(chunks):
            kv[c, :, low] = jnp.zeros((2, W, PAIR), bf16)

    pad_copy.wait()
    suffix_start = rows * n - G
    valid_end = suffix_start - pad[0]
    first_row = me * rows
    j = iota((all_keys, 2 * rows), 0)
    i = iota((all_keys, 2 * rows), 1)
    i = jnp.where(i >= rows, i - rows, i)
    key_pos = first_row - W + j
    apart = i - (j - W)
    within = (apart <= W) & (apart >= -W) & (key_pos >= 0) & (key_pos < valid_end)
    bias[...] = jnp.where(within | (j >= 2 * W + rows), 0.0, very_negative)
    near_pos = first_row - W + iota((W + rows, 2 * G), 0)
    key_bias[...] = jnp.where(
        (near_pos < valid_end) | (near_pos >= suffix_start), 0.0, very_negative
    )
    query_lane = iota((1, 2 * rows), 1)
    query_pos = first_row + jnp.where(query_lane >= rows, query_lane - rows, query_lane)
    row_live = jnp.where(query_pos < suffix_start, 1.0, 0.0)

    @pl.when(is_last)
    def _():
        for c in range(chunks):
            sfx[c, 0:2] = own_qg[c, :, tail]
            sfx[c, 2:4] = kv[c, :, W + rows - G : W + rows]

    def suffix_stats(c, keys):
        query_two = two_heads(sfx[c, 0], scale)
        grad_two = two_heads(sfx[c, 1], 1.0)
        scores = dot_nt(kv[c, 0, keys], query_two) + key_bias[keys]
        largest = jnp.max(scores, axis=0, keepdims=True)
        expo = jnp.exp(scores - largest)
        dprob = dot_nt(kv[c, 1, keys], grad_two)
        total = jnp.sum(expo, axis=0, keepdims=True)
        weighted = jnp.sum(expo * dprob, axis=0, keepdims=True)
        expo_s[c, keys] = expo
        dprob_s[c, keys] = dprob
        stats[c, 0:1] = largest
        stats[c, 1:2] = largest + jnp.log(total)
        stats[c, 2:3] = weighted / total

    def pair_of(ref, c, at):
        return ref[c, at : at + 1], ref[c, at + 1 : at + 2]

    def put(ref, c, values):
        ref[c, 0:1] = values[0]
        ref[c, 1:2] = values[1]

    def suffix_parts(c, keys, whole):
        top, delta = whole
        probs = expo_s[c, keys] * jnp.exp(stats[c, 0:1] - top)
        probs_low = probs.astype(bf16)
        dscore = (probs * (dprob_s[c, keys] - delta)).astype(bf16)
        query_two = two_heads(sfx[c, 0], scale)
        grad_two = two_heads(sfx[c, 1], 1.0)
        att_part = one_pair(dot_tn(probs_low, kv[c, 1, keys]))
        query_part = one_pair(dot_tn(dscore, kv[c, 0, keys])) * scale
        fin_grad[c, 0, keys] = dot_nn(dscore, query_two)
        fin_grad[c, 1, keys] = dot_nn(probs_low, grad_two)
        return att_part, query_part

    both = slice(0, W + rows)

    def suffix_pass(c):
        @pl.when(middle)
        def _():
            send_suf(c).wait_recv()

            @pl.when(me > 1)
            def _():
                send_suf(c).start()

            @pl.when(me == 1)
            def _():
                send_suf_bottom(c).start()

        @pl.when((me == 1) & (c % 2 == 1) & (lead + c // 2 < chunks))
        def _():
            send_low(lead + c // 2).start()

        @pl.when(me > 1)
        def _():
            suffix_stats(c, own)

        @pl.when(me == 1)
        def _():
            wait_high(c)
            suffix_stats(c, both)
            put(to_above, c, pair_of(stats, c, 1))
            send_rise(c).start()

        @pl.when(is_last)
        def _():
            put(to_below, c, pair_of(stats, c, 1))
            send_fall(c).start()

            @pl.when(c + AHEAD < chunks)
            def _():
                send_suf(c + AHEAD).start()

        @pl.when((c == chunks - 1) & is_last)
        def _():
            for k in range(chunks):
                send_low_last(k).start()

    def pass_down(c):
        send_fall(c).wait_recv()
        put(to_below, c, merge(pair_of(stats, c, 1), pair_of(from_above, c, 0)))
        send_fall(c).start()

        @pl.when(c == chunks - 1)
        def _():
            for k in range(chunks):
                @pl.when(k >= lead)
                def _():
                    send_low(k).start()

    def finish_first(c):
        send_fall(c).wait_recv()
        whole = merge(pair_of(stats, c, 1), pair_of(from_above, c, 0))
        att_part, query_part = suffix_parts(c, both, whole)
        chain_out[c, 0] = att_part.astype(bf16)
        chain_out[c, 1] = query_part.astype(bf16)
        send_chain(c).start()

        @pl.when(c == chunks - 1)
        def _():
            for k in range(early):
                send_down(k).start()

    def finish(c):
        send_rise(c).wait_recv()
        to_here = merge(pair_of(stats, c, 1), pair_of(from_below, c, 0))

        def parts(whole):
            att_part, query_part = suffix_parts(c, own, whole)
            send_chain(c).wait_recv()
            att_sum = att_part + chain_in[c, 0].astype(f32)
            query_sum = query_part + chain_in[c, 1].astype(f32)
            return att_sum.astype(bf16), query_sum.astype(bf16)

        @pl.when(has_above)
        def _():
            put(to_above, c, to_here)
            send_rise(c).start()
            att_sum, query_sum = parts(merge(to_here, pair_of(from_above, c, 0)))
            chain_out[c, 0] = att_sum
            chain_out[c, 1] = query_sum
            send_chain(c).start()

        @pl.when(is_last)
        def _():
            att_sum, query_sum = parts(to_here)
            att_ref[tail, columns_of(c)] = att_sum
            qgrad_ref[tail, columns_of(c)] = query_sum

    def band(c):
        @pl.when(me > 1)
        def _():
            wait_high(c)

        @pl.when(me == 0)
        def _():
            send_suf_bottom(c).wait_recv()

        @pl.when(me < last - 1)
        def _():
            send_low(c).wait_recv()

        @pl.when(me == last - 1)
        def _():
            send_low_last(c).wait_recv()

        kv[c, :, suf] = sfx[c, 2:4]
        query_two = two_heads(own_qg[c, 0], scale)
        grad_two = two_heads(own_qg[c, 1], 1.0)
        keys = kv[c, 0]
        values = kv[c, 1]
        scores = dot_nt(keys, query_two) + bias[...]
        largest = jnp.max(scores, axis=0, keepdims=True)
        expo = jnp.exp(scores - largest)
        total = jnp.sum(expo, axis=0, keepdims=True)
        dprob = dot_nt(values, grad_two)
        inverse = 1.0 / total
        delta = jnp.sum(expo * dprob, axis=0, keepdims=True) * inverse
        probs = expo * (inverse * row_live)
        probs_low = probs.astype(bf16)
        dscore = (probs * (dprob - delta)).astype(bf16)
        att_ref[:, columns_of(c)] = one_pair(dot_tn(probs_low, values)).astype(bf16)
        qgrad_ref[:, columns_of(c)] = (one_pair(dot_tn(dscore, keys)) * scale).astype(bf16)
        key_all = dot_nn(dscore, query_two)
        value_all = dot_nn(probs_low, grad_two)

        @pl.when(me == 1)
        def _():
            down_out[c, 0] = (key_all[low] + fin_grad[c, 0, low]).astype(bf16)
            down_out[c, 1] = (value_all[low] + fin_grad[c, 1, low]).astype(bf16)

        @pl.when(me != 1)
        def _():
            down_out[c, 0] = key_all[low].astype(bf16)
            down_out[c, 1] = value_all[low].astype(bf16)

        @pl.when(me == 0)
        def _():
            add_out[c, 0] = key_all[suf].astype(bf16)
            add_out[c, 1] = value_all[suf].astype(bf16)
            send_add(c).start()

        up_out[c, 0] = key_all[high].astype(bf16)
        up_out[c, 1] = value_all[high].astype(bf16)
        band_grad[c, 0] = key_all[own]
        band_grad[c, 1] = value_all[own]
        suf_grad[c, 0] = key_all[suf]
        suf_grad[c, 1] = value_all[suf]

        @pl.when(has_below & ((me > 1) | (c >= early)))
        def _():
            send_down(c).start()

    def combine(c):
        @pl.when(has_below)
        def _():
            band_grad[c] = band_grad[c] + fin_grad[c, :, own]

            @pl.when(me < last)
            def _():
                pairs_from(c, up_in, None, up_recv)
                band_grad[c, :, 0:W] = band_grad[c, :, 0:W] + up_in[c].astype(f32)

            @pl.when(is_last)
            def _():
                pairs_from(c, up_in, slice(0, near), up_recv)
                band_grad[c, :, 0:near] = band_grad[c, :, 0:near] + up_in[c, :, 0:near].astype(f32)
                send_add(c).wait_recv()
                band_grad[c, :, tail] = (
                    band_grad[c, :, tail] + suf_grad[c] + add_in[c].astype(f32)
                )

        @pl.when(has_above)
        def _():
            pairs_from(c, down_in, None, down_recv)
            band_grad[c, :, rows - W : rows] = band_grad[c, :, rows - W : rows] + down_in[
                c
            ].astype(f32)

        kgrad_ref[:, columns_of(c)] = band_grad[c, 0].astype(bf16)
        vgrad_ref[:, columns_of(c)] = band_grad[c, 1].astype(bf16)

    def within_chunks(t):
        return (t >= 0) & (t < chunks)

    def by_role(bottom, first, between, top):
        return jnp.where(
            me == 0, bottom, jnp.where(me == 1, first, jnp.where(is_last, top, between))
        )

    never = 0 * me - 1

    def step(t, carry):
        @pl.when((t < chunks) & has_below)
        def _():
            suffix_pass(t)

        @pl.when(within_chunks(t - 1) & (me > 1) & has_above)
        def _():
            pass_down(t - 1)

        @pl.when(within_chunks(t - 1) & (me == 1))
        def _():
            finish_first(t - 1)

        a = by_role(never, t - chunks - FIRST_ADD, t - chunks - BETWEEN_ADD, never)

        @pl.when(within_chunks(a))
        def _():
            send_add(a).wait_recv()
            add_out[a] = (suf_grad[a] + add_in[a].astype(f32)).astype(bf16)
            send_add(a).start()

        first_band = jnp.where(
            t <= early, t - 1, jnp.where(t <= chunks, never, t - chunks - 1 + early)
        )
        b = by_role(t, first_band, t - chunks, t - chunks)

        @pl.when(within_chunks(b))
        def _():
            band(b)

        f = jnp.where(is_last, t - 2 * chunks, t - chunks + 1)

        @pl.when(within_chunks(f) & (me > 1))
        def _():
            finish(f)

        first_up = jnp.where(t <= early, t - 1, never)
        for c in range(early, chunks):
            turn = chunks + UP_TURN + c + (UP_HOLD if c >= early + UP_FREE else 0)
            first_up = jnp.where(t == turn, c, first_up)
        u = by_role(t - 1 - BOTTOM_HOLD, first_up, t - chunks - 1, never)

        @pl.when(within_chunks(u))
        def _():
            @pl.when(me < last - 1)
            def _():
                send_up(u).start()

            @pl.when(me == last - 1)
            def _():
                send_up_last(u).start()

        k = by_role(
            t - chunks - 1, t - 2 * chunks - FIRST_LAST, t - 2 * chunks - BETWEEN_HOLD, t - 3 * chunks
        )

        @pl.when(within_chunks(k))
        def _():
            combine(k)

        return carry

    steps = by_role(
        2 * chunks + 1 + BOTTOM_HOLD, 3 * chunks + FIRST_LAST, 3 * chunks + BETWEEN_HOLD, 4 * chunks
    )
    lax.fori_loop(0, steps, step, 0)

    def sent(source, sem):
        remote(source, source, sem, suf_recv.at[0], below).wait_send()

    @pl.when(has_below)
    def _():
        sent(down_out, down_send)

        @pl.when(me == 1)
        def _():
            sent(sfx.at[:, 2:4], suf_send)

        @pl.when(has_above)
        def _():
            sent(kv.at[:, :, own], low_send)
            sent(to_above, rise_send)
            sent(chain_out, chain_send)

        @pl.when(is_last)
        def _():
            sent(kv.at[:, :, W : W + near], low_send)

        @pl.when(me > 1)
        def _():
            sent(sfx, suf_send)
            sent(to_below, fall_send)

    @pl.when(has_above)
    def _():
        sent(kv.at[:, :, own], high_send)
        sent(add_out, add_send)

    @pl.when(me < last - 1)
    def _():
        sent(up_out, up_send)

    @pl.when(me == last - 1)
    def _():
        sent(up_out.at[:, :, :near], up_send)


def spill(*refs):
    sems = refs[8]
    copies = [
        pltpu.make_async_copy(refs[k], refs[4 + k].at[0], sems.at[k]) for k in range(4)
    ]
    for copy in copies:
        copy.start()
    for copy in copies:
        copy.wait()


def per_device(n, query_vectors, key_vectors, value_vectors, out_grad, pad_length):
    rows, features = query_vectors.shape[1:]
    chunks = features // PAIR
    all_keys = rows + 2 * W + G
    vmem = pl.BlockSpec(memory_space=pltpu.VMEM)
    dma = pltpu.SemaphoreType.DMA
    hbm = pl.BlockSpec(memory_space=pltpu.HBM)
    outs = pl.pallas_call(
        functools.partial(kernel, n, rows, chunks),
        out_shape=(pltpu.VMEM((rows, features), bf16),) * 4,
        in_specs=[hbm] * 5,
        out_specs=(vmem,) * 4,
        scratch_shapes=[
            pltpu.SMEM((1,), jnp.int32),
            pltpu.VMEM((chunks, 2, all_keys, PAIR), bf16),
            pltpu.VMEM((chunks, 4, G, PAIR), bf16),
            pltpu.VMEM((chunks, 2, rows, PAIR), bf16),
            pltpu.VMEM((chunks, 8, 2 * G), f32),
            pltpu.VMEM((all_keys, 2 * rows), f32),
            pltpu.VMEM((W + rows, 2 * G), f32),
            pltpu.VMEM((chunks, W + rows, 2 * G), f32),
            pltpu.VMEM((chunks, W + rows, 2 * G), f32),
            pltpu.VMEM((chunks, 2, rows, PAIR), f32),
            pltpu.VMEM((chunks, 2, W + rows, PAIR), f32),
            pltpu.VMEM((chunks, 2, G, PAIR), f32),
        ]
        + [pltpu.VMEM((chunks, 2, W, PAIR), bf16)] * 4
        + [pltpu.VMEM((chunks, 2, G, PAIR), bf16)] * 4
        + [pltpu.VMEM((chunks, 2, 2 * G), f32)] * 4
        + [pltpu.SemaphoreType.REGULAR, dma, dma((2,))]
            + [dma] * 9
        + [dma((chunks,))] * 6
        + [dma((chunks // HIGH_GROUP,))]
        + [dma((chunks // 2 + 1,))] * 2,
        compiler_params=pltpu.CompilerParams(
            collective_id=0, has_side_effects=True, vmem_limit_bytes=48 << 20
        ),
    )(pad_length, *(pltpu.with_memory_space_constraint(x, pltpu.HBM) for x in (query_vectors, key_vectors, value_vectors, out_grad)))
    anywhere = pl.BlockSpec(memory_space=pl.ANY)
    return pl.pallas_call(
        spill,
        out_shape=(jax.ShapeDtypeStruct((1, rows, features), bf16),) * 4,
        in_specs=[vmem] * 4,
        out_specs=(anywhere,) * 4,
        scratch_shapes=[dma((4,))],
    )(*(pltpu.with_memory_space_constraint(x, pltpu.VMEM) for x in outs))


def solution(mesh):
    rows = P(("group", "doc"), "seq", None)
    return jax.shard_map(
        functools.partial(per_device, mesh.shape["seq"]),
        mesh=mesh,
        in_specs=(rows, rows, rows, rows, P(("group", "doc"))),
        out_specs=(rows,) * 4,
        check_vma=False,
    )
```

```python
import functools
import math

import jax
import jax.numpy as jnp
from jax import lax
from jax.experimental import pallas as pl
from jax.experimental.pallas import tpu as pltpu
from jax.sharding import PartitionSpec as P

D = 1024
H = 16
W = 128
G = 64
HEAD = D // H
PAIR = 2 * HEAD
AHEAD = 2
HOP_AHEAD = 3
FAR_AHEAD = 2
BOTTOM_HOLD = 6
BETWEEN_HOLD = 8
EARLY = 3
HIGH_GROUP = 4
UP_HOLD = 1
UP_TURN = 2
UP_FREE = 2
FIRST_ADD = 0
BETWEEN_ADD = 6
FIRST_LAST = 3

MESH = pl.DeviceIdType.MESH
very_negative = -1e30
scale = 1.0 / math.sqrt(HEAD)
f32 = jnp.float32
bf16 = jnp.bfloat16


def dot_nt(a, b):
    return lax.dot_general(a, b, (((1,), (1,)), ((), ())), preferred_element_type=f32)


def dot_nn(a, b):
    return lax.dot_general(a, b, (((1,), (0,)), ((), ())), preferred_element_type=f32)


def dot_tn(a, b):
    return lax.dot_general(a, b, (((0,), (0,)), ((), ())), preferred_element_type=f32)


def iota(shape, dim):
    return lax.broadcasted_iota(jnp.int32, shape, dim)


def pair_mask(value):
    lane = iota((1, PAIR), 1)
    first = jnp.where(lane < HEAD, value, 0.0).astype(bf16)
    second = jnp.where(lane < HEAD, 0.0, value).astype(bf16)
    return first, second


def two_heads(rows, value):
    first, second = pair_mask(value)
    return jnp.concatenate([rows * first, rows * second], axis=0)


def one_pair(stacked):
    half = stacked.shape[0] // 2
    lane = iota((half, PAIR), 1)
    return jnp.where(lane < HEAD, stacked[:half], stacked[half:])


def merge(one, two):
    top = jnp.maximum(one[0], two[0])
    share_one = jnp.exp(one[0] - top)
    share_two = jnp.exp(two[0] - top)
    total = share_one + share_two
    mean = (share_one * one[1] + share_two * two[1]) / total
    return top + jnp.log(total), mean


def kernel(
    n, rows, chunks,
    pad_ref, q_ref, k_ref, v_ref, g_ref,
    att_ref, qgrad_ref, kgrad_ref, vgrad_ref,
    pad, kv, sfx, own_qg, stats, bias, key_bias, expo_s, dprob_s,
    band_grad, fin_grad, suf_grad, down_out, down_in, up_out, up_in,
    chain_out, chain_in, add_out, add_in, from_above, to_below, from_below, to_above,
    reply, pad_sem, load_sem,
    suf_send, low_send, high_send, down_send, up_send, chain_send, add_send,
    fall_send, rise_send,
    suf_recv, fall_recv, low_recv, chain_recv, add_recv, rise_recv,
    high_recv, down_recv, up_recv,
):
    me = lax.axis_index("seq")
    last = n - 1
    below = lax.rem(me + n - 1, n)
    above = lax.rem(me + 1, n)
    has_below = me > 0
    has_above = me < last
    is_last = me == last
    middle = has_below & has_above
    all_keys = rows + 2 * W + G
    own = slice(W, W + rows)
    low = slice(0, W)
    high = slice(W + rows, 2 * W + rows)
    suf = slice(2 * W + rows, all_keys)
    tail = slice(rows - G, rows)
    near = min(W, rows - G)

    def columns_of(c):
        if isinstance(c, int):
            return pl.ds(c * PAIR, PAIR)
        return pl.ds(pl.multiple_of(c * PAIR, PAIR), PAIR)

    def remote(src, dst, send, recv, target):
        return pltpu.make_async_remote_copy(
            src_ref=src, dst_ref=dst, send_sem=send, recv_sem=recv,
            device_id={"seq": target}, device_id_type=MESH,
        )

    def start_pair(sources, source_rows, target_of, send, recv, target, c):
        for k, source in enumerate(sources):
            remote(
                source.at[0, source_rows, columns_of(c)], target_of(k), send, recv, target
            ).start()

    def send_suf(c):
        return remote(sfx.at[c], sfx.at[c], suf_send, suf_recv.at[c], below)

    def send_suf_bottom(c):
        keys = sfx.at[c, 2:4]
        return remote(keys, keys, suf_send, suf_recv.at[c], below)

    def send_low(c):
        return remote(kv.at[c, :, own], kv.at[c, :, high], low_send, low_recv.at[c], below)

    def send_low_last(c):
        return remote(
            kv.at[c, :, W : W + near],
            kv.at[c, :, W + rows : W + rows + near],
            low_send, low_recv.at[c], below,
        )

    def send_high(c):
        some = pl.ds(c, HIGH_GROUP)
        return remote(
            kv.at[some, :, own], kv.at[some, :, low],
            high_send, high_recv.at[c // HIGH_GROUP], above,
        )

    def early_suf_last(c):
        start_pair(
            (q_ref, g_ref, k_ref, v_ref), tail, lambda k: sfx.at[c, k],
            suf_send, suf_recv.at[c], below, c,
        )

    def early_low(c):
        start_pair(
            (k_ref, v_ref), slice(0, rows), lambda k: kv.at[c, k, high],
            low_send, low_recv.at[c], below, c,
        )

    def send_down(c):
        return remote(down_out.at[c], down_in.at[c], down_send, down_recv.at[(c + 1) // 4], below)

    def send_up(c):
        return remote(up_out.at[c], up_in.at[c], up_send, up_recv.at[(c + 1) // 4], above)

    def send_up_last(c):
        return remote(
            up_out.at[c, :, :near], up_in.at[c, :, :near], up_send, up_recv.at[(c + 1) // 4], above
        )

    def send_chain(c):
        return remote(chain_out.at[c], chain_in.at[c], chain_send, chain_recv.at[c], above)

    def send_add(c):
        return remote(add_out.at[c], add_in.at[c], add_send, add_recv.at[c], above)

    def send_fall(c):
        return remote(to_below.at[c], from_above.at[c], fall_send, fall_recv.at[c], below)

    def send_rise(c):
        return remote(to_above.at[c], from_below.at[c], rise_send, rise_recv.at[c], above)

    def group_from(c, ref, part, sem):
        for group in range(chunks // 4 + 1):
            first = max(4 * group - 1, 0)
            count = min(4 * group + 3, chunks) - first

            @pl.when(c == first)
            def _():
                some = pl.ds(first, count)
                whole = ref.at[some] if part is None else ref.at[some, :, part]
                pltpu.make_async_copy(whole, whole, sem.at[group]).wait()

    def wait_high(c):
        @pl.when(c % HIGH_GROUP == 0)
        def _():
            send_high(c).wait_recv()

    early = min(EARLY, chunks)
    lead = HOP_AHEAD + FAR_AHEAD * (last - 1 - me)
    barrier = pltpu.get_barrier_semaphore()

    def tell(sem, target):
        pl.semaphore_signal(sem, inc=1, device_id={"seq": target}, device_id_type=MESH)

    pad_copy = pltpu.make_async_copy(pad_ref, pad, pad_sem)
    if n == 4:
        @pl.when(middle)
        def _():
            tell(barrier, jnp.where(me == 1, above, below))
            tell(barrier, jnp.where(me == 1, below, above))
    else:
        @pl.when(has_above)
        def _():
            tell(barrier, above)

    pad_copy.start()
    for c in range(chunks):
        pieces = (
            (k_ref, kv.at[c, 0, own]),
            (v_ref, kv.at[c, 1, own]),
            (q_ref, own_qg.at[c, 0]),
            (g_ref, own_qg.at[c, 1]),
        )
        for k, (source, target) in enumerate(pieces):
            pltpu.make_async_copy(
                source.at[0, :, columns_of(c)], target, load_sem.at[k // 2]
            ).start()

    if n == 4:
        pl.semaphore_wait(barrier, 1)

        @pl.when(me == 0)
        def _():
            tell(reply, above)

        @pl.when(is_last)
        def _():
            tell(reply, below)
    else:
        @pl.when(has_below)
        def _():
            pl.semaphore_wait(barrier, 1)
            tell(reply, below)

    @pl.when(is_last)
    def _():
        for c in range(AHEAD):
            early_suf_last(c)

    for c in range(chunks):
        @pl.when(middle & (me > 1) & (c < lead))
        def _():
            early_low(c)

    loaded = (kv.at[:, :, own], own_qg)
    for k, target in enumerate(loaded):
        pltpu.make_async_copy(target, target, load_sem.at[k]).wait()

    def start_high():
        for c in range(0, chunks, HIGH_GROUP):
            send_high(c).start()

    def start_low_first():
        for c in range(chunks):
            @pl.when(c < lead)
            def _():
                send_low(c).start()

    if n == 4:
        @pl.when(me == 0)
        def _():
            start_high()

        @pl.when(me == 1)
        def _():
            start_high()
            pl.semaphore_wait(reply, 1)
            start_low_first()

        @pl.when(me == 2)
        def _():
            pl.semaphore_wait(reply, 1)
            start_high()
    else:
        @pl.when(me == 1)
        def _():
            start_low_first()

        @pl.when(has_above)
        def _():
            pl.semaphore_wait(reply, 1)
            start_high()

    @pl.when(is_last)
    def _():
        for c in range(chunks):
            kv[c, :, high] = jnp.zeros((2, W, PAIR), bf16)

    @pl.when(me == last - 1)
    def _():
        for c in range(chunks):
            kv[c, :, W + rows + near : 2 * W + rows] = jnp.zeros((2, W - near, PAIR), bf16)

    @pl.when(me == 0)
    def _():
        for c in range(chunks):
            kv[c, :, low] = jnp.zeros((2, W, PAIR), bf16)

    pad_copy.wait()
    suffix_start = rows * n - G
    valid_end = suffix_start - pad[0]
    first_row = me * rows
    j = iota((all_keys, 2 * rows), 0)
    i = iota((all_keys, 2 * rows), 1)
    i = jnp.where(i >= rows, i - rows, i)
    key_pos = first_row - W + j
    apart = i - (j - W)
    within = (apart <= W) & (apart >= -W) & (key_pos >= 0) & (key_pos < valid_end)
    bias[...] = jnp.where(within | (j >= 2 * W + rows), 0.0, very_negative)
    near_pos = first_row - W + iota((W + rows, 2 * G), 0)
    key_bias[...] = jnp.where(
        (near_pos < valid_end) | (near_pos >= suffix_start), 0.0, very_negative
    )
    query_lane = iota((1, 2 * rows), 1)
    query_pos = first_row + jnp.where(query_lane >= rows, query_lane - rows, query_lane)
    row_live = jnp.where(query_pos < suffix_start, 1.0, 0.0)

    @pl.when(is_last)
    def _():
        for c in range(chunks):
            sfx[c, 0:2] = own_qg[c, :, tail]
            sfx[c, 2:4] = kv[c, :, W + rows - G : W + rows]

    def suffix_stats(c, keys):
        query_two = two_heads(sfx[c, 0], scale)
        grad_two = two_heads(sfx[c, 1], 1.0)
        scores = dot_nt(kv[c, 0, keys], query_two) + key_bias[keys]
        largest = jnp.max(scores, axis=0, keepdims=True)
        expo = jnp.exp(scores - largest)
        dprob = dot_nt(kv[c, 1, keys], grad_two)
        total = jnp.sum(expo, axis=0, keepdims=True)
        weighted = jnp.sum(expo * dprob, axis=0, keepdims=True)
        expo_s[c, keys] = expo
        dprob_s[c, keys] = dprob
        stats[c, 0:1] = largest
        stats[c, 1:2] = largest + jnp.log(total)
        stats[c, 2:3] = weighted / total

    def pair_of(ref, c, at):
        return ref[c, at : at + 1], ref[c, at + 1 : at + 2]

    def put(ref, c, values):
        ref[c, 0:1] = values[0]
        ref[c, 1:2] = values[1]

    def suffix_parts(c, keys, whole):
        top, delta = whole
        probs = expo_s[c, keys] * jnp.exp(stats[c, 0:1] - top)
        probs_low = probs.astype(bf16)
        dscore = (probs * (dprob_s[c, keys] - delta)).astype(bf16)
        query_two = two_heads(sfx[c, 0], scale)
        grad_two = two_heads(sfx[c, 1], 1.0)
        att_part = one_pair(dot_tn(probs_low, kv[c, 1, keys]))
        query_part = one_pair(dot_tn(dscore, kv[c, 0, keys])) * scale
        fin_grad[c, 0, keys] = dot_nn(dscore, query_two)
        fin_grad[c, 1, keys] = dot_nn(probs_low, grad_two)
        return att_part, query_part

    both = slice(0, W + rows)

    def suffix_pass(c):
        @pl.when(middle)
        def _():
            send_suf(c).wait_recv()

            @pl.when(me > 1)
            def _():
                send_suf(c).start()

            @pl.when(me == 1)
            def _():
                send_suf_bottom(c).start()

        @pl.when((me == 1) & (c % 2 == 1) & (lead + c // 2 < chunks))
        def _():
            send_low(lead + c // 2).start()

        @pl.when(me > 1)
        def _():
            suffix_stats(c, own)

        @pl.when(me == 1)
        def _():
            wait_high(c)
            suffix_stats(c, both)
            put(to_above, c, pair_of(stats, c, 1))
            send_rise(c).start()

        @pl.when(is_last)
        def _():
            put(to_below, c, pair_of(stats, c, 1))
            send_fall(c).start()

            @pl.when(c + AHEAD < chunks)
            def _():
                send_suf(c + AHEAD).start()

        @pl.when((c == chunks - 1) & is_last)
        def _():
            for k in range(chunks):
                send_low_last(k).start()

    def pass_down(c):
        send_fall(c).wait_recv()
        put(to_below, c, merge(pair_of(stats, c, 1), pair_of(from_above, c, 0)))
        send_fall(c).start()

        @pl.when(c == chunks - 1)
        def _():
            for k in range(chunks):
                @pl.when(k >= lead)
                def _():
                    send_low(k).start()

    def finish_first(c):
        send_fall(c).wait_recv()
        whole = merge(pair_of(stats, c, 1), pair_of(from_above, c, 0))
        att_part, query_part = suffix_parts(c, both, whole)
        chain_out[c, 0] = att_part.astype(bf16)
        chain_out[c, 1] = query_part.astype(bf16)
        send_chain(c).start()

        @pl.when(c == chunks - 1)
        def _():
            for k in range(early):
                send_down(k).start()

    def finish(c):
        send_rise(c).wait_recv()
        to_here = merge(pair_of(stats, c, 1), pair_of(from_below, c, 0))

        def parts(whole):
            att_part, query_part = suffix_parts(c, own, whole)
            send_chain(c).wait_recv()
            att_sum = att_part + chain_in[c, 0].astype(f32)
            query_sum = query_part + chain_in[c, 1].astype(f32)
            return att_sum.astype(bf16), query_sum.astype(bf16)

        @pl.when(has_above)
        def _():
            put(to_above, c, to_here)
            send_rise(c).start()
            att_sum, query_sum = parts(merge(to_here, pair_of(from_above, c, 0)))
            chain_out[c, 0] = att_sum
            chain_out[c, 1] = query_sum
            send_chain(c).start()

        @pl.when(is_last)
        def _():
            att_sum, query_sum = parts(to_here)
            att_ref[tail, columns_of(c)] = att_sum
            qgrad_ref[tail, columns_of(c)] = query_sum

    def band(c):
        @pl.when(me > 1)
        def _():
            wait_high(c)

        @pl.when(me == 0)
        def _():
            send_suf_bottom(c).wait_recv()

        @pl.when(me < last - 1)
        def _():
            send_low(c).wait_recv()

        @pl.when(me == last - 1)
        def _():
            send_low_last(c).wait_recv()

        kv[c, :, suf] = sfx[c, 2:4]
        query_two = two_heads(own_qg[c, 0], scale)
        grad_two = two_heads(own_qg[c, 1], 1.0)
        keys = kv[c, 0]
        values = kv[c, 1]
        scores = dot_nt(keys, query_two) + bias[...]
        largest = jnp.max(scores, axis=0, keepdims=True)
        expo = jnp.exp(scores - largest)
        total = jnp.sum(expo, axis=0, keepdims=True)
        dprob = dot_nt(values, grad_two)
        inverse = 1.0 / total
        delta = jnp.sum(expo * dprob, axis=0, keepdims=True) * inverse
        probs = expo * (inverse * row_live)
        probs_low = probs.astype(bf16)
        dscore = (probs * (dprob - delta)).astype(bf16)
        att_ref[:, columns_of(c)] = one_pair(dot_tn(probs_low, values)).astype(bf16)
        qgrad_ref[:, columns_of(c)] = (one_pair(dot_tn(dscore, keys)) * scale).astype(bf16)
        key_all = dot_nn(dscore, query_two)
        value_all = dot_nn(probs_low, grad_two)

        @pl.when(me == 1)
        def _():
            down_out[c, 0] = (key_all[low] + fin_grad[c, 0, low]).astype(bf16)
            down_out[c, 1] = (value_all[low] + fin_grad[c, 1, low]).astype(bf16)

        @pl.when(me != 1)
        def _():
            down_out[c, 0] = key_all[low].astype(bf16)
            down_out[c, 1] = value_all[low].astype(bf16)

        @pl.when(me == 0)
        def _():
            add_out[c, 0] = key_all[suf].astype(bf16)
            add_out[c, 1] = value_all[suf].astype(bf16)
            send_add(c).start()

        up_out[c, 0] = key_all[high].astype(bf16)
        up_out[c, 1] = value_all[high].astype(bf16)
        band_grad[c, 0] = key_all[own]
        band_grad[c, 1] = value_all[own]
        suf_grad[c, 0] = key_all[suf]
        suf_grad[c, 1] = value_all[suf]

        @pl.when(has_below & ((me > 1) | (c >= early)))
        def _():
            send_down(c).start()

    def combine(c):
        @pl.when(has_below)
        def _():
            band_grad[c] = band_grad[c] + fin_grad[c, :, own]

            @pl.when(me < last)
            def _():
                group_from(c, up_in, None, up_recv)
                band_grad[c, :, 0:W] = band_grad[c, :, 0:W] + up_in[c].astype(f32)

            @pl.when(is_last)
            def _():
                group_from(c, up_in, slice(0, near), up_recv)
                band_grad[c, :, 0:near] = band_grad[c, :, 0:near] + up_in[c, :, 0:near].astype(f32)
                send_add(c).wait_recv()
                band_grad[c, :, tail] = (
                    band_grad[c, :, tail] + suf_grad[c] + add_in[c].astype(f32)
                )

        @pl.when(has_above)
        def _():
            group_from(c, down_in, None, down_recv)
            band_grad[c, :, rows - W : rows] = band_grad[c, :, rows - W : rows] + down_in[
                c
            ].astype(f32)

        kgrad_ref[:, columns_of(c)] = band_grad[c, 0].astype(bf16)
        vgrad_ref[:, columns_of(c)] = band_grad[c, 1].astype(bf16)

    def within_chunks(t):
        return (t >= 0) & (t < chunks)

    def by_role(bottom, first, between, top):
        return jnp.where(
            me == 0, bottom, jnp.where(me == 1, first, jnp.where(is_last, top, between))
        )

    never = 0 * me - 1

    def step(t, carry):
        @pl.when((t < chunks) & has_below)
        def _():
            suffix_pass(t)

        @pl.when(within_chunks(t - 1) & (me > 1) & has_above)
        def _():
            pass_down(t - 1)

        @pl.when(within_chunks(t - 1) & (me == 1))
        def _():
            finish_first(t - 1)

        a = by_role(never, t - chunks - FIRST_ADD, t - chunks - BETWEEN_ADD, never)

        @pl.when(within_chunks(a))
        def _():
            send_add(a).wait_recv()
            add_out[a] = (suf_grad[a] + add_in[a].astype(f32)).astype(bf16)
            send_add(a).start()

        first_band = jnp.where(
            t <= early, t - 1, jnp.where(t <= chunks, never, t - chunks - 1 + early)
        )
        b = by_role(t, first_band, t - chunks, t - chunks)

        @pl.when(within_chunks(b))
        def _():
            band(b)

        f = jnp.where(is_last, t - 2 * chunks, t - chunks + 1)

        @pl.when(within_chunks(f) & (me > 1))
        def _():
            finish(f)

        first_up = jnp.where(t <= early, t - 1, never)
        for c in range(early, chunks):
            turn = chunks + UP_TURN + c + (UP_HOLD if c >= early + UP_FREE else 0)
            first_up = jnp.where(t == turn, c, first_up)
        u = by_role(t - 1 - BOTTOM_HOLD, first_up, t - chunks - 1, never)

        @pl.when(within_chunks(u))
        def _():
            @pl.when(me < last - 1)
            def _():
                send_up(u).start()

            @pl.when(me == last - 1)
            def _():
                send_up_last(u).start()

        k = by_role(
            t - chunks - 1, t - 2 * chunks - FIRST_LAST, t - 2 * chunks - BETWEEN_HOLD, t - 3 * chunks
        )

        @pl.when(within_chunks(k))
        def _():
            combine(k)

        return carry

    steps = by_role(
        2 * chunks + 1 + BOTTOM_HOLD, 3 * chunks + FIRST_LAST, 3 * chunks + BETWEEN_HOLD, 4 * chunks
    )
    lax.fori_loop(0, steps, step, 0)

    def sent(source, sem):
        remote(source, source, sem, suf_recv.at[0], below).wait_send()

    @pl.when(has_below)
    def _():
        sent(down_out, down_send)

        @pl.when(me == 1)
        def _():
            sent(sfx.at[:, 2:4], suf_send)

        @pl.when(has_above)
        def _():
            sent(kv.at[:, :, own], low_send)
            sent(to_above, rise_send)
            sent(chain_out, chain_send)

        @pl.when(is_last)
        def _():
            sent(kv.at[:, :, W : W + near], low_send)

        @pl.when(me > 1)
        def _():
            sent(sfx, suf_send)
            sent(to_below, fall_send)

    @pl.when(has_above)
    def _():
        sent(kv.at[:, :, own], high_send)
        sent(add_out, add_send)

    @pl.when(me < last - 1)
    def _():
        sent(up_out, up_send)

    @pl.when(me == last - 1)
    def _():
        sent(up_out.at[:, :, :near], up_send)


def spill(*refs):
    sems = refs[8]
    copies = [
        pltpu.make_async_copy(refs[k], refs[4 + k].at[0], sems.at[k]) for k in range(4)
    ]
    for copy in copies:
        copy.start()
    for copy in copies:
        copy.wait()


def per_device(n, query_vectors, key_vectors, value_vectors, out_grad, pad_length):
    rows, features = query_vectors.shape[1:]
    chunks = features // PAIR
    all_keys = rows + 2 * W + G
    vmem = pl.BlockSpec(memory_space=pltpu.VMEM)
    dma = pltpu.SemaphoreType.DMA
    hbm = pl.BlockSpec(memory_space=pltpu.HBM)
    outs = pl.pallas_call(
        functools.partial(kernel, n, rows, chunks),
        out_shape=(pltpu.VMEM((rows, features), bf16),) * 4,
        in_specs=[hbm] * 5,
        out_specs=(vmem,) * 4,
        scratch_shapes=[
            pltpu.SMEM((1,), jnp.int32),
            pltpu.VMEM((chunks, 2, all_keys, PAIR), bf16),
            pltpu.VMEM((chunks, 4, G, PAIR), bf16),
            pltpu.VMEM((chunks, 2, rows, PAIR), bf16),
            pltpu.VMEM((chunks, 8, 2 * G), f32),
            pltpu.VMEM((all_keys, 2 * rows), f32),
            pltpu.VMEM((W + rows, 2 * G), f32),
            pltpu.VMEM((chunks, W + rows, 2 * G), f32),
            pltpu.VMEM((chunks, W + rows, 2 * G), f32),
            pltpu.VMEM((chunks, 2, rows, PAIR), f32),
            pltpu.VMEM((chunks, 2, W + rows, PAIR), f32),
            pltpu.VMEM((chunks, 2, G, PAIR), f32),
        ]
        + [pltpu.VMEM((chunks, 2, W, PAIR), bf16)] * 4
        + [pltpu.VMEM((chunks, 2, G, PAIR), bf16)] * 4
        + [pltpu.VMEM((chunks, 2, 2 * G), f32)] * 4
        + [pltpu.SemaphoreType.REGULAR, dma, dma((2,))]
            + [dma] * 9
        + [dma((chunks,))] * 6
        + [dma((chunks // HIGH_GROUP,))]
        + [dma((chunks // 4 + 1,))] * 2,
        compiler_params=pltpu.CompilerParams(
            collective_id=0, has_side_effects=True, vmem_limit_bytes=48 << 20
        ),
    )(pad_length, *(pltpu.with_memory_space_constraint(x, pltpu.HBM) for x in (query_vectors, key_vectors, value_vectors, out_grad)))
    anywhere = pl.BlockSpec(memory_space=pl.ANY)
    return pl.pallas_call(
        spill,
        out_shape=(jax.ShapeDtypeStruct((1, rows, features), bf16),) * 4,
        in_specs=[vmem] * 4,
        out_specs=(anywhere,) * 4,
        scratch_shapes=[dma((4,))],
    )(*(pltpu.with_memory_space_constraint(x, pltpu.VMEM) for x in outs))


def solution(mesh):
    rows = P(("group", "doc"), "seq", None)
    return jax.shard_map(
        functools.partial(per_device, mesh.shape["seq"]),
        mesh=mesh,
        in_specs=(rows, rows, rows, rows, P(("group", "doc"))),
        out_specs=(rows,) * 4,
        check_vma=False,
    )
```

```python
import functools
import math

import jax
import jax.numpy as jnp
from jax import lax
from jax.experimental import pallas as pl
from jax.experimental.pallas import tpu as pltpu
from jax.sharding import PartitionSpec as P

D = 1024
H = 16
W = 128
G = 64
HEAD = D // H
PAIR = 2 * HEAD
AHEAD = 2
HOP_AHEAD = 3
FAR_AHEAD = 2
BOTTOM_HOLD = 6
BETWEEN_HOLD = 8
EARLY = 3
HIGH_GROUP = 4
UP_HOLD = 1
UP_TURN = 2
UP_FREE = 2
FIRST_ADD = 0
BETWEEN_ADD = 6
FIRST_LAST = 3

MESH = pl.DeviceIdType.MESH
very_negative = -1e30
scale = 1.0 / math.sqrt(HEAD)
f32 = jnp.float32
bf16 = jnp.bfloat16


def dot_nt(a, b):
    return lax.dot_general(a, b, (((1,), (1,)), ((), ())), preferred_element_type=f32)


def dot_nn(a, b):
    return lax.dot_general(a, b, (((1,), (0,)), ((), ())), preferred_element_type=f32)


def dot_tn(a, b):
    return lax.dot_general(a, b, (((0,), (0,)), ((), ())), preferred_element_type=f32)


def iota(shape, dim):
    return lax.broadcasted_iota(jnp.int32, shape, dim)


def pair_mask(value):
    lane = iota((1, PAIR), 1)
    first = jnp.where(lane < HEAD, value, 0.0).astype(bf16)
    second = jnp.where(lane < HEAD, 0.0, value).astype(bf16)
    return first, second


def two_heads(rows, value):
    first, second = pair_mask(value)
    return jnp.concatenate([rows * first, rows * second], axis=0)


def one_pair(stacked):
    half = stacked.shape[0] // 2
    lane = iota((half, PAIR), 1)
    return jnp.where(lane < HEAD, stacked[:half], stacked[half:])


def merge(one, two):
    top = jnp.maximum(one[0], two[0])
    share_one = jnp.exp(one[0] - top)
    share_two = jnp.exp(two[0] - top)
    total = share_one + share_two
    mean = (share_one * one[1] + share_two * two[1]) / total
    return top + jnp.log(total), mean


def kernel(
    n, rows, chunks,
    pad_ref, q_ref, k_ref, v_ref, g_ref,
    att_ref, qgrad_ref, kgrad_ref, vgrad_ref,
    pad, kv, sfx, own_qg, stats, bias, key_bias, expo_s, dprob_s,
    band_grad, fin_grad, suf_grad, down_out, down_in, up_out, up_in,
    chain_out, chain_in, add_out, add_in, from_above, to_below, from_below, to_above,
    reply, pad_sem, load_sem,
    suf_send, low_send, high_send, down_send, up_send, chain_send, add_send,
    fall_send, rise_send,
    suf_recv, fall_recv, low_recv, chain_recv, add_recv, rise_recv,
    high_recv, down_recv, up_recv,
):
    me = lax.axis_index("seq")
    last = n - 1
    below = lax.rem(me + n - 1, n)
    above = lax.rem(me + 1, n)
    has_below = me > 0
    has_above = me < last
    is_last = me == last
    middle = has_below & has_above
    all_keys = rows + 2 * W + G
    own = slice(W, W + rows)
    low = slice(0, W)
    high = slice(W + rows, 2 * W + rows)
    suf = slice(2 * W + rows, all_keys)
    tail = slice(rows - G, rows)
    near = min(W, rows - G)

    def columns_of(c):
        if isinstance(c, int):
            return pl.ds(c * PAIR, PAIR)
        return pl.ds(pl.multiple_of(c * PAIR, PAIR), PAIR)

    def remote(src, dst, send, recv, target):
        return pltpu.make_async_remote_copy(
            src_ref=src, dst_ref=dst, send_sem=send, recv_sem=recv,
            device_id={"seq": target}, device_id_type=MESH,
        )

    def start_pair(sources, source_rows, target_of, send, recv, target, c):
        for k, source in enumerate(sources):
            remote(
                source.at[0, source_rows, columns_of(c)], target_of(k), send, recv, target
            ).start()

    def send_suf(c):
        return remote(sfx.at[c], sfx.at[c], suf_send, suf_recv.at[c], below)

    def send_suf_bottom(c):
        keys = sfx.at[c, 2:4]
        return remote(keys, keys, suf_send, suf_recv.at[c], below)

    def low_slot(c):
        return max(c - 2, 0) if isinstance(c, int) else jnp.maximum(c - 2, 0)

    def wait_low(c, part):
        def wait(first, count):
            some = kv.at[pl.ds(first, count), :, part]
            pltpu.make_async_copy(some, some, low_recv.at[low_slot(c)]).wait()

        @pl.when(c == 0)
        def _():
            wait(0, 3)

        @pl.when(c > 2)
        def _():
            wait(c, 1)

    def send_low(c):
        return remote(kv.at[c, :, own], kv.at[c, :, high], low_send, low_recv.at[low_slot(c)], below)

    def send_low_last(c):
        return remote(
            kv.at[c, :, W : W + near],
            kv.at[c, :, W + rows : W + rows + near],
            low_send, low_recv.at[low_slot(c)], below,
        )

    def send_high(c):
        some = pl.ds(c, HIGH_GROUP)
        return remote(
            kv.at[some, :, own], kv.at[some, :, low],
            high_send, high_recv.at[c // HIGH_GROUP], above,
        )

    def early_suf_last(c):
        start_pair(
            (q_ref, g_ref, k_ref, v_ref), tail, lambda k: sfx.at[c, k],
            suf_send, suf_recv.at[c], below, c,
        )

    def early_low(c):
        start_pair(
            (k_ref, v_ref), slice(0, rows), lambda k: kv.at[c, k, high],
            low_send, low_recv.at[low_slot(c)], below, c,
        )

    def send_down(c):
        return remote(down_out.at[c], down_in.at[c], down_send, down_recv.at[(c + 1) // 4], below)

    def send_up(c):
        return remote(up_out.at[c], up_in.at[c], up_send, up_recv.at[(c + 1) // 4], above)

    def send_up_last(c):
        return remote(
            up_out.at[c, :, :near], up_in.at[c, :, :near], up_send, up_recv.at[(c + 1) // 4], above
        )

    def send_chain(c):
        return remote(chain_out.at[c], chain_in.at[c], chain_send, chain_recv.at[c], above)

    def send_add(c):
        return remote(add_out.at[c], add_in.at[c], add_send, add_recv.at[c], above)

    def send_fall(c):
        return remote(to_below.at[c], from_above.at[c], fall_send, fall_recv.at[c], below)

    def send_rise(c):
        return remote(to_above.at[c], from_below.at[c], rise_send, rise_recv.at[c], above)

    def group_from(c, ref, part, sem):
        for group in range(chunks // 4 + 1):
            first = max(4 * group - 1, 0)
            count = min(4 * group + 3, chunks) - first

            @pl.when(c == first)
            def _():
                some = pl.ds(first, count)
                whole = ref.at[some] if part is None else ref.at[some, :, part]
                pltpu.make_async_copy(whole, whole, sem.at[group]).wait()

    def wait_high(c):
        @pl.when(c % HIGH_GROUP == 0)
        def _():
            send_high(c).wait_recv()

    early = min(EARLY, chunks)
    lead = HOP_AHEAD + FAR_AHEAD * (last - 1 - me)
    barrier = pltpu.get_barrier_semaphore()

    def tell(sem, target):
        pl.semaphore_signal(sem, inc=1, device_id={"seq": target}, device_id_type=MESH)

    pad_copy = pltpu.make_async_copy(pad_ref, pad, pad_sem)
    if n == 4:
        @pl.when(middle)
        def _():
            tell(barrier, jnp.where(me == 1, above, below))
            tell(barrier, jnp.where(me == 1, below, above))
    else:
        @pl.when(has_above)
        def _():
            tell(barrier, above)

    pad_copy.start()
    for c in range(chunks):
        pieces = (
            (k_ref, kv.at[c, 0, own]),
            (v_ref, kv.at[c, 1, own]),
            (q_ref, own_qg.at[c, 0]),
            (g_ref, own_qg.at[c, 1]),
        )
        for k, (source, target) in enumerate(pieces):
            pltpu.make_async_copy(
                source.at[0, :, columns_of(c)], target, load_sem.at[k // 2]
            ).start()

    if n == 4:
        pl.semaphore_wait(barrier, 1)

        @pl.when(me == 0)
        def _():
            tell(reply, above)

        @pl.when(is_last)
        def _():
            tell(reply, below)
    else:
        @pl.when(has_below)
        def _():
            pl.semaphore_wait(barrier, 1)
            tell(reply, below)

    @pl.when(is_last)
    def _():
        for c in range(AHEAD):
            early_suf_last(c)

    for c in range(chunks):
        @pl.when(middle & (me > 1) & (c < lead))
        def _():
            early_low(c)

    loaded = (kv.at[:, :, own], own_qg)
    for k, target in enumerate(loaded):
        pltpu.make_async_copy(target, target, load_sem.at[k]).wait()

    def start_high():
        for c in range(0, chunks, HIGH_GROUP):
            send_high(c).start()

    def start_low_first():
        for c in range(chunks):
            @pl.when(c < lead)
            def _():
                send_low(c).start()

    if n == 4:
        @pl.when(me == 0)
        def _():
            start_high()

        @pl.when(me == 1)
        def _():
            start_high()
            pl.semaphore_wait(reply, 1)
            start_low_first()

        @pl.when(me == 2)
        def _():
            pl.semaphore_wait(reply, 1)
            start_high()
    else:
        @pl.when(me == 1)
        def _():
            start_low_first()

        @pl.when(has_above)
        def _():
            pl.semaphore_wait(reply, 1)
            start_high()

    @pl.when(is_last)
    def _():
        for c in range(chunks):
            kv[c, :, high] = jnp.zeros((2, W, PAIR), bf16)

    @pl.when(me == last - 1)
    def _():
        for c in range(chunks):
            kv[c, :, W + rows + near : 2 * W + rows] = jnp.zeros((2, W - near, PAIR), bf16)

    @pl.when(me == 0)
    def _():
        for c in range(chunks):
            kv[c, :, low] = jnp.zeros((2, W, PAIR), bf16)

    pad_copy.wait()
    suffix_start = rows * n - G
    valid_end = suffix_start - pad[0]
    first_row = me * rows
    j = iota((all_keys, 2 * rows), 0)
    i = iota((all_keys, 2 * rows), 1)
    i = jnp.where(i >= rows, i - rows, i)
    key_pos = first_row - W + j
    apart = i - (j - W)
    within = (apart <= W) & (apart >= -W) & (key_pos >= 0) & (key_pos < valid_end)
    bias[...] = jnp.where(within | (j >= 2 * W + rows), 0.0, very_negative)
    near_pos = first_row - W + iota((W + rows, 2 * G), 0)
    key_bias[...] = jnp.where(
        (near_pos < valid_end) | (near_pos >= suffix_start), 0.0, very_negative
    )
    query_lane = iota((1, 2 * rows), 1)
    query_pos = first_row + jnp.where(query_lane >= rows, query_lane - rows, query_lane)
    row_live = jnp.where(query_pos < suffix_start, 1.0, 0.0)

    @pl.when(is_last)
    def _():
        for c in range(chunks):
            sfx[c, 0:2] = own_qg[c, :, tail]
            sfx[c, 2:4] = kv[c, :, W + rows - G : W + rows]

    def suffix_stats(c, keys):
        query_two = two_heads(sfx[c, 0], scale)
        grad_two = two_heads(sfx[c, 1], 1.0)
        scores = dot_nt(kv[c, 0, keys], query_two) + key_bias[keys]
        largest = jnp.max(scores, axis=0, keepdims=True)
        expo = jnp.exp(scores - largest)
        dprob = dot_nt(kv[c, 1, keys], grad_two)
        total = jnp.sum(expo, axis=0, keepdims=True)
        weighted = jnp.sum(expo * dprob, axis=0, keepdims=True)
        expo_s[c, keys] = expo
        dprob_s[c, keys] = dprob
        stats[c, 0:1] = largest
        stats[c, 1:2] = largest + jnp.log(total)
        stats[c, 2:3] = weighted / total

    def pair_of(ref, c, at):
        return ref[c, at : at + 1], ref[c, at + 1 : at + 2]

    def put(ref, c, values):
        ref[c, 0:1] = values[0]
        ref[c, 1:2] = values[1]

    def suffix_parts(c, keys, whole):
        top, delta = whole
        probs = expo_s[c, keys] * jnp.exp(stats[c, 0:1] - top)
        probs_low = probs.astype(bf16)
        dscore = (probs * (dprob_s[c, keys] - delta)).astype(bf16)
        query_two = two_heads(sfx[c, 0], scale)
        grad_two = two_heads(sfx[c, 1], 1.0)
        att_part = one_pair(dot_tn(probs_low, kv[c, 1, keys]))
        query_part = one_pair(dot_tn(dscore, kv[c, 0, keys])) * scale
        fin_grad[c, 0, keys] = dot_nn(dscore, query_two)
        fin_grad[c, 1, keys] = dot_nn(probs_low, grad_two)
        return att_part, query_part

    both = slice(0, W + rows)

    def suffix_pass(c):
        @pl.when(middle)
        def _():
            send_suf(c).wait_recv()

            @pl.when(me > 1)
            def _():
                send_suf(c).start()

            @pl.when(me == 1)
            def _():
                send_suf_bottom(c).start()

        @pl.when((me == 1) & (c % 2 == 1) & (lead + c // 2 < chunks))
        def _():
            send_low(lead + c // 2).start()

        @pl.when(me > 1)
        def _():
            suffix_stats(c, own)

        @pl.when(me == 1)
        def _():
            wait_high(c)
            suffix_stats(c, both)
            put(to_above, c, pair_of(stats, c, 1))
            send_rise(c).start()

        @pl.when(is_last)
        def _():
            put(to_below, c, pair_of(stats, c, 1))
            send_fall(c).start()

            @pl.when(c + AHEAD < chunks)
            def _():
                send_suf(c + AHEAD).start()

        @pl.when((c == chunks - 1) & is_last)
        def _():
            for k in range(chunks):
                send_low_last(k).start()

    def pass_down(c):
        send_fall(c).wait_recv()
        put(to_below, c, merge(pair_of(stats, c, 1), pair_of(from_above, c, 0)))
        send_fall(c).start()

        @pl.when(c == chunks - 1)
        def _():
            for k in range(chunks):
                @pl.when(k >= lead)
                def _():
                    send_low(k).start()

    def finish_first(c):
        send_fall(c).wait_recv()
        whole = merge(pair_of(stats, c, 1), pair_of(from_above, c, 0))
        att_part, query_part = suffix_parts(c, both, whole)
        chain_out[c, 0] = att_part.astype(bf16)
        chain_out[c, 1] = query_part.astype(bf16)
        send_chain(c).start()

        @pl.when(c == chunks - 1)
        def _():
            for k in range(early):
                send_down(k).start()

    def finish(c):
        send_rise(c).wait_recv()
        to_here = merge(pair_of(stats, c, 1), pair_of(from_below, c, 0))

        def parts(whole):
            att_part, query_part = suffix_parts(c, own, whole)
            send_chain(c).wait_recv()
            att_sum = att_part + chain_in[c, 0].astype(f32)
            query_sum = query_part + chain_in[c, 1].astype(f32)
            return att_sum.astype(bf16), query_sum.astype(bf16)

        @pl.when(has_above)
        def _():
            put(to_above, c, to_here)
            send_rise(c).start()
            att_sum, query_sum = parts(merge(to_here, pair_of(from_above, c, 0)))
            chain_out[c, 0] = att_sum
            chain_out[c, 1] = query_sum
            send_chain(c).start()

        @pl.when(is_last)
        def _():
            att_sum, query_sum = parts(to_here)
            att_ref[tail, columns_of(c)] = att_sum
            qgrad_ref[tail, columns_of(c)] = query_sum

    def band(c):
        @pl.when(me > 1)
        def _():
            wait_high(c)

        @pl.when(me == 0)
        def _():
            send_suf_bottom(c).wait_recv()

        @pl.when(me < last - 1)
        def _():
            wait_low(c, high)

        @pl.when(me == last - 1)
        def _():
            wait_low(c, slice(W + rows, W + rows + near))

        kv[c, :, suf] = sfx[c, 2:4]
        query_two = two_heads(own_qg[c, 0], scale)
        grad_two = two_heads(own_qg[c, 1], 1.0)
        keys = kv[c, 0]
        values = kv[c, 1]
        scores = dot_nt(keys, query_two) + bias[...]
        largest = jnp.max(scores, axis=0, keepdims=True)
        expo = jnp.exp(scores - largest)
        total = jnp.sum(expo, axis=0, keepdims=True)
        dprob = dot_nt(values, grad_two)
        inverse = 1.0 / total
        delta = jnp.sum(expo * dprob, axis=0, keepdims=True) * inverse
        probs = expo * (inverse * row_live)
        probs_low = probs.astype(bf16)
        dscore = (probs * (dprob - delta)).astype(bf16)
        att_ref[:, columns_of(c)] = one_pair(dot_tn(probs_low, values)).astype(bf16)
        qgrad_ref[:, columns_of(c)] = (one_pair(dot_tn(dscore, keys)) * scale).astype(bf16)
        key_all = dot_nn(dscore, query_two)
        value_all = dot_nn(probs_low, grad_two)

        @pl.when(me == 1)
        def _():
            down_out[c, 0] = (key_all[low] + fin_grad[c, 0, low]).astype(bf16)
            down_out[c, 1] = (value_all[low] + fin_grad[c, 1, low]).astype(bf16)

        @pl.when(me != 1)
        def _():
            down_out[c, 0] = key_all[low].astype(bf16)
            down_out[c, 1] = value_all[low].astype(bf16)

        @pl.when(me == 0)
        def _():
            add_out[c, 0] = key_all[suf].astype(bf16)
            add_out[c, 1] = value_all[suf].astype(bf16)
            send_add(c).start()

        up_out[c, 0] = key_all[high].astype(bf16)
        up_out[c, 1] = value_all[high].astype(bf16)
        band_grad[c, 0] = key_all[own]
        band_grad[c, 1] = value_all[own]
        suf_grad[c, 0] = key_all[suf]
        suf_grad[c, 1] = value_all[suf]

        @pl.when(has_below & ((me > 1) | (c >= early)))
        def _():
            send_down(c).start()

    def combine(c):
        @pl.when(has_below)
        def _():
            band_grad[c] = band_grad[c] + fin_grad[c, :, own]

            @pl.when(me < last)
            def _():
                group_from(c, up_in, None, up_recv)
                band_grad[c, :, 0:W] = band_grad[c, :, 0:W] + up_in[c].astype(f32)

            @pl.when(is_last)
            def _():
                group_from(c, up_in, slice(0, near), up_recv)
                band_grad[c, :, 0:near] = band_grad[c, :, 0:near] + up_in[c, :, 0:near].astype(f32)
                send_add(c).wait_recv()
                band_grad[c, :, tail] = (
                    band_grad[c, :, tail] + suf_grad[c] + add_in[c].astype(f32)
                )

        @pl.when(has_above)
        def _():
            group_from(c, down_in, None, down_recv)
            band_grad[c, :, rows - W : rows] = band_grad[c, :, rows - W : rows] + down_in[
                c
            ].astype(f32)

        kgrad_ref[:, columns_of(c)] = band_grad[c, 0].astype(bf16)
        vgrad_ref[:, columns_of(c)] = band_grad[c, 1].astype(bf16)

    def within_chunks(t):
        return (t >= 0) & (t < chunks)

    def by_role(bottom, first, between, top):
        return jnp.where(
            me == 0, bottom, jnp.where(me == 1, first, jnp.where(is_last, top, between))
        )

    never = 0 * me - 1

    def step(t, carry):
        @pl.when((t < chunks) & has_below)
        def _():
            suffix_pass(t)

        @pl.when(within_chunks(t - 1) & (me > 1) & has_above)
        def _():
            pass_down(t - 1)

        @pl.when(within_chunks(t - 1) & (me == 1))
        def _():
            finish_first(t - 1)

        a = by_role(never, t - chunks - FIRST_ADD, t - chunks - BETWEEN_ADD, never)

        @pl.when(within_chunks(a))
        def _():
            send_add(a).wait_recv()
            add_out[a] = (suf_grad[a] + add_in[a].astype(f32)).astype(bf16)
            send_add(a).start()

        first_band = jnp.where(
            t <= early, t - 1, jnp.where(t <= chunks, never, t - chunks - 1 + early)
        )
        b = by_role(t, first_band, t - chunks, t - chunks)

        @pl.when(within_chunks(b))
        def _():
            band(b)

        f = jnp.where(is_last, t - 2 * chunks, t - chunks + 1)

        @pl.when(within_chunks(f) & (me > 1))
        def _():
            finish(f)

        first_up = jnp.where(t <= early, t - 1, never)
        for c in range(early, chunks):
            turn = chunks + UP_TURN + c + (UP_HOLD if c >= early + UP_FREE else 0)
            first_up = jnp.where(t == turn, c, first_up)
        u = by_role(t - 1 - BOTTOM_HOLD, first_up, t - chunks - 1, never)

        @pl.when(within_chunks(u))
        def _():
            @pl.when(me < last - 1)
            def _():
                send_up(u).start()

            @pl.when(me == last - 1)
            def _():
                send_up_last(u).start()

        k = by_role(
            t - chunks - 1, t - 2 * chunks - FIRST_LAST, t - 2 * chunks - BETWEEN_HOLD, t - 3 * chunks
        )

        @pl.when(within_chunks(k))
        def _():
            combine(k)

        return carry

    steps = by_role(
        2 * chunks + 1 + BOTTOM_HOLD, 3 * chunks + FIRST_LAST, 3 * chunks + BETWEEN_HOLD, 4 * chunks
    )
    lax.fori_loop(0, steps, step, 0)

    def sent(source, sem):
        remote(source, source, sem, suf_recv.at[0], below).wait_send()

    @pl.when(has_below)
    def _():
        sent(down_out, down_send)

        @pl.when(me == 1)
        def _():
            sent(sfx.at[:, 2:4], suf_send)

        @pl.when(has_above)
        def _():
            sent(kv.at[:, :, own], low_send)
            sent(to_above, rise_send)
            sent(chain_out, chain_send)

        @pl.when(is_last)
        def _():
            sent(kv.at[:, :, W : W + near], low_send)

        @pl.when(me > 1)
        def _():
            sent(sfx, suf_send)
            sent(to_below, fall_send)

    @pl.when(has_above)
    def _():
        sent(kv.at[:, :, own], high_send)
        sent(add_out, add_send)

    @pl.when(me < last - 1)
    def _():
        sent(up_out, up_send)

    @pl.when(me == last - 1)
    def _():
        sent(up_out.at[:, :, :near], up_send)


def spill(*refs):
    sems = refs[8]
    copies = [
        pltpu.make_async_copy(refs[k], refs[4 + k].at[0], sems.at[k]) for k in range(4)
    ]
    for copy in copies:
        copy.start()
    for copy in copies:
        copy.wait()


def per_device(n, query_vectors, key_vectors, value_vectors, out_grad, pad_length):
    rows, features = query_vectors.shape[1:]
    chunks = features // PAIR
    all_keys = rows + 2 * W + G
    vmem = pl.BlockSpec(memory_space=pltpu.VMEM)
    dma = pltpu.SemaphoreType.DMA
    hbm = pl.BlockSpec(memory_space=pltpu.HBM)
    outs = pl.pallas_call(
        functools.partial(kernel, n, rows, chunks),
        out_shape=(pltpu.VMEM((rows, features), bf16),) * 4,
        in_specs=[hbm] * 5,
        out_specs=(vmem,) * 4,
        scratch_shapes=[
            pltpu.SMEM((1,), jnp.int32),
            pltpu.VMEM((chunks, 2, all_keys, PAIR), bf16),
            pltpu.VMEM((chunks, 4, G, PAIR), bf16),
            pltpu.VMEM((chunks, 2, rows, PAIR), bf16),
            pltpu.VMEM((chunks, 8, 2 * G), f32),
            pltpu.VMEM((all_keys, 2 * rows), f32),
            pltpu.VMEM((W + rows, 2 * G), f32),
            pltpu.VMEM((chunks, W + rows, 2 * G), f32),
            pltpu.VMEM((chunks, W + rows, 2 * G), f32),
            pltpu.VMEM((chunks, 2, rows, PAIR), f32),
            pltpu.VMEM((chunks, 2, W + rows, PAIR), f32),
            pltpu.VMEM((chunks, 2, G, PAIR), f32),
        ]
        + [pltpu.VMEM((chunks, 2, W, PAIR), bf16)] * 4
        + [pltpu.VMEM((chunks, 2, G, PAIR), bf16)] * 4
        + [pltpu.VMEM((chunks, 2, 2 * G), f32)] * 4
        + [pltpu.SemaphoreType.REGULAR, dma, dma((2,))]
            + [dma] * 9
        + [dma((chunks,))] * 2
        + [dma((chunks - 2,))]
        + [dma((chunks,))] * 3
        + [dma((chunks // HIGH_GROUP,))]
        + [dma((chunks // 4 + 1,))] * 2,
        compiler_params=pltpu.CompilerParams(
            collective_id=0, has_side_effects=True, vmem_limit_bytes=48 << 20
        ),
    )(pad_length, *(pltpu.with_memory_space_constraint(x, pltpu.HBM) for x in (query_vectors, key_vectors, value_vectors, out_grad)))
    anywhere = pl.BlockSpec(memory_space=pl.ANY)
    return pl.pallas_call(
        spill,
        out_shape=(jax.ShapeDtypeStruct((1, rows, features), bf16),) * 4,
        in_specs=[vmem] * 4,
        out_specs=(anywhere,) * 4,
        scratch_shapes=[dma((4,))],
    )(*(pltpu.with_memory_space_constraint(x, pltpu.VMEM) for x in outs))


def solution(mesh):
    rows = P(("group", "doc"), "seq", None)
    return jax.shard_map(
        functools.partial(per_device, mesh.shape["seq"]),
        mesh=mesh,
        in_specs=(rows, rows, rows, rows, P(("group", "doc"))),
        out_specs=(rows,) * 4,
        check_vma=False,
    )
```

```python
import functools
import math

import jax
import jax.numpy as jnp
from jax import lax
from jax.experimental import pallas as pl
from jax.experimental.pallas import tpu as pltpu
from jax.sharding import PartitionSpec as P

D = 1024
H = 16
W = 128
G = 64
HEAD = D // H
PAIR = 2 * HEAD
AHEAD = 2
HOP_AHEAD = 3
FAR_AHEAD = 2
BOTTOM_HOLD = 6
BETWEEN_HOLD = 8
EARLY = 3
HIGH_GROUP = 4
UP_HOLD = 1
UP_TURN = 1
UP_FREE = 2
FIRST_ADD = 0
BETWEEN_ADD = 6
FIRST_LAST = 3

MESH = pl.DeviceIdType.MESH
very_negative = -1e30
scale = 1.0 / math.sqrt(HEAD)
f32 = jnp.float32
bf16 = jnp.bfloat16


def dot_nt(a, b):
    return lax.dot_general(a, b, (((1,), (1,)), ((), ())), preferred_element_type=f32)


def dot_nn(a, b):
    return lax.dot_general(a, b, (((1,), (0,)), ((), ())), preferred_element_type=f32)


def dot_tn(a, b):
    return lax.dot_general(a, b, (((0,), (0,)), ((), ())), preferred_element_type=f32)


def iota(shape, dim):
    return lax.broadcasted_iota(jnp.int32, shape, dim)


def pair_mask(value):
    lane = iota((1, PAIR), 1)
    first = jnp.where(lane < HEAD, value, 0.0).astype(bf16)
    second = jnp.where(lane < HEAD, 0.0, value).astype(bf16)
    return first, second


def two_heads(rows, value):
    first, second = pair_mask(value)
    return jnp.concatenate([rows * first, rows * second], axis=0)


def one_pair(stacked):
    half = stacked.shape[0] // 2
    lane = iota((half, PAIR), 1)
    return jnp.where(lane < HEAD, stacked[:half], stacked[half:])


def merge(one, two):
    top = jnp.maximum(one[0], two[0])
    share_one = jnp.exp(one[0] - top)
    share_two = jnp.exp(two[0] - top)
    total = share_one + share_two
    mean = (share_one * one[1] + share_two * two[1]) / total
    return top + jnp.log(total), mean


def kernel(
    n, rows, chunks,
    pad_ref, q_ref, k_ref, v_ref, g_ref,
    att_ref, qgrad_ref, kgrad_ref, vgrad_ref,
    pad, kv, sfx, own_qg, stats, bias, key_bias, expo_s, dprob_s,
    band_grad, fin_grad, suf_grad, down_out, down_in, up_out, up_in,
    chain_out, chain_in, add_out, add_in, from_above, to_below, from_below, to_above,
    reply, pad_sem, load_sem,
    suf_send, low_send, high_send, down_send, up_send, chain_send, add_send,
    fall_send, rise_send,
    suf_recv, fall_recv, low_recv, chain_recv, add_recv, rise_recv,
    high_recv, down_recv, up_recv,
):
    me = lax.axis_index("seq")
    last = n - 1
    below = lax.rem(me + n - 1, n)
    above = lax.rem(me + 1, n)
    has_below = me > 0
    has_above = me < last
    is_last = me == last
    middle = has_below & has_above
    all_keys = rows + 2 * W + G
    own = slice(W, W + rows)
    low = slice(0, W)
    high = slice(W + rows, 2 * W + rows)
    suf = slice(2 * W + rows, all_keys)
    tail = slice(rows - G, rows)
    near = min(W, rows - G)

    def columns_of(c):
        if isinstance(c, int):
            return pl.ds(c * PAIR, PAIR)
        return pl.ds(pl.multiple_of(c * PAIR, PAIR), PAIR)

    def remote(src, dst, send, recv, target):
        return pltpu.make_async_remote_copy(
            src_ref=src, dst_ref=dst, send_sem=send, recv_sem=recv,
            device_id={"seq": target}, device_id_type=MESH,
        )

    def start_pair(sources, source_rows, target_of, send, recv, target, c):
        for k, source in enumerate(sources):
            remote(
                source.at[0, source_rows, columns_of(c)], target_of(k), send, recv, target
            ).start()

    def send_suf(c):
        return remote(sfx.at[c], sfx.at[c], suf_send, suf_recv.at[c], below)

    def send_suf_bottom(c):
        keys = sfx.at[c, 2:4]
        return remote(keys, keys, suf_send, suf_recv.at[c], below)

    def send_low(c):
        return remote(kv.at[c, :, own], kv.at[c, :, high], low_send, low_recv.at[c], below)

    def send_low_last(c):
        return remote(
            kv.at[c, :, W : W + near],
            kv.at[c, :, W + rows : W + rows + near],
            low_send, low_recv.at[c], below,
        )

    def send_high(c):
        some = pl.ds(c, HIGH_GROUP)
        return remote(
            kv.at[some, :, own], kv.at[some, :, low],
            high_send, high_recv.at[c // HIGH_GROUP], above,
        )

    def early_suf_last(c):
        start_pair(
            (q_ref, g_ref, k_ref, v_ref), tail, lambda k: sfx.at[c, k],
            suf_send, suf_recv.at[c], below, c,
        )

    def early_low(c):
        start_pair(
            (k_ref, v_ref), slice(0, rows), lambda k: kv.at[c, k, high],
            low_send, low_recv.at[c], below, c,
        )

    def send_down(c):
        return remote(down_out.at[c], down_in.at[c], down_send, down_recv.at[(c + 1) // 4], below)

    def send_up(c):
        return remote(up_out.at[c], up_in.at[c], up_send, up_recv.at[(c + 1) // 4], above)

    def send_up_last(c):
        return remote(
            up_out.at[c, :, :near], up_in.at[c, :, :near], up_send, up_recv.at[(c + 1) // 4], above
        )

    def send_chain(c):
        return remote(chain_out.at[c], chain_in.at[c], chain_send, chain_recv.at[c], above)

    def send_add(c):
        return remote(add_out.at[c], add_in.at[c], add_send, add_recv.at[c], above)

    def send_fall(c):
        return remote(to_below.at[c], from_above.at[c], fall_send, fall_recv.at[c], below)

    def send_rise(c):
        return remote(to_above.at[c], from_below.at[c], rise_send, rise_recv.at[c], above)

    def group_from(c, ref, part, sem):
        for group in range(chunks // 4 + 1):
            first = max(4 * group - 1, 0)
            count = min(4 * group + 3, chunks) - first

            @pl.when(c == first)
            def _():
                some = pl.ds(first, count)
                whole = ref.at[some] if part is None else ref.at[some, :, part]
                pltpu.make_async_copy(whole, whole, sem.at[group]).wait()

    def wait_high(c):
        @pl.when(c % HIGH_GROUP == 0)
        def _():
            send_high(c).wait_recv()

    early = min(EARLY, chunks)
    lead = HOP_AHEAD + FAR_AHEAD * (last - 1 - me)
    barrier = pltpu.get_barrier_semaphore()

    def tell(sem, target):
        pl.semaphore_signal(sem, inc=1, device_id={"seq": target}, device_id_type=MESH)

    pad_copy = pltpu.make_async_copy(pad_ref, pad, pad_sem)
    if n == 4:
        @pl.when(middle)
        def _():
            tell(barrier, jnp.where(me == 1, above, below))
            tell(barrier, jnp.where(me == 1, below, above))
    else:
        @pl.when(has_above)
        def _():
            tell(barrier, above)

    pad_copy.start()
    for c in range(chunks):
        pieces = (
            (k_ref, kv.at[c, 0, own]),
            (v_ref, kv.at[c, 1, own]),
            (q_ref, own_qg.at[c, 0]),
            (g_ref, own_qg.at[c, 1]),
        )
        for k, (source, target) in enumerate(pieces):
            pltpu.make_async_copy(
                source.at[0, :, columns_of(c)], target, load_sem.at[k // 2]
            ).start()

    if n == 4:
        pl.semaphore_wait(barrier, 1)

        @pl.when(me == 0)
        def _():
            tell(reply, above)

        @pl.when(is_last)
        def _():
            tell(reply, below)
    else:
        @pl.when(has_below)
        def _():
            pl.semaphore_wait(barrier, 1)
            tell(reply, below)

    @pl.when(is_last)
    def _():
        for c in range(AHEAD):
            early_suf_last(c)

    for c in range(chunks):
        @pl.when(middle & (me > 1) & (c < lead))
        def _():
            early_low(c)

    loaded = (kv.at[:, :, own], own_qg)
    for k, target in enumerate(loaded):
        pltpu.make_async_copy(target, target, load_sem.at[k]).wait()

    def start_high():
        for c in range(0, chunks, HIGH_GROUP):
            send_high(c).start()

    def start_low_first():
        for c in range(chunks):
            @pl.when(c < lead)
            def _():
                send_low(c).start()

    if n == 4:
        @pl.when(me == 0)
        def _():
            start_high()

        @pl.when(me == 1)
        def _():
            start_high()
            pl.semaphore_wait(reply, 1)
            start_low_first()

        @pl.when(me == 2)
        def _():
            pl.semaphore_wait(reply, 1)
            start_high()
    else:
        @pl.when(me == 1)
        def _():
            start_low_first()

        @pl.when(has_above)
        def _():
            pl.semaphore_wait(reply, 1)
            start_high()

    @pl.when(is_last)
    def _():
        for c in range(chunks):
            kv[c, :, high] = jnp.zeros((2, W, PAIR), bf16)

    @pl.when(me == last - 1)
    def _():
        for c in range(chunks):
            kv[c, :, W + rows + near : 2 * W + rows] = jnp.zeros((2, W - near, PAIR), bf16)

    @pl.when(me == 0)
    def _():
        for c in range(chunks):
            kv[c, :, low] = jnp.zeros((2, W, PAIR), bf16)

    pad_copy.wait()
    suffix_start = rows * n - G
    valid_end = suffix_start - pad[0]
    first_row = me * rows
    j = iota((all_keys, 2 * rows), 0)
    i = iota((all_keys, 2 * rows), 1)
    i = jnp.where(i >= rows, i - rows, i)
    key_pos = first_row - W + j
    apart = i - (j - W)
    within = (apart <= W) & (apart >= -W) & (key_pos >= 0) & (key_pos < valid_end)
    bias[...] = jnp.where(within | (j >= 2 * W + rows), 0.0, very_negative)
    near_pos = first_row - W + iota((W + rows, 2 * G), 0)
    key_bias[...] = jnp.where(
        (near_pos < valid_end) | (near_pos >= suffix_start), 0.0, very_negative
    )
    query_lane = iota((1, 2 * rows), 1)
    query_pos = first_row + jnp.where(query_lane >= rows, query_lane - rows, query_lane)
    row_live = jnp.where(query_pos < suffix_start, 1.0, 0.0)

    @pl.when(is_last)
    def _():
        for c in range(chunks):
            sfx[c, 0:2] = own_qg[c, :, tail]
            sfx[c, 2:4] = kv[c, :, W + rows - G : W + rows]

    def suffix_stats(c, keys):
        query_two = two_heads(sfx[c, 0], scale)
        grad_two = two_heads(sfx[c, 1], 1.0)
        scores = dot_nt(kv[c, 0, keys], query_two) + key_bias[keys]
        largest = jnp.max(scores, axis=0, keepdims=True)
        expo = jnp.exp(scores - largest)
        dprob = dot_nt(kv[c, 1, keys], grad_two)
        total = jnp.sum(expo, axis=0, keepdims=True)
        weighted = jnp.sum(expo * dprob, axis=0, keepdims=True)
        expo_s[c, keys] = expo
        dprob_s[c, keys] = dprob
        stats[c, 0:1] = largest
        stats[c, 1:2] = largest + jnp.log(total)
        stats[c, 2:3] = weighted / total

    def pair_of(ref, c, at):
        return ref[c, at : at + 1], ref[c, at + 1 : at + 2]

    def put(ref, c, values):
        ref[c, 0:1] = values[0]
        ref[c, 1:2] = values[1]

    def suffix_parts(c, keys, whole):
        top, delta = whole
        probs = expo_s[c, keys] * jnp.exp(stats[c, 0:1] - top)
        probs_low = probs.astype(bf16)
        dscore = (probs * (dprob_s[c, keys] - delta)).astype(bf16)
        query_two = two_heads(sfx[c, 0], scale)
        grad_two = two_heads(sfx[c, 1], 1.0)
        att_part = one_pair(dot_tn(probs_low, kv[c, 1, keys]))
        query_part = one_pair(dot_tn(dscore, kv[c, 0, keys])) * scale
        fin_grad[c, 0, keys] = dot_nn(dscore, query_two)
        fin_grad[c, 1, keys] = dot_nn(probs_low, grad_two)
        return att_part, query_part

    both = slice(0, W + rows)

    def suffix_pass(c):
        @pl.when(middle)
        def _():
            send_suf(c).wait_recv()

            @pl.when(me > 1)
            def _():
                send_suf(c).start()

            @pl.when(me == 1)
            def _():
                send_suf_bottom(c).start()

        @pl.when((me == 1) & (c % 2 == 1) & (lead + c // 2 < chunks))
        def _():
            send_low(lead + c // 2).start()

        @pl.when(me > 1)
        def _():
            suffix_stats(c, own)

        @pl.when(me == 1)
        def _():
            wait_high(c)
            suffix_stats(c, both)
            put(to_above, c, pair_of(stats, c, 1))
            send_rise(c).start()

        @pl.when(is_last)
        def _():
            put(to_below, c, pair_of(stats, c, 1))
            send_fall(c).start()

            @pl.when(c + AHEAD < chunks)
            def _():
                send_suf(c + AHEAD).start()

        @pl.when((c == chunks - 1) & is_last)
        def _():
            for k in range(chunks):
                send_low_last(k).start()

    def pass_down(c):
        send_fall(c).wait_recv()
        put(to_below, c, merge(pair_of(stats, c, 1), pair_of(from_above, c, 0)))
        send_fall(c).start()

        @pl.when(c == chunks - 1)
        def _():
            for k in range(chunks):
                @pl.when(k >= lead)
                def _():
                    send_low(k).start()

    def finish_first(c):
        send_fall(c).wait_recv()
        whole = merge(pair_of(stats, c, 1), pair_of(from_above, c, 0))
        att_part, query_part = suffix_parts(c, both, whole)
        chain_out[c, 0] = att_part.astype(bf16)
        chain_out[c, 1] = query_part.astype(bf16)
        send_chain(c).start()

        @pl.when(c == chunks - 1)
        def _():
            for k in range(early):
                send_down(k).start()

    def finish(c):
        send_rise(c).wait_recv()
        to_here = merge(pair_of(stats, c, 1), pair_of(from_below, c, 0))

        def parts(whole):
            att_part, query_part = suffix_parts(c, own, whole)
            send_chain(c).wait_recv()
            att_sum = att_part + chain_in[c, 0].astype(f32)
            query_sum = query_part + chain_in[c, 1].astype(f32)
            return att_sum.astype(bf16), query_sum.astype(bf16)

        @pl.when(has_above)
        def _():
            put(to_above, c, to_here)
            send_rise(c).start()
            att_sum, query_sum = parts(merge(to_here, pair_of(from_above, c, 0)))
            chain_out[c, 0] = att_sum
            chain_out[c, 1] = query_sum
            send_chain(c).start()

        @pl.when(is_last)
        def _():
            att_sum, query_sum = parts(to_here)
            att_ref[tail, columns_of(c)] = att_sum
            qgrad_ref[tail, columns_of(c)] = query_sum

    def band(c):
        @pl.when(me > 1)
        def _():
            wait_high(c)

        @pl.when(me == 0)
        def _():
            send_suf_bottom(c).wait_recv()

        @pl.when(me < last - 1)
        def _():
            send_low(c).wait_recv()

        @pl.when(me == last - 1)
        def _():
            send_low_last(c).wait_recv()

        kv[c, :, suf] = sfx[c, 2:4]
        query_two = two_heads(own_qg[c, 0], scale)
        grad_two = two_heads(own_qg[c, 1], 1.0)
        keys = kv[c, 0]
        values = kv[c, 1]
        scores = dot_nt(keys, query_two) + bias[...]
        largest = jnp.max(scores, axis=0, keepdims=True)
        expo = jnp.exp(scores - largest)
        total = jnp.sum(expo, axis=0, keepdims=True)
        dprob = dot_nt(values, grad_two)
        inverse = 1.0 / total
        delta = jnp.sum(expo * dprob, axis=0, keepdims=True) * inverse
        probs = expo * (inverse * row_live)
        probs_low = probs.astype(bf16)
        dscore = (probs * (dprob - delta)).astype(bf16)
        att_ref[:, columns_of(c)] = one_pair(dot_tn(probs_low, values)).astype(bf16)
        qgrad_ref[:, columns_of(c)] = (one_pair(dot_tn(dscore, keys)) * scale).astype(bf16)
        key_all = dot_nn(dscore, query_two)
        value_all = dot_nn(probs_low, grad_two)

        @pl.when(me == 1)
        def _():
            down_out[c, 0] = (key_all[low] + fin_grad[c, 0, low]).astype(bf16)
            down_out[c, 1] = (value_all[low] + fin_grad[c, 1, low]).astype(bf16)

        @pl.when(me != 1)
        def _():
            down_out[c, 0] = key_all[low].astype(bf16)
            down_out[c, 1] = value_all[low].astype(bf16)

        @pl.when(me == 0)
        def _():
            add_out[c, 0] = key_all[suf].astype(bf16)
            add_out[c, 1] = value_all[suf].astype(bf16)
            send_add(c).start()

        up_out[c, 0] = key_all[high].astype(bf16)
        up_out[c, 1] = value_all[high].astype(bf16)
        band_grad[c, 0] = key_all[own]
        band_grad[c, 1] = value_all[own]
        suf_grad[c, 0] = key_all[suf]
        suf_grad[c, 1] = value_all[suf]

        @pl.when(has_below & ((me > 1) | (c >= early)))
        def _():
            send_down(c).start()

    def combine(c):
        @pl.when(has_below)
        def _():
            band_grad[c] = band_grad[c] + fin_grad[c, :, own]

            @pl.when(me < last)
            def _():
                group_from(c, up_in, None, up_recv)
                band_grad[c, :, 0:W] = band_grad[c, :, 0:W] + up_in[c].astype(f32)

            @pl.when(is_last)
            def _():
                group_from(c, up_in, slice(0, near), up_recv)
                band_grad[c, :, 0:near] = band_grad[c, :, 0:near] + up_in[c, :, 0:near].astype(f32)
                send_add(c).wait_recv()
                band_grad[c, :, tail] = (
                    band_grad[c, :, tail] + suf_grad[c] + add_in[c].astype(f32)
                )

        @pl.when(has_above)
        def _():
            group_from(c, down_in, None, down_recv)
            band_grad[c, :, rows - W : rows] = band_grad[c, :, rows - W : rows] + down_in[
                c
            ].astype(f32)

        kgrad_ref[:, columns_of(c)] = band_grad[c, 0].astype(bf16)
        vgrad_ref[:, columns_of(c)] = band_grad[c, 1].astype(bf16)

    def within_chunks(t):
        return (t >= 0) & (t < chunks)

    def by_role(bottom, first, between, top):
        return jnp.where(
            me == 0, bottom, jnp.where(me == 1, first, jnp.where(is_last, top, between))
        )

    never = 0 * me - 1

    def step(t, carry):
        @pl.when((t < chunks) & has_below)
        def _():
            suffix_pass(t)

        @pl.when(within_chunks(t - 1) & (me > 1) & has_above)
        def _():
            pass_down(t - 1)

        @pl.when(within_chunks(t - 1) & (me == 1))
        def _():
            finish_first(t - 1)

        a = by_role(never, t - chunks - FIRST_ADD, t - chunks - BETWEEN_ADD, never)

        @pl.when(within_chunks(a))
        def _():
            send_add(a).wait_recv()
            add_out[a] = (suf_grad[a] + add_in[a].astype(f32)).astype(bf16)
            send_add(a).start()

        first_band = jnp.where(
            t <= early, t - 1, jnp.where(t <= chunks, never, t - chunks - 1 + early)
        )
        b = by_role(t, first_band, t - chunks, t - chunks)

        @pl.when(within_chunks(b))
        def _():
            band(b)

        f = jnp.where(is_last, t - 2 * chunks, t - chunks + 1)

        @pl.when(within_chunks(f) & (me > 1))
        def _():
            finish(f)

        first_up = jnp.where(t <= early, t - 1, never)
        for c in range(early, chunks):
            turn = chunks + UP_TURN + c + (UP_HOLD if c >= early + UP_FREE else 0)
            first_up = jnp.where(t == turn, c, first_up)
        u = by_role(t - 1 - BOTTOM_HOLD, first_up, t - chunks - 1, never)

        @pl.when(within_chunks(u))
        def _():
            @pl.when(me < last - 1)
            def _():
                send_up(u).start()

            @pl.when(me == last - 1)
            def _():
                send_up_last(u).start()

        k = by_role(
            t - chunks - 1, t - 2 * chunks - FIRST_LAST, t - 2 * chunks - BETWEEN_HOLD, t - 3 * chunks
        )

        @pl.when(within_chunks(k))
        def _():
            combine(k)

        return carry

    steps = by_role(
        2 * chunks + 1 + BOTTOM_HOLD, 3 * chunks + FIRST_LAST, 3 * chunks + BETWEEN_HOLD, 4 * chunks
    )
    lax.fori_loop(0, steps, step, 0)

    def sent(source, sem):
        remote(source, source, sem, suf_recv.at[0], below).wait_send()

    @pl.when(has_below)
    def _():
        sent(down_out, down_send)

        @pl.when(me == 1)
        def _():
            sent(sfx.at[:, 2:4], suf_send)

        @pl.when(has_above)
        def _():
            sent(kv.at[:, :, own], low_send)
            sent(to_above, rise_send)
            sent(chain_out, chain_send)

        @pl.when(is_last)
        def _():
            sent(kv.at[:, :, W : W + near], low_send)

        @pl.when(me > 1)
        def _():
            sent(sfx, suf_send)
            sent(to_below, fall_send)

    @pl.when(has_above)
    def _():
        sent(kv.at[:, :, own], high_send)
        sent(add_out, add_send)

    @pl.when(me < last - 1)
    def _():
        sent(up_out, up_send)

    @pl.when(me == last - 1)
    def _():
        sent(up_out.at[:, :, :near], up_send)


def spill(*refs):
    sems = refs[8]
    copies = [
        pltpu.make_async_copy(refs[k], refs[4 + k].at[0], sems.at[k]) for k in range(4)
    ]
    for copy in copies:
        copy.start()
    for copy in copies:
        copy.wait()


def per_device(n, query_vectors, key_vectors, value_vectors, out_grad, pad_length):
    rows, features = query_vectors.shape[1:]
    chunks = features // PAIR
    all_keys = rows + 2 * W + G
    vmem = pl.BlockSpec(memory_space=pltpu.VMEM)
    dma = pltpu.SemaphoreType.DMA
    hbm = pl.BlockSpec(memory_space=pltpu.HBM)
    outs = pl.pallas_call(
        functools.partial(kernel, n, rows, chunks),
        out_shape=(pltpu.VMEM((rows, features), bf16),) * 4,
        in_specs=[hbm] * 5,
        out_specs=(vmem,) * 4,
        scratch_shapes=[
            pltpu.SMEM((1,), jnp.int32),
            pltpu.VMEM((chunks, 2, all_keys, PAIR), bf16),
            pltpu.VMEM((chunks, 4, G, PAIR), bf16),
            pltpu.VMEM((chunks, 2, rows, PAIR), bf16),
            pltpu.VMEM((chunks, 8, 2 * G), f32),
            pltpu.VMEM((all_keys, 2 * rows), f32),
            pltpu.VMEM((W + rows, 2 * G), f32),
            pltpu.VMEM((chunks, W + rows, 2 * G), f32),
            pltpu.VMEM((chunks, W + rows, 2 * G), f32),
            pltpu.VMEM((chunks, 2, rows, PAIR), f32),
            pltpu.VMEM((chunks, 2, W + rows, PAIR), f32),
            pltpu.VMEM((chunks, 2, G, PAIR), f32),
        ]
        + [pltpu.VMEM((chunks, 2, W, PAIR), bf16)] * 4
        + [pltpu.VMEM((chunks, 2, G, PAIR), bf16)] * 4
        + [pltpu.VMEM((chunks, 2, 2 * G), f32)] * 4
        + [pltpu.SemaphoreType.REGULAR, dma, dma((2,))]
            + [dma] * 9
        + [dma((chunks,))] * 6
        + [dma((chunks // HIGH_GROUP,))]
        + [dma((chunks // 4 + 1,))] * 2,
        compiler_params=pltpu.CompilerParams(
            collective_id=0, has_side_effects=True, vmem_limit_bytes=48 << 20
        ),
    )(pad_length, *(pltpu.with_memory_space_constraint(x, pltpu.HBM) for x in (query_vectors, key_vectors, value_vectors, out_grad)))
    anywhere = pl.BlockSpec(memory_space=pl.ANY)
    return pl.pallas_call(
        spill,
        out_shape=(jax.ShapeDtypeStruct((1, rows, features), bf16),) * 4,
        in_specs=[vmem] * 4,
        out_specs=(anywhere,) * 4,
        scratch_shapes=[dma((4,))],
    )(*(pltpu.with_memory_space_constraint(x, pltpu.VMEM) for x in outs))


def solution(mesh):
    rows = P(("group", "doc"), "seq", None)
    return jax.shard_map(
        functools.partial(per_device, mesh.shape["seq"]),
        mesh=mesh,
        in_specs=(rows, rows, rows, rows, P(("group", "doc"))),
        out_specs=(rows,) * 4,
        check_vma=False,
    )
```
